32 devices in a mesh: band: 4 (over x, core), freq: 8 (over z, y).
Axes of the slice: x: 2, y: 2, z: 4, core: 2. Of those that a mesh axis runs over, the one named last changes fastest.
Arguments:
- spectrum: float32 [8, 36, 64, 64], P('freq', None, 'band'), may hold values from 0.05 to 1
- velocity: float32 [2, 24, 64, 64], P(None, None, 'band', 'freq'), may hold values from -3 to 3
- gain_matrix: bfloat16 [288, 288], replicated, may hold values from -0.375 to 0.375
- quad_matrix: bfloat16 [288, 288], replicated, may hold values from -0.375 to 0.375
- limiter_flags: int32 [8, 64, 64], replicated, may hold values 0 or 1
- sea_mask: int32 [64, 64], replicated, may hold values 0 or 1
- current_route: int32 [8], replicated, may hold values from 0 to 23
- stokes_route: int32 [8, 4], replicated, may hold values from 0 to 23
Outputs:
- spectrum_out: float32 [8, 36, 64, 64], P('freq', None, 'band')
- velocity_out: float32 [2, 24, 64, 64], P(None, None, 'band', 'freq')
The draws below stay inside these ranges and needn't reach their ends.
All inputs are finite; a program needn't handle non-finite values.
Results may differ from the reference program's by a relative error of at most 0.00045.
Values sent between devices are 32-bit elements; how exact they have to be, the bound alone decides.
A program may use at most 64 MiB of HBM per device.

```python
import jax
import jax.numpy as jnp
from jax import lax

DIR = 36
LAT_DEV = 16
LAYERS = 24
SUB = 4
CYCLES = 2
OSTEPS = 3
KS = 4
F = 8
COMP = 288
NLAT = 64
NLON = 64
N_BAND = 4


def place_ends(values, rng, least, top_value):
    place = [jax.random.randint(jax.random.fold_in(rng, axis), (), 0, length) for axis, length in enumerate(values.shape)]
    widest = values.shape.index(max(values.shape))
    next_to = place[:widest] + [(place[widest] + 1) % values.shape[widest]] + place[widest + 1:]
    return values.at[tuple(place)].set(least).at[tuple(next_to)].set(top_value)


def block_scale(stream_key, extent, cuts, least, high):
    loudness, own = 1.0, jax.random.fold_in(stream_key, 6)
    for axis_at, shards_of in cuts:
        heights = jnp.exp(jax.random.uniform(jax.random.fold_in(own, axis_at), (shards_of,), jnp.float32, least / len(cuts), high / len(cuts)))
        loudness = loudness * jnp.repeat(heights, extent[axis_at] // shards_of).reshape([-1 if axis == axis_at else 1 for axis in range(len(extent))])
    return loudness


def scatter_about(rng, dims, deviation, limit, pieces=(), kind=jnp.bfloat16):
    loudness = block_scale(rng, dims, pieces, -0.22, 0.18) if pieces else 1.0
    array = jax.random.normal(rng, dims, jnp.float32) * deviation * loudness
    return jnp.minimum(jnp.maximum(array, -limit), limit).astype(kind)


def setup_inputs(seed: int = 0) -> dict:
    seeds = jax.random.split(jax.random.key(seed), 9)
    spectrum = jnp.clip(0.05 + 0.95 * jax.random.uniform(seeds[0], (F, DIR, NLAT, NLON), jnp.float32) ** block_scale(seeds[0], (F, DIR, NLAT, NLON), ((0, 8), (2, 4)), -0.2, 0.2), 0.05, 1.0)
    velocity = scatter_about(seeds[1], (2, LAYERS, NLAT, NLON), 0.5, 3.0, ((2, 4), (3, 8)), jnp.float32)
    gain_matrix = scatter_about(seeds[2], (COMP, COMP), COMP ** -0.5, 0.375)
    quad_matrix = scatter_about(seeds[3], (COMP, COMP), COMP ** -0.5, 0.375)
    limiter_flags = place_ends((jax.random.randint(seeds[4], (CYCLES * SUB, NLAT, NLON), 0, 2) < 1).astype(jnp.int32), jax.random.fold_in(seeds[4], 1), 0, 1)
    sea_mask = place_ends((jax.random.randint(seeds[5], (NLAT, NLON), 0, 4) < 3).astype(jnp.int32), jax.random.fold_in(seeds[5], 1), 0, 1)
    current_route = place_ends(jax.random.randint(seeds[6], (F,), 0, LAYERS), jax.random.fold_in(seeds[6], 1), 0, LAYERS - 1).astype(jnp.int32)
    stokes_route = place_ends(jax.random.randint(seeds[7], (F, KS), 0, LAYERS), jax.random.fold_in(seeds[7], 1), 0, LAYERS - 1).astype(jnp.int32)
    return dict(spectrum=spectrum, velocity=velocity, gain_matrix=gain_matrix, quad_matrix=quad_matrix, limiter_flags=limiter_flags, sea_mask=sea_mask, current_route=current_route, stokes_route=stokes_route)


precise = lax.Precision.HIGHEST
ocean_dt = 0.2
viscous = 0.5
coriolis = 1.0
mixing = 0.5
friction = 0.1


def directions(how_many):
    angles = (jnp.arange(how_many, dtype=jnp.float32) + 0.5) * (2.0 * jnp.pi / how_many)
    return jnp.cos(angles), jnp.sin(angles)


def speed_of(position, total_count):
    return 0.5 + 0.3 * (position.astype(jnp.float32) + 0.5) / total_count


def wavenumber(position, total_count):
    return 0.5 + 1.5 * (position.astype(jnp.float32) + 0.5) / total_count


def pad_last(values):
    zero_col = jnp.zeros(values.shape[:-1] + (1,), values.dtype)
    return jnp.concatenate([zero_col, values, zero_col], axis=-1)


def transport(lower_side, upper_side, courant, limiter):
    upwind = jnp.maximum(courant, 0.0) * lower_side + jnp.minimum(courant, 0.0) * upper_side
    wendroff = 0.5 * courant * (lower_side + upper_side) - 0.5 * courant * courant * (upper_side - lower_side)
    return upwind + limiter * (wendroff - upwind)


def substep(extended, current, limiter_rows, sea_rows, rate_now, cos_table, sin_table):
    limiter = limiter_rows.astype(jnp.float32)
    drifts = 0.15 * jnp.tanh(current)
    north_drift = drifts[..., 1:2, :, :]
    face_north = 0.5 * (north_drift[..., :-1, :] + north_drift[..., 1:, :])
    courant = rate_now * sin_table[:, None, None] + face_north
    flux_north = transport(extended[..., :-1, :], extended[..., 1:, :], courant, limiter[1:, :])
    shifted = extended[..., 1:-1, :] - (flux_north[..., 1:, :] - flux_north[..., :-1, :])
    east_drift = pad_last(drifts[..., 0:1, 1:-1, :])
    face_east = 0.5 * (east_drift[..., :-1] + east_drift[..., 1:])
    courant_east = rate_now * cos_table[:, None, None] + face_east
    padded = pad_last(shifted)
    limiter_east = pad_last(limiter[1:-1, :])[:, 1:]
    flux_east = transport(padded[..., :-1], padded[..., 1:], courant_east, limiter_east)
    result = shifted - (flux_east[..., 1:] - flux_east[..., :-1])
    return result * sea_rows.astype(jnp.float32)


def source(block, gain_matrix, quad_matrix):
    block_shape = block.shape
    flattened = block.reshape(block_shape[0] * block_shape[1], -1)
    gain_arg = jnp.dot(gain_matrix, flattened.astype(jnp.bfloat16), preferred_element_type=jnp.float32)
    quartic = jnp.dot(quad_matrix, (flattened * flattened).astype(jnp.bfloat16), preferred_element_type=jnp.float32)
    updated = flattened * (1.0 + 0.5 * jnp.tanh(gain_arg) - 0.25 * jnp.tanh(quartic))
    return updated.reshape(block_shape)


def deposit_table(stokes_route):
    layer_ids = jnp.arange(LAYERS, dtype=jnp.int32)
    weights = 1.0 / (1.0 + jnp.arange(stokes_route.shape[1], dtype=jnp.float32))
    hits = (stokes_route[:, :, None] == layer_ids[None, None, :]).astype(jnp.float32)
    return jnp.sum(hits * weights[None, :, None], axis=1)


def stokes_profile(spectrum, numbers, deposit):
    cos_table, sin_table = directions(spectrum.shape[1])
    factor = numbers * (spectrum.shape[1] ** -0.5)
    eastward = jnp.einsum("fdrc,d->frc", spectrum, cos_table, precision=precise) * factor[:, None, None]
    northward = jnp.einsum("fdrc,d->frc", spectrum, sin_table, precision=precise) * factor[:, None, None]
    stacked = jnp.stack([eastward, northward], axis=1)
    return jnp.einsum("fl,fsrc->slrc", deposit, stacked, precision=precise)


def ocean_step(padded, stokes, sea_tile):
    inner = padded[:, :, 1:-1, 1:-1]
    laplace = padded[:, :, 2:, 1:-1] + padded[:, :, :-2, 1:-1] + padded[:, :, 1:-1, 2:] + padded[:, :, 1:-1, :-2] - 4.0 * inner
    vertical = jnp.pad(inner, ((0, 0), (1, 1), (0, 0), (0, 0)))
    mixing_term = vertical[:, 2:] + vertical[:, :-2] - 2.0 * inner
    moving = inner + stokes
    turning = jnp.stack([moving[1], -moving[0]])
    tendency = viscous * laplace + coriolis * turning + mixing * mixing_term - friction * inner
    return (inner + ocean_dt * tendency) * sea_tile.astype(jnp.float32)


def reference(spectrum, velocity, gain_matrix, quad_matrix, limiter_flags, sea_mask, current_route, stokes_route):
    freq_total = spectrum.shape[0]
    cos_table, sin_table = directions(DIR)
    indices = jnp.arange(freq_total, dtype=jnp.int32)
    speeds = speed_of(indices, freq_total)
    numbers = wavenumber(indices, freq_total)
    current = jnp.swapaxes(velocity[:, current_route], 0, 1)
    current_ext = jnp.pad(current, ((0, 0), (0, 0), (1, 1), (0, 0)))
    flag_ext = jnp.pad(limiter_flags, ((0, 0), (1, 1), (0, 0)))
    deposit = deposit_table(stokes_route)
    stokes = jnp.zeros((2, LAYERS) + spectrum.shape[2:], jnp.float32)
    for cycle_index in range(CYCLES):
        def advect(packed):
            field_now, drift_ext, rate_now = packed
            for step_index in range(SUB):
                extended = jnp.pad(field_now, ((0, 0), (1, 1), (0, 0)))
                field_now = substep(extended, drift_ext, flag_ext[cycle_index * SUB + step_index], sea_mask, rate_now, cos_table, sin_table)
            return field_now

        spectrum = lax.map(advect, (spectrum, current_ext, speeds))
        if cycle_index == 0:
            stokes = stokes_profile(spectrum, numbers, deposit)
        blocks = spectrum.reshape(freq_total, DIR, N_BAND, LAT_DEV, spectrum.shape[3])
        blocks = jnp.moveaxis(blocks, 2, 0)
        blocks = lax.map(lambda piece: source(piece, gain_matrix, quad_matrix), blocks)
        spectrum = jnp.moveaxis(blocks, 0, 2).reshape(freq_total, DIR, N_BAND * LAT_DEV, blocks.shape[-1])
    for step_index in range(OSTEPS):
        padded = jnp.pad(velocity, ((0, 0), (0, 0), (1, 1), (1, 1)))
        velocity = ocean_step(padded, stokes, sea_mask)
    return spectrum, velocity
```

```python
import functools

import jax
import jax.numpy as jnp
import numpy as np
from jax import lax
from jax.experimental import pallas as pl
from jax.experimental.pallas import tpu as pltpu
from jax.sharding import PartitionSpec as P

DIR = 36
LAYERS = 24
SUB = 4
CYCLES = 2
OSTEPS = 3


precise = lax.Precision.HIGHEST
ocean_dt = 0.2
viscous = 0.5
coriolis = 1.0
mixing = 0.5
friction = 0.1


GROUP = 8
LANES = 128
DIRP = -(-DIR // GROUP) * GROUP
GROUPS = DIRP // GROUP
HALO = SUB
DEPTH = CYCLES * SUB
PARTS = ((0, 2), (2, GROUPS))
MESH = pl.DeviceIdType.MESH


def swap_pieces(blocks, piece, width):
    lane = lax.broadcasted_iota(jnp.int32, blocks[0].shape, 1)
    out = list(blocks)
    far = width // 2
    while far:
        low = (lane & (far * piece)) == 0
        for a in range(width):
            if a & far:
                continue
            b = a + far
            x, y = out[a], out[b]
            out[a] = jnp.where(low, x, pltpu.roll(y, far * piece, 1))
            out[b] = jnp.where(low, pltpu.roll(x, LANES - far * piece, 1), y)
        far //= 2
    return out


def packing(rows, planes, pitch, tile_cols):
    places = LANES // tile_cols
    free = set(range(places))
    left = {
        m: [q for q in range(LANES // pitch) if 0 <= m + planes * q - HALO < rows]
        for m in range(planes)
    }
    moves, where = [], {}
    while any(left.values()):
        best = None
        for m in range(planes):
            for by in range(places):
                fits = [
                    q for q in left[m] if (q * pitch // tile_cols + by) % places in free
                ]
                if best is None or len(fits) > len(best[2]):
                    best = (m, by, fits)
        m, by, fits = best
        spots = [(q * pitch // tile_cols + by) % places for q in fits]
        moves.append((m, (by * tile_cols - HALO) % LANES, spots))
        for q, spot in zip(fits, spots):
            where[m + planes * q - HALO] = spot
            free.remove(spot)
            left[m].remove(q)
    return moves, where


def pack(blocks, moves, tile_cols):
    lane = lax.broadcasted_iota(jnp.int32, blocks[0].shape, 1)
    total = None
    for m, shift, spots in moves:
        piece = pltpu.roll(blocks[m], shift, 1) if shift else blocks[m]
        if total is None:
            total = piece
            continue
        hit = None
        for spot in spots:
            one = (lane >= spot * tile_cols) & (lane < (spot + 1) * tile_cols)
            hit = one if hit is None else hit | one
        total = jnp.where(hit, piece, total)
    return total


def parts_of(courant):
    up, down = jnp.maximum(courant, 0.0), jnp.minimum(courant, 0.0)
    return up, down, 0.5 * (courant * courant - (up - down))


def kernel(
    bands,
    freqs,
    cols,
    route,
    stokes_route,
    spectrum,
    velocity,
    gain_in,
    quad_in,
    flags_in,
    sea_in,
    widen_in,
    wave_in,
    trig_in,
    result,
    ocean_out,
    spec,
    halo_low,
    halo_high,
    vel,
    gain_raw,
    quad_raw,
    widen,
    wave,
    trig,
    gain,
    quad,
    flag_raw,
    sea_raw,
    flag_blk,
    sea_blk,
    flag_north,
    flag_east,
    flag_north2,
    flag_east2,
    sea2,
    tile,
    tiles,
    route_out,
    route_own,
    route_low,
    route_high,
    drift,
    faces,
    faces2,
    coef,
    coef2,
    leave,
    arrive,
    first,
    packed,
    back,
    final,
    done,
    ocean,
    weight,
    vout,
    load_sems,
    halo_sems,
    route_sems,
    tile_sems,
    out_sems,
    back_sems,
    store_sems,
):
    band = lax.axis_index("band")
    me = lax.axis_index("freq")
    f32 = jnp.float32
    rows = spectrum.shape[1]
    tile_cols = velocity.shape[2]
    tall = rows + 2 * DEPTH
    block = max(LANES, cols)
    slots = block // cols
    n = tall // slots
    pitch = tile_cols + 2 * HALO
    per = LANES // pitch
    planes = (rows + 2 * HALO) // per
    seam = LANES - pitch
    moves, spot_of = packing(rows, planes, pitch, tile_cols)
    has_low = band > 0
    has_high = band < bands - 1

    def others(fn):
        def step(i, carry):
            fn(lax.rem(me + i, freqs))
            return carry

        lax.fori_loop(1, freqs, step, 0)

    def every(fn):
        def step(i, carry):
            fn(i)
            return carry

        lax.fori_loop(0, freqs, step, 0)

    def copy(src, dst, sems, slot_send, slot_recv, to_band, to_freq):
        return pltpu.make_async_remote_copy(
            src_ref=src,
            dst_ref=dst,
            send_sem=sems.at[(0,) + slot_send],
            recv_sem=sems.at[(1,) + slot_recv],
            device_id=(to_band, to_freq),
            device_id_type=MESH,
        )

    def rolled(x, shift):
        shift %= x.shape[1]
        return pltpu.roll(x, shift, 1) if shift else x

    def strided(ref, size, base, at):
        depth = ref.shape[1]
        if cols > LANES:
            return ref[pl.ds(base, size), at, :]
        return ref.reshape(ref.shape[0] * depth, cols)[
            pl.ds(base * depth + at, size, stride=depth), :
        ]

    def await_bytes(ref, sem):
        pltpu.make_async_copy(ref, ref, sem).wait()

    rest = pl.ds(0, freqs - 1)

    barrier = pltpu.get_barrier_semaphore()

    def greet(to_band, to_freq):
        pl.semaphore_signal(barrier, inc=1, device_id=(to_band, to_freq), device_id_type=MESH)

    load_vel = pltpu.make_async_copy(velocity, vel, load_sems.at[0])
    load_vel.start()
    others(lambda f: greet(band, f))

    @pl.when(has_low)
    def _():
        every(lambda f: greet(band - 1, f))

    @pl.when(has_high)
    def _():
        every(lambda f: greet(band + 1, f))

    load_spec = pltpu.make_async_copy(spectrum, spec.at[pl.ds(0, DIR)], load_sems.at[1])
    load_grid = [
        pltpu.make_async_copy(src, dst, load_sems.at[2 + i])
        for i, (src, dst) in enumerate(((flags_in, flag_raw), (sea_in, sea_raw)))
    ]
    loads = [
        pltpu.make_async_copy(src, dst, load_sems.at[4 + i])
        for i, (src, dst) in enumerate(
            (
                (wave_in, wave),
                (gain_in, gain_raw),
                (quad_in, quad_raw),
                (widen_in, widen),
                (trig_in, trig),
            )
        )
    ]
    for one in load_grid:
        one.start()
    load_spec.start()
    for one in loads:
        one.start()

    load_vel.wait()
    for c in range(2):
        field = vel[c].reshape(rows * tile_cols, LAYERS)
        tile[c * LAYERS : (c + 1) * LAYERS, :] = field.T

    def prepare(f):
        route_out[f, 0:1, :] = tile[pl.ds(route[f], 1), :]
        route_out[f, 1:2, :] = tile[pl.ds(LAYERS + route[f], 1), :]

    every(prepare)
    count = freqs - 1 + freqs * (has_low.astype(jnp.int32) + has_high.astype(jnp.int32))
    pl.semaphore_wait(barrier, count)

    halo_to_low = copy(
        spectrum.at[:, pl.ds(0, DEPTH)], halo_high.at[pl.ds(0, DIR)], halo_sems,
        (0,), (0,), band - 1, me,
    )
    halo_to_high = copy(
        spectrum.at[:, pl.ds(rows - DEPTH, DEPTH)], halo_low.at[pl.ds(0, DIR)], halo_sems,
        (1,), (1,), band + 1, me,
    )

    def route_copy(f):
        return copy(route_out.at[f], route_own.at[me], route_sems, (0,), (0,), band, f)

    def route_to_low(f):
        return copy(
            route_out.at[f], route_high.at[me], route_sems, (1,), (1,), band - 1, f
        )

    def route_to_high(f):
        return copy(
            route_out.at[f], route_low.at[me], route_sems, (2,), (2,), band + 1, f
        )

    others(lambda f: route_copy(f).start())

    @pl.when(has_low)
    def _():
        every(lambda f: route_to_low(f).start())
        halo_to_low.start()

    @pl.when(has_high)
    def _():
        every(lambda f: route_to_high(f).start())
        halo_to_high.start()

    def near_tiles(fn):
        for down in (-1, 0, 1):
            for side in (-1, 0, 1):
                if down == 0 and side == 0:
                    continue
                to_band, to_freq = band + down, me + side
                there = (to_band >= 0) & (to_band < bands) & (to_freq >= 0) & (to_freq < freqs)
                mine = 3 * (1 + down) + 1 + side
                fn(there, mine, 8 - mine, to_band, to_freq)

    def tile_copy(mine, theirs, to_band, to_freq):
        return copy(tile, tiles.at[theirs], tile_sems, (), (), to_band, to_freq)

    def tile_start(there, mine, theirs, to_band, to_freq):
        @pl.when(there)
        def _():
            tile_copy(mine, theirs, to_band, to_freq).start()

        @pl.when(jnp.logical_not(there))
        def _():
            tiles[mine] = jnp.zeros_like(tile)

    near_tiles(tile_start)
    tiles[4] = tile[...]
    route_own[me] = route_out[me]

    pads = ((DIR, DIRP - DIR),)
    for at, size in pads:
        spec[at : at + size] = jnp.zeros((size, rows, cols), f32)
        halo_low[at : at + size] = jnp.zeros((size, DEPTH, cols), f32)
        halo_high[at : at + size] = jnp.zeros((size, DEPTH, cols), f32)

    @pl.when(jnp.logical_not(has_low))
    def _():
        halo_low[...] = jnp.zeros_like(halo_low)
        route_low[...] = jnp.zeros_like(route_low)

    @pl.when(jnp.logical_not(has_high))
    def _():
        halo_high[...] = jnp.zeros_like(halo_high)
        route_high[...] = jnp.zeros_like(route_high)

    for one in load_grid:
        one.wait()

    steps = CYCLES * SUB
    all_rows = sea_raw.shape[0]
    wide = (8, block)

    def grid_row(at):
        whole = jnp.clip(band * rows - DEPTH + at, 0, all_rows - 1)
        there = has_low if at < DEPTH else (None if at < DEPTH + rows else has_high)
        flag = strided(flag_raw, steps, 0, whole)
        sea = sea_raw[pl.ds(whole, 1), :].astype(f32)
        flag = flag.astype(f32)
        if there is not None:
            there = there.astype(f32)
            flag, sea = flag * there, sea * there
        return flag, sea

    for k in range(n):
        pieces = [grid_row(k + n * s) for s in range(slots)]
        flag_blk[k] = jnp.concatenate([flag for flag, _ in pieces], axis=1)
        sea = jnp.concatenate([sea for _, sea in pieces], axis=1)
        sea_blk[8 * k : 8 * (k + 1), :] = jnp.broadcast_to(sea, wide)

    for k in range(n):
        here = flag_blk[k]
        above = flag_blk[k + 1] if k + 1 < n else rolled(flag_blk[0], -cols)
        beside = rolled(here, -1)
        for sub in range(SUB):
            there = slice(8 * k, 8 * (k + 1))
            flag_north[sub, there, :] = jnp.broadcast_to(above[sub : sub + 1], wide)
            flag_east[sub, there, :] = jnp.broadcast_to(beside[sub : sub + 1], wide)

    lane = lax.broadcasted_iota(jnp.int32, (8, LANES), 1)
    column = me * tile_cols - HALO + (lane & (pitch - 1))
    inside = (column >= 0) & (column < cols)
    window_flags, window_sea = [], []
    for m in range(planes):
        total_flags, total_sea = jnp.zeros((8, LANES), f32), jnp.zeros((8, LANES), f32)
        for q in range(per):
            at = m + planes * q + DEPTH - HALO
            k, s = at % n, at // n
            shift = lax.rem(q * pitch - cols * s - tile_cols * me + HALO + 2 * block, block)
            hit = (lane >= q * pitch) & (lane < (q + 1) * pitch) & inside
            total_flags = jnp.where(
                hit, pltpu.roll(flag_blk[k], shift, 1)[:, :LANES], total_flags
            )
            total_sea = jnp.where(hit, pltpu.roll(sea_blk[8 * k : 8 * (k + 1), :], shift, 1)[:, :LANES], total_sea)
        window_flags.append(total_flags)
        window_sea.append(total_sea)
    for m in range(planes):
        sea2[m] = jnp.concatenate([window_sea[m]] * GROUPS, axis=0)
        above = window_flags[m + 1] if m + 1 < planes else rolled(window_flags[0], -pitch)
        beside = rolled(window_flags[m], -1)
        for sub in range(SUB):
            step = SUB + sub
            flag_north2[sub, m] = jnp.broadcast_to(above[step : step + 1], (DIRP, LANES))
            flag_east2[sub, m] = jnp.broadcast_to(beside[step : step + 1], (DIRP, LANES))

    load_spec.wait()
    for one in loads:
        one.wait()

    for raw, padded in ((gain_raw, gain), (quad_raw, quad)):
        half = jnp.dot(widen[...], raw[...], preferred_element_type=f32).astype(jnp.bfloat16)
        padded[...] = lax.dot_general(
            half, widen[...], (((1,), (1,)), ((), ())), preferred_element_type=f32
        ).astype(jnp.bfloat16)

    layer = lax.broadcasted_iota(jnp.int32, (LAYERS, 1), 0)
    component = lax.broadcasted_iota(jnp.int32, (LAYERS, freqs * DIRP), 1)
    deposits = jnp.zeros((LAYERS, freqs * DIRP), f32)
    for g in range(freqs):
        deposit = jnp.zeros((LAYERS, 1), f32)
        for j in range(stokes_route.shape[0]):
            hit = (layer == stokes_route[j, g]).astype(f32)
            deposit = deposit + hit * (1.0 / (1.0 + j))
        own = (component >= g * DIRP) & (component < (g + 1) * DIRP)
        deposits = jnp.where(own, deposit, deposits)
    for c in range(2):
        weight[c * LAYERS : (c + 1) * LAYERS, :] = deposits * trig[c : c + 1, :]

    await_bytes(route_own.at[rest], route_sems.at[1, 0])

    @pl.when(has_low)
    def _():
        await_bytes(route_low, route_sems.at[1, 2])

    @pl.when(has_high)
    def _():
        await_bytes(route_high, route_sems.at[1, 1])

    stacks = [
        jnp.concatenate(
            [route_low[j], route_own[j], route_high[j], jnp.zeros((2, LANES), f32)], axis=0
        )
        for j in range(freqs)
    ]
    across = []
    for row in range(rows):
        halves = []
        for half in range(block // LANES):
            total = jnp.zeros((8, LANES), f32)
            reach = min(cols, LANES) // tile_cols
            turned = [
                rolled(stacks[half * reach + j], (j - row) * tile_cols) for j in range(reach)
            ]
            for j, one in enumerate(turned):
                lead = j * tile_cols
                total = jnp.where((lane >= lead) & (lane < lead + tile_cols), one, total)
            halves.append(total)
        across.append(jnp.concatenate(halves, axis=1))
    spreads = 0.15 * jnp.tanh(jnp.concatenate(across, axis=0))
    moved = [spreads] + [rolled(spreads, cols * s) for s in range(1, slots)]
    for row in range(rows):
        for source in range(3):
            at = row + DEPTH + rows * (source - 1)
            if at < 0 or at >= tall:
                continue
            k, s = at % n, at // n
            for c in range(2):
                line = 8 * row + 2 * source + c
                drift[c, k : k + 1, cols * s : cols * (s + 1)] = moved[s][
                    line : line + 1, cols * s : cols * (s + 1)
                ]
    blane = lax.broadcasted_iota(jnp.int32, (1, block), 1)
    last = ((blane & (cols - 1)) == cols - 1).astype(f32)
    inner = 1.0 - last
    east, north = drift[0], drift[1]
    above = jnp.concatenate([north[1:], rolled(north[0:1], -cols)], axis=0)
    for i, face in enumerate(
        (0.5 * (north + above), 0.5 * (inner * east + rolled(east, -1)), 0.5 * east)
    ):
        for k in range(n):
            faces[i, 8 * k : 8 * (k + 1), :] = jnp.broadcast_to(face[k : k + 1], wide)

    @pl.when(has_low)
    def _():
        halo_to_high.wait_recv()

    @pl.when(has_high)
    def _():
        halo_to_low.wait_recv()

    number = me.astype(f32) + 0.5
    my_rate = 0.5 + 0.3 * number / freqs

    def row_of(base, at):
        if at < DEPTH:
            return strided(halo_low, GROUP, base, at)
        if at < DEPTH + rows:
            return strided(spec, GROUP, base, at - DEPTH)
        return strided(halo_high, GROUP, base, at - DEPTH - rows)

    def up(x, by):
        return jnp.concatenate([x[8:], rolled(x[:8], -by)], axis=0)

    def down(x, by):
        return jnp.concatenate([rolled(x[-8:], by), x[:-8]], axis=0)

    def advect_first(group, carry):
        base = pl.multiple_of(group * GROUP, GROUP)
        table = wave[pl.ds(base, GROUP), :]

        def rate_of(i):
            rate = jnp.broadcast_to(table[:, i : i + 1] * my_rate, wide)
            return jnp.concatenate([rate] * n, axis=0)

        rate_east = rate_of(0)
        for axis, rate in ((0, rate_of(1)), (1, rate_east)):
            for i, one in enumerate(parts_of(rate + faces[axis])):
                coef[3 * axis + i] = one
        coef[6] = 1.0 - last * jnp.maximum(rate_east + faces[2], 0.0)
        state = jnp.concatenate(
            [
                jnp.concatenate([row_of(base, k + n * s) for s in range(slots)], axis=1)
                for k in range(n)
            ],
            axis=0,
        )
        for sub in range(SUB):
            more = flag_north[sub] * coef[2]
            flux = (coef[0] + more) * state + (coef[1] - more) * up(state, cols)
            state = state - (flux - down(flux, cols))
            more = flag_east[sub] * coef[5]
            flux = (coef[3] + more) * (inner * state) + (coef[4] - more) * rolled(state, -1)
            state = (coef[6] * state - (inner * flux - rolled(flux, 1))) * sea_blk[...]
        width = min(cols, LANES) // pitch
        low_half = lax.broadcasted_iota(jnp.int32, (8 * planes, LANES), 1) < width * pitch
        for odd in range(2):
            turned = rolled(state, HALO - odd * tile_cols)
            for half in range(block // LANES):
                sources = []
                for i in range(width):
                    pieces = []
                    for s in range(slots):
                        lines = []
                        for m in range(planes):
                            at = m + planes * (i + width * s) + DEPTH - HALO
                            assert at // n == s
                            k = at % n
                            lines.append(
                                turned[8 * k : 8 * (k + 1), half * LANES : (half + 1) * LANES]
                            )
                        pieces.append(jnp.concatenate(lines, axis=0))
                    sources.append(pieces[0] if slots == 1 else jnp.where(low_half, *pieces))
                for e, one in enumerate(swap_pieces(sources, pitch, width)):
                    to = 2 * (e + width * half) + odd
                    for m in range(planes):
                        leave[to, pl.ds(base, GROUP), m * LANES : (m + 1) * LANES] = one[
                            8 * m : 8 * (m + 1)
                        ]
        return carry

    def part_rows(part):
        low, high = PARTS[part]
        return pl.ds(low * GROUP, (high - low) * GROUP)

    def out_copy(part, f):
        there = part_rows(part)
        return copy(
            leave.at[f, there], arrive.at[me, there], out_sems, (part,), (part,), band, f
        )

    for part, (low, high) in enumerate(PARTS):
        lax.fori_loop(low, high, advect_first, 0)
        others(lambda f: out_copy(part, f).start())
    arrive[me] = leave[me]

    deep = 1 + has_low.astype(jnp.int32) + has_high.astype(jnp.int32)
    broad = 1 + (me > 0).astype(jnp.int32) + (me < freqs - 1).astype(jnp.int32)

    def await_tiles(way):
        for a in (2, 3):
            for b in (2, 3):

                @pl.when((deep == a) & (broad == b))
                def _():
                    await_bytes(tiles.at[pl.ds(0, a * b - 1)], tile_sems.at[way])

    await_tiles(1)
    tall_lane = lax.broadcasted_iota(jnp.int32, tile.shape, 1)
    for m in range(planes):
        total = jnp.zeros(tile.shape, f32)
        for q in range(per):
            row = m + planes * q - HALO
            down = 0 if row < 0 else (1 if row < rows else 2)
            from_row = row + rows * (1 - down)
            lead = q * pitch
            for side, width, from_col in (
                (0, HALO, tile_cols - HALO), (1, tile_cols, 0), (2, HALO, 0),
            ):
                piece = rolled(tiles[3 * down + side], lead - from_row * tile_cols - from_col)
                total = jnp.where((tall_lane >= lead) & (tall_lane < lead + width), piece, total)
                lead += width
        ocean[:, m * LANES : (m + 1) * LANES] = total

    def face_step(g, carry):
        east = 0.15 * jnp.tanh(ocean[pl.ds(route[g], 1), :])
        north = 0.15 * jnp.tanh(ocean[pl.ds(LAYERS + route[g], 1), :])
        for m in range(planes):
            here = north[:, m * LANES : (m + 1) * LANES]
            above = (
                north[:, (m + 1) * LANES : (m + 2) * LANES]
                if m + 1 < planes
                else rolled(north[:, :LANES], -pitch)
            )
            faces2[g, m : m + 1, :] = 0.5 * (here + above)
            here = east[:, m * LANES : (m + 1) * LANES]
            faces2[g, planes + m : planes + m + 1, :] = 0.5 * (here + rolled(here, -1))
        return carry

    lax.fori_loop(0, freqs, face_step, 0)

    for part in range(len(PARTS)):
        await_bytes(arrive.at[rest, part_rows(part)], out_sems.at[1, part])

    def source(whole):
        grown = jnp.dot(gain[...], whole.astype(jnp.bfloat16), preferred_element_type=f32)
        quartic = jnp.dot(
            quad[...], (whole * whole).astype(jnp.bfloat16), preferred_element_type=f32
        )
        return whole * (1.0 + 0.5 * jnp.tanh(grown) - 0.25 * jnp.tanh(quartic))

    total_rows = freqs * DIRP
    for m in range(planes):
        there = slice(m * LANES, (m + 1) * LANES)
        whole = arrive[:, :, there].reshape(total_rows, LANES) * sea2[m][0:1]
        first[:, :, there] = source(whole).reshape(freqs, DIRP, LANES)

    def advect_second(g, carry):
        rate = 0.5 + 0.3 * (g.astype(f32) + 0.5) / freqs
        table = wave[...] * rate
        rate_east = jnp.broadcast_to(table[:, 0:1], (DIRP, LANES))
        rate_north = jnp.broadcast_to(table[:, 1:2], (DIRP, LANES))
        state = [first[g, :, m * LANES : (m + 1) * LANES] for m in range(planes)]
        for m in range(planes):
            for axis, rate in ((0, rate_north), (planes, rate_east)):
                face = faces2[g, axis + m : axis + m + 1, :]
                for i, one in enumerate(parts_of(rate + face)):
                    coef2[3 * (axis + m) + i] = one
        for sub in range(SUB):
            fluxes = []
            for m in range(planes):
                here = 3 * m
                more = flag_north2[sub, m] * coef2[here + 2]
                above = state[m + 1] if m + 1 < planes else rolled(state[0], -pitch)
                fluxes.append(
                    (coef2[here] + more) * state[m] + (coef2[here + 1] - more) * above
                )
            cells = [
                state[m] - (fluxes[m] - (fluxes[m - 1] if m else rolled(fluxes[-1], pitch)))
                for m in range(planes)
            ]
            fluxes = []
            for m in range(planes):
                here = 3 * (planes + m)
                more = flag_east2[sub, m] * coef2[here + 2]
                fluxes.append(
                    (coef2[here] + more) * cells[m]
                    + (coef2[here + 1] - more) * rolled(cells[m], -1)
                )
            state = [
                (cells[m] - (fluxes[m] - rolled(fluxes[m], 1))) * sea2[m] for m in range(planes)
            ]
        packed[g] = pack(state, moves, tile_cols)
        return carry

    lax.fori_loop(0, freqs, advect_second, 0)
    back[...] = source(packed[...].reshape(total_rows, LANES)).reshape(freqs, DIRP, LANES)

    def back_copy(f):
        return copy(back.at[f], final.at[me], back_sems, (), (), band, f)

    others(lambda f: back_copy(f).start())
    final[me] = back[me]

    stokes = jnp.dot(
        weight[...], arrive[...].reshape(total_rows, planes * LANES),
        precision=precise, preferred_element_type=f32,
    )
    level = lax.broadcasted_iota(jnp.int32, (LAYERS, LANES), 0)
    planes_of = range(planes)

    def split(x, c):
        return [
            x[c * LAYERS : (c + 1) * LAYERS, m * LANES : (m + 1) * LANES] for m in planes_of
        ]

    def spreading(field):
        outs = []
        for m in planes_of:
            here = field[m]
            above = field[m + 1] if m + 1 < planes else rolled(field[0], -pitch)
            below = field[m - 1] if m else rolled(field[-1], pitch)
            sides = rolled(here, 1) + rolled(here, -1)
            over = jnp.where(level < LAYERS - 1, pltpu.roll(here, LAYERS - 1, 0), 0.0)
            under = jnp.where(level > 0, pltpu.roll(here, 1, 0), 0.0)
            outs.append(
                viscous * (sides + above + below - 4.0 * here)
                + mixing * (over + under - 2.0 * here)
                - friction * here
            )
        return outs

    both = ocean[...]
    u, v = split(both, 0), split(both, 1)
    stokes_east, stokes_north = split(stokes, 0), split(stokes, 1)
    for _ in range(OSTEPS):
        change_u, change_v = spreading(u), spreading(v)
        u, v = (
            [
                (u[m] + ocean_dt * (change_u[m] + coriolis * (v[m] + stokes_north[m])))
                * sea2[m][0:1]
                for m in planes_of
            ],
            [
                (v[m] + ocean_dt * (change_v[m] - coriolis * (u[m] + stokes_east[m])))
                * sea2[m][0:1]
                for m in planes_of
            ],
        )
    for c, field in enumerate((u, v)):
        turned = pack(field, moves, tile_cols).T
        for row in range(rows):
            spot = spot_of[row]
            vout[c, row] = turned[spot * tile_cols : (spot + 1) * tile_cols, :]
    store_ocean = pltpu.make_async_copy(vout, ocean_out, store_sems.at[1])
    store_ocean.start()

    await_bytes(route_out.at[rest], route_sems.at[0, 0])

    @pl.when(has_low)
    def _():
        await_bytes(route_out, route_sems.at[0, 1])
        halo_to_low.wait_send()

    @pl.when(has_high)
    def _():
        await_bytes(route_out, route_sems.at[0, 2])
        halo_to_high.wait_send()

    await_tiles(0)
    for part in range(len(PARTS)):
        await_bytes(leave.at[rest, part_rows(part)], out_sems.at[0, part])

    await_bytes(final.at[rest], back_sems.at[1])
    width = min(freqs, LANES // tile_cols)
    reach = width * tile_cols
    row_at = {spot: row for row, spot in spot_of.items()}
    for chunk in range(freqs // width):
        columns = [final[chunk * width + j] for j in range(width)]
        for i, one in enumerate(swap_pieces(columns, tile_cols, width)):
            for s in range(LANES // reach):
                row = row_at[s * width + i]
                cells = rolled(one, -s * reach)[:, :reach]
                if cols > LANES:
                    done[:, row, chunk * reach : (chunk + 1) * reach] = cells
                else:
                    done.reshape(DIRP * rows, cols)[pl.ds(row, DIRP, stride=rows), :] = cells
    store = pltpu.make_async_copy(done.at[pl.ds(0, DIR)], result, store_sems.at[0])
    store.start()
    await_bytes(back.at[rest], back_sems.at[0])
    store_ocean.wait()
    store.wait()


def body(
    spectrum,
    velocity,
    gain_matrix,
    quad_matrix,
    limiter_flags,
    sea_mask,
    current_route,
    stokes_route,
):
    bands = lax.axis_size("band")
    freqs = lax.axis_size("freq")
    rows, cols = spectrum.shape[2:]
    tile_cols = velocity.shape[3]
    pitch = tile_cols + 2 * HALO
    planes = (rows + 2 * HALO) * pitch // LANES
    tall = rows + 2 * DEPTH
    block = max(LANES, cols)
    n = tall * cols // block
    parts = freqs * DIRP
    assert CYCLES == 2 and spectrum.shape[0] == 1 and rows % 8 == 0 and DEPTH % 8 == 0
    assert rows * tile_cols == LANES and rows >= DEPTH and tile_cols >= HALO >= OSTEPS
    assert pitch == 2 * tile_cols and LANES % pitch == 0 and freqs * tile_cols == cols
    assert (rows + 2 * HALO) % (LANES // pitch) == 0 and cols & (cols - 1) == 0
    assert block % cols == 0 and n * block == tall * cols and cols % pitch == 0
    assert bands > 1 and freqs > 1 and CYCLES * SUB == 8 and 2 * planes <= 8 and block // cols <= 2
    angles = (np.arange(DIR) + 0.5) * (2.0 * np.pi / DIR)
    waves = np.stack([np.cos(angles), np.sin(angles)])
    wave = np.zeros((DIRP, 2), np.float32)
    wave[:DIR] = waves.T
    factor = (0.5 + 1.5 * (np.arange(freqs) + 0.5) / freqs) * DIR ** (-0.5)
    trig = np.zeros((2, freqs, DIRP), np.float32)
    trig[:, :, :DIR] = waves[:, None, :] * factor[None, :, None]
    comps = freqs * DIR
    widen = np.zeros((parts, comps), np.float32)
    index = np.arange(comps)
    widen[index // DIR * DIRP + index % DIR, index] = 1.0
    f32, bf16 = jnp.float32, jnp.bfloat16
    anywhere = pl.BlockSpec(memory_space=pl.ANY)
    scalars = pl.BlockSpec(memory_space=pltpu.SMEM)
    dma = pltpu.SemaphoreType.DMA
    vmem = pltpu.VMEM
    tile_cells = rows * tile_cols
    layers = 2 * LAYERS
    result, ocean = pl.pallas_call(
        functools.partial(kernel, bands, freqs, cols),
        out_shape=(
            jax.ShapeDtypeStruct((DIR, rows, cols), f32),
            jax.ShapeDtypeStruct((2, rows, tile_cols, LAYERS), f32),
        ),
        in_specs=[scalars] * 2 + [anywhere] * 9,
        out_specs=(anywhere, anywhere),
        scratch_shapes=[
            vmem((DIRP, rows, cols), f32),
            vmem((DIRP, DEPTH, cols), f32),
            vmem((DIRP, DEPTH, cols), f32),
            vmem((2, rows, tile_cols, LAYERS), f32),
            vmem((comps, comps), bf16),
            vmem((comps, comps), bf16),
            vmem((parts, comps), bf16),
            vmem((DIRP, 2), f32),
            vmem((2, parts), f32),
            vmem((parts, parts), bf16),
            vmem((parts, parts), bf16),
            vmem(limiter_flags.shape, jnp.int32),
            vmem(sea_mask.shape, jnp.int32),
            vmem((n, 8, block), f32),
            vmem((8 * n, block), f32),
            vmem((SUB, 8 * n, block), f32),
            vmem((SUB, 8 * n, block), f32),
            vmem((SUB, planes, DIRP, LANES), f32),
            vmem((SUB, planes, DIRP, LANES), f32),
            vmem((planes, DIRP, LANES), f32),
            vmem((layers, tile_cells), f32),
            vmem((9, layers, tile_cells), f32),
            vmem((freqs, 2, tile_cells), f32),
            vmem((freqs, 2, tile_cells), f32),
            vmem((freqs, 2, tile_cells), f32),
            vmem((freqs, 2, tile_cells), f32),
            vmem((2, n, block), f32),
            vmem((3, 8 * n, block), f32),
            vmem((freqs, 8, LANES), f32),
            vmem((7, 8 * n, block), f32),
            vmem((6 * planes, DIRP, LANES), f32),
            vmem((freqs, DIRP, planes * LANES), f32),
            vmem((freqs, DIRP, planes * LANES), f32),
            vmem((freqs, DIRP, planes * LANES), f32),
            vmem((freqs, DIRP, LANES), f32),
            vmem((freqs, DIRP, LANES), f32),
            vmem((freqs, DIRP, LANES), f32),
            vmem((DIRP, rows, cols), f32),
            vmem((layers, planes * LANES), f32),
            vmem((layers, parts), f32),
            vmem((2, rows, tile_cols, LAYERS), f32),
            dma((9,)),
            dma((2, 2)),
            dma((2, 3)),
            dma((2,)),
            dma((2, len(PARTS))),
            dma((2,)),
            dma((2,)),
        ],
        compiler_params=pltpu.CompilerParams(
            collective_id=0, has_side_effects=True, vmem_limit_bytes=60 * 1024 * 1024
        ),
    )(
        current_route,
        stokes_route.T,
        spectrum.reshape(DIR, rows, cols),
        velocity.transpose(0, 2, 3, 1),
        gain_matrix,
        quad_matrix,
        limiter_flags,
        sea_mask,
        jnp.asarray(widen, bf16),
        jnp.asarray(wave),
        jnp.asarray(trig.reshape(2, parts)),
    )
    return (result.reshape(1, DIR, rows, cols), ocean.transpose(0, 3, 1, 2))


def solution(mesh):
    return jax.shard_map(
        body,
        mesh=mesh,
        in_specs=(
            P("freq", None, "band", None),
            P(None, None, "band", "freq"),
            P(),
            P(),
            P(),
            P(),
            P(),
            P(),
        ),
        out_specs=(P("freq", None, "band", None), P(None, None, "band", "freq")),
        check_vma=False,
    )
```

```python
import functools

import jax
import jax.numpy as jnp
import numpy as np
from jax import lax
from jax.experimental import pallas as pl
from jax.experimental.pallas import tpu as pltpu
from jax.sharding import PartitionSpec as P

DIR = 36
LAYERS = 24
SUB = 4
CYCLES = 2
OSTEPS = 3


precise = lax.Precision.HIGHEST
ocean_dt = 0.2
viscous = 0.5
coriolis = 1.0
mixing = 0.5
friction = 0.1


GROUP = 8
LANES = 128
DIRP = -(-DIR // GROUP) * GROUP
GROUPS = DIRP // GROUP
HALO = SUB
DEPTH = CYCLES * SUB
PARTS = ((0, 2), (2, GROUPS))
MESH = pl.DeviceIdType.MESH


def swap_pieces(blocks, piece, width):
    lane = lax.broadcasted_iota(jnp.int32, blocks[0].shape, 1)
    out = list(blocks)
    far = width // 2
    while far:
        low = (lane & (far * piece)) == 0
        for a in range(width):
            if a & far:
                continue
            b = a + far
            x, y = out[a], out[b]
            out[a] = jnp.where(low, x, pltpu.roll(y, far * piece, 1))
            out[b] = jnp.where(low, pltpu.roll(x, LANES - far * piece, 1), y)
        far //= 2
    return out


def packing(rows, planes, pitch, tile_cols):
    places = LANES // tile_cols
    free = set(range(places))
    left = {
        m: [q for q in range(LANES // pitch) if 0 <= m + planes * q - HALO < rows]
        for m in range(planes)
    }
    moves, where = [], {}
    while any(left.values()):
        best = None
        for m in range(planes):
            for by in range(places):
                fits = [
                    q for q in left[m] if (q * pitch // tile_cols + by) % places in free
                ]
                if best is None or len(fits) > len(best[2]):
                    best = (m, by, fits)
        m, by, fits = best
        spots = [(q * pitch // tile_cols + by) % places for q in fits]
        moves.append((m, (by * tile_cols - HALO) % LANES, spots))
        for q, spot in zip(fits, spots):
            where[m + planes * q - HALO] = spot
            free.remove(spot)
            left[m].remove(q)
    return moves, where


def pack(blocks, moves, tile_cols):
    lane = lax.broadcasted_iota(jnp.int32, blocks[0].shape, 1)
    total = None
    for m, shift, spots in moves:
        piece = pltpu.roll(blocks[m], shift, 1) if shift else blocks[m]
        if total is None:
            total = piece
            continue
        hit = None
        for spot in spots:
            one = (lane >= spot * tile_cols) & (lane < (spot + 1) * tile_cols)
            hit = one if hit is None else hit | one
        total = jnp.where(hit, piece, total)
    return total


def parts_of(courant):
    up, down = jnp.maximum(courant, 0.0), jnp.minimum(courant, 0.0)
    return up, down, 0.5 * (courant * courant - (up - down))


def kernel(
    bands,
    freqs,
    cols,
    route,
    stokes_route,
    spectrum,
    velocity,
    gain_in,
    quad_in,
    flags_in,
    sea_in,
    widen_in,
    wave_in,
    trig_in,
    result,
    ocean_out,
    spec,
    halo_low,
    halo_high,
    vel,
    gain_raw,
    quad_raw,
    widen,
    wave,
    trig,
    gain,
    quad,
    flag_raw,
    sea_raw,
    flag_blk,
    sea_blk,
    flag_north,
    flag_east,
    flag_north2,
    flag_east2,
    sea2,
    tile,
    tiles,
    route_out,
    route_own,
    route_low,
    route_high,
    drift,
    faces,
    faces2,
    coef,
    coef2,
    leave,
    arrive,
    first,
    packed,
    back,
    final,
    done,
    ocean,
    weight,
    vout,
    load_sems,
    halo_sems,
    route_sems,
    tile_sems,
    out_sems,
    back_sems,
    store_sems,
):
    band = lax.axis_index("band")
    me = lax.axis_index("freq")
    f32 = jnp.float32
    rows = spectrum.shape[1]
    tile_cols = velocity.shape[2]
    tall = rows + 2 * DEPTH
    block = max(LANES, cols)
    slots = block // cols
    n = tall // slots
    pitch = tile_cols + 2 * HALO
    per = LANES // pitch
    planes = (rows + 2 * HALO) // per
    seam = LANES - pitch
    moves, spot_of = packing(rows, planes, pitch, tile_cols)
    has_low = band > 0
    has_high = band < bands - 1

    def others(fn):
        def step(i, carry):
            fn(lax.rem(me + i, freqs))
            return carry

        lax.fori_loop(1, freqs, step, 0)

    def every(fn):
        def step(i, carry):
            fn(i)
            return carry

        lax.fori_loop(0, freqs, step, 0)

    def copy(src, dst, sems, slot_send, slot_recv, to_band, to_freq):
        return pltpu.make_async_remote_copy(
            src_ref=src,
            dst_ref=dst,
            send_sem=sems.at[(0,) + slot_send],
            recv_sem=sems.at[(1,) + slot_recv],
            device_id=(to_band, to_freq),
            device_id_type=MESH,
        )

    def rolled(x, shift):
        shift %= x.shape[1]
        return pltpu.roll(x, shift, 1) if shift else x

    def strided(ref, size, base, at):
        depth = ref.shape[1]
        if cols > LANES:
            return ref[pl.ds(base, size), at, :]
        return ref.reshape(ref.shape[0] * depth, cols)[
            pl.ds(base * depth + at, size, stride=depth), :
        ]

    def await_bytes(ref, sem):
        pltpu.make_async_copy(ref, ref, sem).wait()

    rest = pl.ds(0, freqs - 1)

    barrier = pltpu.get_barrier_semaphore()

    def greet(to_band, to_freq):
        pl.semaphore_signal(barrier, inc=1, device_id=(to_band, to_freq), device_id_type=MESH)

    load_vel = pltpu.make_async_copy(velocity, vel, load_sems.at[0])
    load_vel.start()
    others(lambda f: greet(band, f))

    @pl.when(has_low)
    def _():
        every(lambda f: greet(band - 1, f))

    @pl.when(has_high)
    def _():
        every(lambda f: greet(band + 1, f))

    load_spec = pltpu.make_async_copy(spectrum, spec.at[pl.ds(0, DIR)], load_sems.at[1])
    load_grid = [
        pltpu.make_async_copy(src, dst, load_sems.at[2 + i])
        for i, (src, dst) in enumerate(((flags_in, flag_raw), (sea_in, sea_raw)))
    ]
    loads = [
        pltpu.make_async_copy(src, dst, load_sems.at[4 + i])
        for i, (src, dst) in enumerate(
            (
                (wave_in, wave),
                (gain_in, gain_raw),
                (quad_in, quad_raw),
                (widen_in, widen),
                (trig_in, trig),
            )
        )
    ]
    for one in load_grid:
        one.start()
    load_spec.start()
    for one in loads:
        one.start()

    load_vel.wait()
    for c in range(2):
        field = vel[c].reshape(rows * tile_cols, LAYERS)
        tile[c * LAYERS : (c + 1) * LAYERS, :] = field.T

    def prepare(f):
        route_out[f, 0:1, :] = tile[pl.ds(route[f], 1), :]
        route_out[f, 1:2, :] = tile[pl.ds(LAYERS + route[f], 1), :]

    every(prepare)
    count = freqs - 1 + freqs * (has_low.astype(jnp.int32) + has_high.astype(jnp.int32))
    pl.semaphore_wait(barrier, count)

    halo_to_low = copy(
        spectrum.at[:, pl.ds(0, DEPTH)], halo_high.at[pl.ds(0, DIR)], halo_sems,
        (0,), (0,), band - 1, me,
    )
    halo_to_high = copy(
        spectrum.at[:, pl.ds(rows - DEPTH, DEPTH)], halo_low.at[pl.ds(0, DIR)], halo_sems,
        (1,), (1,), band + 1, me,
    )

    def route_copy(f):
        return copy(route_out.at[f], route_own.at[me], route_sems, (0,), (0,), band, f)

    def route_to_low(f):
        return copy(
            route_out.at[f], route_high.at[me], route_sems, (1,), (1,), band - 1, f
        )

    def route_to_high(f):
        return copy(
            route_out.at[f], route_low.at[me], route_sems, (2,), (2,), band + 1, f
        )

    others(lambda f: route_copy(f).start())

    @pl.when(has_low)
    def _():
        every(lambda f: route_to_low(f).start())
        halo_to_low.start()

    @pl.when(has_high)
    def _():
        every(lambda f: route_to_high(f).start())
        halo_to_high.start()

    def near_tiles(fn):
        for down in (-1, 0, 1):
            for side in (-1, 0, 1):
                if down == 0 and side == 0:
                    continue
                to_band, to_freq = band + down, me + side
                there = (to_band >= 0) & (to_band < bands) & (to_freq >= 0) & (to_freq < freqs)
                mine = 3 * (1 + down) + 1 + side
                fn(there, mine, 8 - mine, to_band, to_freq)

    def tile_copy(mine, theirs, to_band, to_freq):
        return copy(tile, tiles.at[theirs], tile_sems, (), (), to_band, to_freq)

    def tile_start(there, mine, theirs, to_band, to_freq):
        @pl.when(there)
        def _():
            tile_copy(mine, theirs, to_band, to_freq).start()

        @pl.when(jnp.logical_not(there))
        def _():
            tiles[mine] = jnp.zeros_like(tile)

    near_tiles(tile_start)
    tiles[4] = tile[...]
    route_own[me] = route_out[me]

    pads = ((DIR, DIRP - DIR),)
    for at, size in pads:
        spec[at : at + size] = jnp.zeros((size, rows, cols), f32)
        halo_low[at : at + size] = jnp.zeros((size, DEPTH, cols), f32)
        halo_high[at : at + size] = jnp.zeros((size, DEPTH, cols), f32)

    @pl.when(jnp.logical_not(has_low))
    def _():
        halo_low[...] = jnp.zeros_like(halo_low)
        route_low[...] = jnp.zeros_like(route_low)

    @pl.when(jnp.logical_not(has_high))
    def _():
        halo_high[...] = jnp.zeros_like(halo_high)
        route_high[...] = jnp.zeros_like(route_high)

    for one in load_grid:
        one.wait()

    steps = CYCLES * SUB
    all_rows = sea_raw.shape[0]
    wide = (8, block)

    def grid_row(at):
        whole = jnp.clip(band * rows - DEPTH + at, 0, all_rows - 1)
        there = has_low if at < DEPTH else (None if at < DEPTH + rows else has_high)
        flag = strided(flag_raw, steps, 0, whole)
        sea = sea_raw[pl.ds(whole, 1), :].astype(f32)
        flag = flag.astype(f32)
        if there is not None:
            there = there.astype(f32)
            flag, sea = flag * there, sea * there
        return flag, sea

    for k in range(n):
        pieces = [grid_row(k + n * s) for s in range(slots)]
        flag_blk[k] = jnp.concatenate([flag for flag, _ in pieces], axis=1)
        sea = jnp.concatenate([sea for _, sea in pieces], axis=1)
        sea_blk[8 * k : 8 * (k + 1), :] = jnp.broadcast_to(sea, wide)

    for k in range(n):
        here = flag_blk[k]
        above = flag_blk[k + 1] if k + 1 < n else rolled(flag_blk[0], -cols)
        beside = rolled(here, -1)
        for sub in range(SUB):
            there = slice(8 * k, 8 * (k + 1))
            flag_north[sub, there, :] = jnp.broadcast_to(above[sub : sub + 1], wide)
            flag_east[sub, there, :] = jnp.broadcast_to(beside[sub : sub + 1], wide)

    lane = lax.broadcasted_iota(jnp.int32, (8, LANES), 1)
    column = me * tile_cols - HALO + (lane & (pitch - 1))
    inside = (column >= 0) & (column < cols)
    window_flags, window_sea = [], []
    for m in range(planes):
        total_flags, total_sea = jnp.zeros((8, LANES), f32), jnp.zeros((8, LANES), f32)
        for q in range(per):
            at = m + planes * q + DEPTH - HALO
            k, s = at % n, at // n
            shift = lax.rem(q * pitch - cols * s - tile_cols * me + HALO + 2 * block, block)
            hit = (lane >= q * pitch) & (lane < (q + 1) * pitch) & inside
            total_flags = jnp.where(
                hit, pltpu.roll(flag_blk[k], shift, 1)[:, :LANES], total_flags
            )
            total_sea = jnp.where(hit, pltpu.roll(sea_blk[8 * k : 8 * (k + 1), :], shift, 1)[:, :LANES], total_sea)
        window_flags.append(total_flags)
        window_sea.append(total_sea)
    for m in range(planes):
        sea2[m] = jnp.concatenate([window_sea[m]] * GROUPS, axis=0)
        above = window_flags[m + 1] if m + 1 < planes else rolled(window_flags[0], -pitch)
        beside = rolled(window_flags[m], -1)
        for sub in range(SUB):
            step = SUB + sub
            flag_north2[sub, m] = jnp.broadcast_to(above[step : step + 1], (DIRP, LANES))
            flag_east2[sub, m] = jnp.broadcast_to(beside[step : step + 1], (DIRP, LANES))

    load_spec.wait()
    for one in loads:
        one.wait()

    for raw, padded in ((gain_raw, gain), (quad_raw, quad)):
        half = jnp.dot(widen[...], raw[...], preferred_element_type=f32).astype(jnp.bfloat16)
        padded[...] = lax.dot_general(
            half, widen[...], (((1,), (1,)), ((), ())), preferred_element_type=f32
        ).astype(jnp.bfloat16)

    layer = lax.broadcasted_iota(jnp.int32, (LAYERS, 1), 0)
    component = lax.broadcasted_iota(jnp.int32, (LAYERS, freqs * DIRP), 1)
    deposits = jnp.zeros((LAYERS, freqs * DIRP), f32)
    for g in range(freqs):
        deposit = jnp.zeros((LAYERS, 1), f32)
        for j in range(stokes_route.shape[0]):
            hit = (layer == stokes_route[j, g]).astype(f32)
            deposit = deposit + hit * (1.0 / (1.0 + j))
        own = (component >= g * DIRP) & (component < (g + 1) * DIRP)
        deposits = jnp.where(own, deposit, deposits)
    for c in range(2):
        weight[c * LAYERS : (c + 1) * LAYERS, :] = deposits * trig[c : c + 1, :]

    await_bytes(route_own.at[rest], route_sems.at[1, 0])

    @pl.when(has_low)
    def _():
        await_bytes(route_low, route_sems.at[1, 2])

    @pl.when(has_high)
    def _():
        await_bytes(route_high, route_sems.at[1, 1])

    stacks = [
        jnp.concatenate(
            [route_low[j], route_own[j], route_high[j], jnp.zeros((2, LANES), f32)], axis=0
        )
        for j in range(freqs)
    ]
    across = []
    for row in range(rows):
        halves = []
        for half in range(block // LANES):
            total = jnp.zeros((8, LANES), f32)
            reach = min(cols, LANES) // tile_cols
            turned = [
                rolled(stacks[half * reach + j], (j - row) * tile_cols) for j in range(reach)
            ]
            for j, one in enumerate(turned):
                lead = j * tile_cols
                total = jnp.where((lane >= lead) & (lane < lead + tile_cols), one, total)
            halves.append(total)
        across.append(jnp.concatenate(halves, axis=1))
    spreads = 0.15 * jnp.tanh(jnp.concatenate(across, axis=0))
    moved = [spreads] + [rolled(spreads, cols * s) for s in range(1, slots)]
    for row in range(rows):
        for source in range(3):
            at = row + DEPTH + rows * (source - 1)
            if at < 0 or at >= tall:
                continue
            k, s = at % n, at // n
            for c in range(2):
                line = 8 * row + 2 * source + c
                drift[c, k : k + 1, cols * s : cols * (s + 1)] = moved[s][
                    line : line + 1, cols * s : cols * (s + 1)
                ]
    blane = lax.broadcasted_iota(jnp.int32, (1, block), 1)
    last = ((blane & (cols - 1)) == cols - 1).astype(f32)
    inner = 1.0 - last
    east, north = drift[0], drift[1]
    above = jnp.concatenate([north[1:], rolled(north[0:1], -cols)], axis=0)
    for i, face in enumerate(
        (0.5 * (north + above), 0.5 * (inner * east + rolled(east, -1)), 0.5 * east)
    ):
        for k in range(n):
            faces[i, 8 * k : 8 * (k + 1), :] = jnp.broadcast_to(face[k : k + 1], wide)

    @pl.when(has_low)
    def _():
        halo_to_high.wait_recv()

    @pl.when(has_high)
    def _():
        halo_to_low.wait_recv()

    number = me.astype(f32) + 0.5
    my_rate = 0.5 + 0.3 * number / freqs

    def row_of(base, at):
        if at < DEPTH:
            return strided(halo_low, GROUP, base, at)
        if at < DEPTH + rows:
            return strided(spec, GROUP, base, at - DEPTH)
        return strided(halo_high, GROUP, base, at - DEPTH - rows)

    def up(x, by):
        return jnp.concatenate([x[8:], rolled(x[:8], -by)], axis=0)

    def down(x, by):
        return jnp.concatenate([rolled(x[-8:], by), x[:-8]], axis=0)

    def advect_first(group, carry):
        base = group * GROUP
        table = wave[pl.ds(base, GROUP), :]

        def rate_of(i):
            rate = jnp.broadcast_to(table[:, i : i + 1] * my_rate, wide)
            return jnp.concatenate([rate] * n, axis=0)

        rate_east = rate_of(0)
        for axis, rate in ((0, rate_of(1)), (1, rate_east)):
            for i, one in enumerate(parts_of(rate + faces[axis])):
                coef[3 * axis + i] = one
        coef[6] = 1.0 - last * jnp.maximum(rate_east + faces[2], 0.0)
        state = jnp.concatenate(
            [
                jnp.concatenate([row_of(base, k + n * s) for s in range(slots)], axis=1)
                for k in range(n)
            ],
            axis=0,
        )
        for sub in range(SUB):
            more = flag_north[sub] * coef[2]
            flux = (coef[0] + more) * state + (coef[1] - more) * up(state, cols)
            state = state - (flux - down(flux, cols))
            more = flag_east[sub] * coef[5]
            flux = (coef[3] + more) * (inner * state) + (coef[4] - more) * rolled(state, -1)
            state = (coef[6] * state - (inner * flux - rolled(flux, 1))) * sea_blk[...]
        width = min(cols, LANES) // pitch
        low_half = lax.broadcasted_iota(jnp.int32, (8 * planes, LANES), 1) < width * pitch
        for odd in range(2):
            turned = rolled(state, HALO - odd * tile_cols)
            for half in range(block // LANES):
                sources = []
                for i in range(width):
                    pieces = []
                    for s in range(slots):
                        lines = []
                        for m in range(planes):
                            at = m + planes * (i + width * s) + DEPTH - HALO
                            assert at // n == s
                            k = at % n
                            lines.append(
                                turned[8 * k : 8 * (k + 1), half * LANES : (half + 1) * LANES]
                            )
                        pieces.append(jnp.concatenate(lines, axis=0))
                    sources.append(pieces[0] if slots == 1 else jnp.where(low_half, *pieces))
                for e, one in enumerate(swap_pieces(sources, pitch, width)):
                    to = 2 * (e + width * half) + odd
                    for m in range(planes):
                        leave[to, pl.ds(base, GROUP), m * LANES : (m + 1) * LANES] = one[
                            8 * m : 8 * (m + 1)
                        ]
        return carry

    def part_rows(part):
        low, high = PARTS[part]
        return pl.ds(low * GROUP, (high - low) * GROUP)

    def out_copy(part, f):
        there = part_rows(part)
        return copy(
            leave.at[f, there], arrive.at[me, there], out_sems, (part,), (part,), band, f
        )

    for part, (low, high) in enumerate(PARTS):
        [advect_first(i, 0) for i in range(low, high)]
        others(lambda f: out_copy(part, f).start())
    arrive[me] = leave[me]

    deep = 1 + has_low.astype(jnp.int32) + has_high.astype(jnp.int32)
    broad = 1 + (me > 0).astype(jnp.int32) + (me < freqs - 1).astype(jnp.int32)

    def await_tiles(way):
        for a in (2, 3):
            for b in (2, 3):

                @pl.when((deep == a) & (broad == b))
                def _():
                    await_bytes(tiles.at[pl.ds(0, a * b - 1)], tile_sems.at[way])

    await_tiles(1)
    tall_lane = lax.broadcasted_iota(jnp.int32, tile.shape, 1)
    for m in range(planes):
        total = jnp.zeros(tile.shape, f32)
        for q in range(per):
            row = m + planes * q - HALO
            down = 0 if row < 0 else (1 if row < rows else 2)
            from_row = row + rows * (1 - down)
            lead = q * pitch
            for side, width, from_col in (
                (0, HALO, tile_cols - HALO), (1, tile_cols, 0), (2, HALO, 0),
            ):
                piece = rolled(tiles[3 * down + side], lead - from_row * tile_cols - from_col)
                total = jnp.where((tall_lane >= lead) & (tall_lane < lead + width), piece, total)
                lead += width
        ocean[:, m * LANES : (m + 1) * LANES] = total

    def face_step(g, carry):
        east = 0.15 * jnp.tanh(ocean[pl.ds(route[g], 1), :])
        north = 0.15 * jnp.tanh(ocean[pl.ds(LAYERS + route[g], 1), :])
        for m in range(planes):
            here = north[:, m * LANES : (m + 1) * LANES]
            above = (
                north[:, (m + 1) * LANES : (m + 2) * LANES]
                if m + 1 < planes
                else rolled(north[:, :LANES], -pitch)
            )
            faces2[g, m : m + 1, :] = 0.5 * (here + above)
            here = east[:, m * LANES : (m + 1) * LANES]
            faces2[g, planes + m : planes + m + 1, :] = 0.5 * (here + rolled(here, -1))
        return carry

    lax.fori_loop(0, freqs, face_step, 0)

    for part in range(len(PARTS)):
        await_bytes(arrive.at[rest, part_rows(part)], out_sems.at[1, part])

    def source(whole):
        grown = jnp.dot(gain[...], whole.astype(jnp.bfloat16), preferred_element_type=f32)
        quartic = jnp.dot(
            quad[...], (whole * whole).astype(jnp.bfloat16), preferred_element_type=f32
        )
        return whole * (1.0 + 0.5 * jnp.tanh(grown) - 0.25 * jnp.tanh(quartic))

    total_rows = freqs * DIRP
    for m in range(planes):
        there = slice(m * LANES, (m + 1) * LANES)
        whole = arrive[:, :, there].reshape(total_rows, LANES) * sea2[m][0:1]
        first[:, :, there] = source(whole).reshape(freqs, DIRP, LANES)

    def advect_second(g, carry):
        rate = 0.5 + 0.3 * (g.astype(f32) + 0.5) / freqs
        table = wave[...] * rate
        rate_east = jnp.broadcast_to(table[:, 0:1], (DIRP, LANES))
        rate_north = jnp.broadcast_to(table[:, 1:2], (DIRP, LANES))
        state = [first[g, :, m * LANES : (m + 1) * LANES] for m in range(planes)]
        for m in range(planes):
            for axis, rate in ((0, rate_north), (planes, rate_east)):
                face = faces2[g, axis + m : axis + m + 1, :]
                for i, one in enumerate(parts_of(rate + face)):
                    coef2[3 * (axis + m) + i] = one
        for sub in range(SUB):
            fluxes = []
            for m in range(planes):
                here = 3 * m
                more = flag_north2[sub, m] * coef2[here + 2]
                above = state[m + 1] if m + 1 < planes else rolled(state[0], -pitch)
                fluxes.append(
                    (coef2[here] + more) * state[m] + (coef2[here + 1] - more) * above
                )
            cells = [
                state[m] - (fluxes[m] - (fluxes[m - 1] if m else rolled(fluxes[-1], pitch)))
                for m in range(planes)
            ]
            fluxes = []
            for m in range(planes):
                here = 3 * (planes + m)
                more = flag_east2[sub, m] * coef2[here + 2]
                fluxes.append(
                    (coef2[here] + more) * cells[m]
                    + (coef2[here + 1] - more) * rolled(cells[m], -1)
                )
            state = [
                (cells[m] - (fluxes[m] - rolled(fluxes[m], 1))) * sea2[m] for m in range(planes)
            ]
        packed[g] = pack(state, moves, tile_cols)
        return carry

    [advect_second(jnp.int32(g), 0) for g in range(freqs)]
    back[...] = source(packed[...].reshape(total_rows, LANES)).reshape(freqs, DIRP, LANES)

    def back_copy(f):
        return copy(back.at[f], final.at[me], back_sems, (), (), band, f)

    others(lambda f: back_copy(f).start())
    final[me] = back[me]

    stokes = jnp.dot(
        weight[...], arrive[...].reshape(total_rows, planes * LANES),
        precision=precise, preferred_element_type=f32,
    )
    level = lax.broadcasted_iota(jnp.int32, (LAYERS, LANES), 0)
    planes_of = range(planes)

    def split(x, c):
        return [
            x[c * LAYERS : (c + 1) * LAYERS, m * LANES : (m + 1) * LANES] for m in planes_of
        ]

    def spreading(field):
        outs = []
        for m in planes_of:
            here = field[m]
            above = field[m + 1] if m + 1 < planes else rolled(field[0], -pitch)
            below = field[m - 1] if m else rolled(field[-1], pitch)
            sides = rolled(here, 1) + rolled(here, -1)
            over = jnp.where(level < LAYERS - 1, pltpu.roll(here, LAYERS - 1, 0), 0.0)
            under = jnp.where(level > 0, pltpu.roll(here, 1, 0), 0.0)
            outs.append(
                viscous * (sides + above + below - 4.0 * here)
                + mixing * (over + under - 2.0 * here)
                - friction * here
            )
        return outs

    both = ocean[...]
    u, v = split(both, 0), split(both, 1)
    stokes_east, stokes_north = split(stokes, 0), split(stokes, 1)
    for _ in range(OSTEPS):
        change_u, change_v = spreading(u), spreading(v)
        u, v = (
            [
                (u[m] + ocean_dt * (change_u[m] + coriolis * (v[m] + stokes_north[m])))
                * sea2[m][0:1]
                for m in planes_of
            ],
            [
                (v[m] + ocean_dt * (change_v[m] - coriolis * (u[m] + stokes_east[m])))
                * sea2[m][0:1]
                for m in planes_of
            ],
        )
    for c, field in enumerate((u, v)):
        turned = pack(field, moves, tile_cols).T
        for row in range(rows):
            spot = spot_of[row]
            vout[c, row] = turned[spot * tile_cols : (spot + 1) * tile_cols, :]
    store_ocean = pltpu.make_async_copy(vout, ocean_out, store_sems.at[1])
    store_ocean.start()

    await_bytes(route_out.at[rest], route_sems.at[0, 0])

    @pl.when(has_low)
    def _():
        await_bytes(route_out, route_sems.at[0, 1])
        halo_to_low.wait_send()

    @pl.when(has_high)
    def _():
        await_bytes(route_out, route_sems.at[0, 2])
        halo_to_high.wait_send()

    await_tiles(0)
    for part in range(len(PARTS)):
        await_bytes(leave.at[rest, part_rows(part)], out_sems.at[0, part])

    await_bytes(final.at[rest], back_sems.at[1])
    width = min(freqs, LANES // tile_cols)
    reach = width * tile_cols
    row_at = {spot: row for row, spot in spot_of.items()}
    for chunk in range(freqs // width):
        columns = [final[chunk * width + j] for j in range(width)]
        for i, one in enumerate(swap_pieces(columns, tile_cols, width)):
            for s in range(LANES // reach):
                row = row_at[s * width + i]
                cells = rolled(one, -s * reach)[:, :reach]
                if cols > LANES:
                    done[:, row, chunk * reach : (chunk + 1) * reach] = cells
                else:
                    done.reshape(DIRP * rows, cols)[pl.ds(row, DIRP, stride=rows), :] = cells
    store = pltpu.make_async_copy(done.at[pl.ds(0, DIR)], result, store_sems.at[0])
    store.start()
    await_bytes(back.at[rest], back_sems.at[0])
    store_ocean.wait()
    store.wait()


def body(
    spectrum,
    velocity,
    gain_matrix,
    quad_matrix,
    limiter_flags,
    sea_mask,
    current_route,
    stokes_route,
):
    bands = lax.axis_size("band")
    freqs = lax.axis_size("freq")
    rows, cols = spectrum.shape[2:]
    tile_cols = velocity.shape[3]
    pitch = tile_cols + 2 * HALO
    planes = (rows + 2 * HALO) * pitch // LANES
    tall = rows + 2 * DEPTH
    block = max(LANES, cols)
    n = tall * cols // block
    parts = freqs * DIRP
    assert CYCLES == 2 and spectrum.shape[0] == 1 and rows % 8 == 0 and DEPTH % 8 == 0
    assert rows * tile_cols == LANES and rows >= DEPTH and tile_cols >= HALO >= OSTEPS
    assert pitch == 2 * tile_cols and LANES % pitch == 0 and freqs * tile_cols == cols
    assert (rows + 2 * HALO) % (LANES // pitch) == 0 and cols & (cols - 1) == 0
    assert block % cols == 0 and n * block == tall * cols and cols % pitch == 0
    assert bands > 1 and freqs > 1 and CYCLES * SUB == 8 and 2 * planes <= 8 and block // cols <= 2
    angles = (np.arange(DIR) + 0.5) * (2.0 * np.pi / DIR)
    waves = np.stack([np.cos(angles), np.sin(angles)])
    wave = np.zeros((DIRP, 2), np.float32)
    wave[:DIR] = waves.T
    factor = (0.5 + 1.5 * (np.arange(freqs) + 0.5) / freqs) * DIR ** (-0.5)
    trig = np.zeros((2, freqs, DIRP), np.float32)
    trig[:, :, :DIR] = waves[:, None, :] * factor[None, :, None]
    comps = freqs * DIR
    widen = np.zeros((parts, comps), np.float32)
    index = np.arange(comps)
    widen[index // DIR * DIRP + index % DIR, index] = 1.0
    f32, bf16 = jnp.float32, jnp.bfloat16
    anywhere = pl.BlockSpec(memory_space=pl.ANY)
    scalars = pl.BlockSpec(memory_space=pltpu.SMEM)
    dma = pltpu.SemaphoreType.DMA
    vmem = pltpu.VMEM
    tile_cells = rows * tile_cols
    layers = 2 * LAYERS
    result, ocean = pl.pallas_call(
        functools.partial(kernel, bands, freqs, cols),
        out_shape=(
            jax.ShapeDtypeStruct((DIR, rows, cols), f32),
            jax.ShapeDtypeStruct((2, rows, tile_cols, LAYERS), f32),
        ),
        in_specs=[scalars] * 2 + [anywhere] * 9,
        out_specs=(anywhere, anywhere),
        scratch_shapes=[
            vmem((DIRP, rows, cols), f32),
            vmem((DIRP, DEPTH, cols), f32),
            vmem((DIRP, DEPTH, cols), f32),
            vmem((2, rows, tile_cols, LAYERS), f32),
            vmem((comps, comps), bf16),
            vmem((comps, comps), bf16),
            vmem((parts, comps), bf16),
            vmem((DIRP, 2), f32),
            vmem((2, parts), f32),
            vmem((parts, parts), bf16),
            vmem((parts, parts), bf16),
            vmem(limiter_flags.shape, jnp.int32),
            vmem(sea_mask.shape, jnp.int32),
            vmem((n, 8, block), f32),
            vmem((8 * n, block), f32),
            vmem((SUB, 8 * n, block), f32),
            vmem((SUB, 8 * n, block), f32),
            vmem((SUB, planes, DIRP, LANES), f32),
            vmem((SUB, planes, DIRP, LANES), f32),
            vmem((planes, DIRP, LANES), f32),
            vmem((layers, tile_cells), f32),
            vmem((9, layers, tile_cells), f32),
            vmem((freqs, 2, tile_cells), f32),
            vmem((freqs, 2, tile_cells), f32),
            vmem((freqs, 2, tile_cells), f32),
            vmem((freqs, 2, tile_cells), f32),
            vmem((2, n, block), f32),
            vmem((3, 8 * n, block), f32),
            vmem((freqs, 8, LANES), f32),
            vmem((7, 8 * n, block), f32),
            vmem((6 * planes, DIRP, LANES), f32),
            vmem((freqs, DIRP, planes * LANES), f32),
            vmem((freqs, DIRP, planes * LANES), f32),
            vmem((freqs, DIRP, planes * LANES), f32),
            vmem((freqs, DIRP, LANES), f32),
            vmem((freqs, DIRP, LANES), f32),
            vmem((freqs, DIRP, LANES), f32),
            vmem((DIRP, rows, cols), f32),
            vmem((layers, planes * LANES), f32),
            vmem((layers, parts), f32),
            vmem((2, rows, tile_cols, LAYERS), f32),
            dma((9,)),
            dma((2, 2)),
            dma((2, 3)),
            dma((2,)),
            dma((2, len(PARTS))),
            dma((2,)),
            dma((2,)),
        ],
        compiler_params=pltpu.CompilerParams(
            collective_id=0, has_side_effects=True, vmem_limit_bytes=60 * 1024 * 1024
        ),
    )(
        current_route,
        stokes_route.T,
        spectrum.reshape(DIR, rows, cols),
        velocity.transpose(0, 2, 3, 1),
        gain_matrix,
        quad_matrix,
        limiter_flags,
        sea_mask,
        jnp.asarray(widen, bf16),
        jnp.asarray(wave),
        jnp.asarray(trig.reshape(2, parts)),
    )
    return (result.reshape(1, DIR, rows, cols), ocean.transpose(0, 3, 1, 2))


def solution(mesh):
    return jax.shard_map(
        body,
        mesh=mesh,
        in_specs=(
            P("freq", None, "band", None),
            P(None, None, "band", "freq"),
            P(),
            P(),
            P(),
            P(),
            P(),
            P(),
        ),
        out_specs=(P("freq", None, "band", None), P(None, None, "band", "freq")),
        check_vma=False,
    )
```

```python
import functools

import jax
import jax.numpy as jnp
import numpy as np
from jax import lax
from jax.experimental import pallas as pl
from jax.experimental.pallas import tpu as pltpu
from jax.sharding import PartitionSpec as P

DIR = 36
LAYERS = 24
SUB = 4
CYCLES = 2
OSTEPS = 3


precise = lax.Precision.HIGHEST
ocean_dt = 0.2
viscous = 0.5
coriolis = 1.0
mixing = 0.5
friction = 0.1


GROUP = 8
LANES = 128
DIRP = -(-DIR // GROUP) * GROUP
GROUPS = DIRP // GROUP
HALO = SUB
DEPTH = CYCLES * SUB
PARTS = ((0, 1), (1, 3), (3, GROUPS))
MESH = pl.DeviceIdType.MESH


def swap_pieces(blocks, piece, width):
    lane = lax.broadcasted_iota(jnp.int32, blocks[0].shape, 1)
    out = list(blocks)
    far = width // 2
    while far:
        low = (lane & (far * piece)) == 0
        for a in range(width):
            if a & far:
                continue
            b = a + far
            x, y = out[a], out[b]
            out[a] = jnp.where(low, x, pltpu.roll(y, far * piece, 1))
            out[b] = jnp.where(low, pltpu.roll(x, LANES - far * piece, 1), y)
        far //= 2
    return out


def packing(rows, planes, pitch, tile_cols):
    places = LANES // tile_cols
    free = set(range(places))
    left = {
        m: [q for q in range(LANES // pitch) if 0 <= m + planes * q - HALO < rows]
        for m in range(planes)
    }
    moves, where = [], {}
    while any(left.values()):
        best = None
        for m in range(planes):
            for by in range(places):
                fits = [
                    q for q in left[m] if (q * pitch // tile_cols + by) % places in free
                ]
                if best is None or len(fits) > len(best[2]):
                    best = (m, by, fits)
        m, by, fits = best
        spots = [(q * pitch // tile_cols + by) % places for q in fits]
        moves.append((m, (by * tile_cols - HALO) % LANES, spots))
        for q, spot in zip(fits, spots):
            where[m + planes * q - HALO] = spot
            free.remove(spot)
            left[m].remove(q)
    return moves, where


def pack(blocks, moves, tile_cols):
    lane = lax.broadcasted_iota(jnp.int32, blocks[0].shape, 1)
    total = None
    for m, shift, spots in moves:
        piece = pltpu.roll(blocks[m], shift, 1) if shift else blocks[m]
        if total is None:
            total = piece
            continue
        hit = None
        for spot in spots:
            one = (lane >= spot * tile_cols) & (lane < (spot + 1) * tile_cols)
            hit = one if hit is None else hit | one
        total = jnp.where(hit, piece, total)
    return total


def parts_of(courant):
    up, down = jnp.maximum(courant, 0.0), jnp.minimum(courant, 0.0)
    return up, down, 0.5 * (courant * courant - (up - down))


def kernel(
    bands,
    freqs,
    cols,
    route_in,
    stokes_in,
    spectrum,
    velocity,
    gain_in,
    quad_in,
    flags_in,
    sea_in,
    widen_in,
    wave_in,
    trig_in,
    final,
    ocean_out,
    route,
    stokes_route,
    spec,
    halo_low,
    halo_high,
    vel,
    gain_raw,
    quad_raw,
    widen,
    wave,
    trig,
    gain,
    quad,
    flag_raw,
    sea_raw,
    flag_blk,
    sea_blk,
    flag_north,
    flag_east,
    flag_north2,
    flag_east2,
    sea2,
    tile,
    ready,
    tiles,
    route_out,
    route_own,
    route_low,
    route_high,
    drift,
    faces,
    faces2,
    coef,
    coef2,
    leave,
    arrive,
    first,
    packed,
    back,
    ocean,
    weight,
    flat,
    load_sems,
    halo_sems,
    route_sems,
    tile_sems,
    out_sems,
    back_sems,
    store_sems,
):
    band = lax.axis_index("band")
    me = lax.axis_index("freq")
    f32 = jnp.float32
    rows = spectrum.shape[1]
    tile_cols = velocity.shape[2]
    tall = rows + 2 * DEPTH
    block = max(LANES, cols)
    slots = block // cols
    n = tall // slots
    pitch = tile_cols + 2 * HALO
    per = LANES // pitch
    planes = (rows + 2 * HALO) // per
    seam = LANES - pitch
    moves, spot_of = packing(rows, planes, pitch, tile_cols)
    has_low = band > 0
    has_high = band < bands - 1

    mid = freqs // 2
    side, place = me // mid, lax.rem(me, mid)
    near = [side * mid + lax.rem(place + i, mid) for i in [*range(2, mid), 1][: mid - 1]]
    far = [(1 - side) * mid + lax.rem(2 * mid - 1 - place - i, mid) for i in range(mid)]
    partners = []
    for i in range(mid):
        partners += near[i : i + 1] + [far[i]]

    def others(fn):
        for f in partners:
            fn(f)

    def every(fn):
        for f in range(freqs):
            fn(f)

    def copy(src, dst, sems, slot_send, slot_recv, to_band, to_freq):
        return pltpu.make_async_remote_copy(
            src_ref=src,
            dst_ref=dst,
            send_sem=sems.at[(0,) + slot_send],
            recv_sem=sems.at[(1,) + slot_recv],
            device_id=(to_band, to_freq),
            device_id_type=MESH,
        )

    def rolled(x, shift):
        shift %= x.shape[1]
        return pltpu.roll(x, shift, 1) if shift else x

    def strided(ref, size, base, at):
        depth = ref.shape[1]
        if cols > LANES:
            return ref[pl.ds(base, size), at, :]
        return ref.reshape(ref.shape[0] * depth, cols)[
            pl.ds(base * depth + at, size, stride=depth), :
        ]

    def await_bytes(ref, sem):
        pltpu.make_async_copy(ref, ref, sem).wait()

    rest = pl.ds(0, freqs - 1)

    barrier = pltpu.get_barrier_semaphore()

    def greet(to_band, to_freq):
        pl.semaphore_signal(barrier, inc=1, device_id=(to_band, to_freq), device_id_type=MESH)

    others(lambda f: greet(band, f))

    @pl.when(has_low)
    def _():
        every(lambda f: greet(band - 1, f))

    @pl.when(has_high)
    def _():
        every(lambda f: greet(band + 1, f))

    load_vel = pltpu.make_async_copy(velocity, vel, load_sems.at[0])
    load_vel.start()
    load_route = pltpu.make_async_copy(route_in, route, load_sems.at[9])
    load_route.start()
    load_stokes = pltpu.make_async_copy(stokes_in, stokes_route, load_sems.at[10])
    load_stokes.start()
    load_spec = pltpu.make_async_copy(spectrum, spec.at[pl.ds(0, DIR)], load_sems.at[1])
    load_grid = [
        pltpu.make_async_copy(src, dst, load_sems.at[2 + i])
        for i, (src, dst) in enumerate(((flags_in, flag_raw), (sea_in, sea_raw)))
    ]
    loads = [
        pltpu.make_async_copy(src, dst, load_sems.at[4 + i])
        for i, (src, dst) in enumerate(
            (
                (wave_in, wave),
                (gain_in, gain_raw),
                (quad_in, quad_raw),
                (widen_in, widen),
                (trig_in, trig),
            )
        )
    ]
    for one in load_grid:
        one.start()
    load_spec.start()
    for one in loads:
        one.start()

    load_vel.wait()
    for c in range(2):
        field = vel[c].reshape(rows * tile_cols, LAYERS)
        tile[c * LAYERS : (c + 1) * LAYERS, :] = field.T

    ready[...] = pltpu.roll(
        0.15 * jnp.tanh(tile[...]), lax.rem(me * tile_cols, LANES), 1
    )

    def prepare(f):
        route_out[f, 0:1, :] = ready[pl.ds(route[f], 1), :]
        route_out[f, 1:2, :] = ready[pl.ds(LAYERS + route[f], 1), :]

    load_route.wait()
    every(prepare)
    count = freqs - 1 + freqs * (has_low.astype(jnp.int32) + has_high.astype(jnp.int32))
    pl.semaphore_wait(barrier, count)

    halo_to_low = copy(
        spectrum.at[:, pl.ds(0, DEPTH)], halo_high.at[pl.ds(0, DIR)], halo_sems,
        (0,), (0,), band - 1, me,
    )
    halo_to_high = copy(
        spectrum.at[:, pl.ds(rows - DEPTH, DEPTH)], halo_low.at[pl.ds(0, DIR)], halo_sems,
        (1,), (1,), band + 1, me,
    )

    def route_copy(f):
        return copy(route_out.at[f], route_own.at[me], route_sems, (0,), (0,), band, f)

    def route_to_low(f):
        return copy(
            route_out.at[f], route_high.at[me], route_sems, (1,), (1,), band - 1, f
        )

    def route_to_high(f):
        return copy(
            route_out.at[f], route_low.at[me], route_sems, (2,), (2,), band + 1, f
        )

    others(lambda f: route_copy(f).start())

    @pl.when(has_low)
    def _():
        every(lambda f: route_to_low(f).start())
        halo_to_low.start()

    @pl.when(has_high)
    def _():
        every(lambda f: route_to_high(f).start())
        halo_to_high.start()

    def near_tiles(fn):
        for down in (-1, 0, 1):
            for side in (-1, 0, 1):
                if down == 0 and side == 0:
                    continue
                to_band, to_freq = band + down, me + side
                there = (to_band >= 0) & (to_band < bands) & (to_freq >= 0) & (to_freq < freqs)
                mine = 3 * (1 + down) + 1 + side
                fn(there, mine, 8 - mine, to_band, to_freq)

    def tile_copy(mine, theirs, to_band, to_freq):
        return copy(tile, tiles.at[theirs], tile_sems, (), (), to_band, to_freq)

    def tile_start(there, mine, theirs, to_band, to_freq):
        @pl.when(there)
        def _():
            tile_copy(mine, theirs, to_band, to_freq).start()

        @pl.when(jnp.logical_not(there))
        def _():
            tiles[mine] = jnp.zeros_like(tile)

    near_tiles(tile_start)
    tiles[4] = tile[...]
    route_own[me] = route_out[me]

    pads = ((DIR, DIRP - DIR),)
    for at, size in pads:
        spec[at : at + size] = jnp.zeros((size, rows, cols), f32)
        halo_low[at : at + size] = jnp.zeros((size, DEPTH, cols), f32)
        halo_high[at : at + size] = jnp.zeros((size, DEPTH, cols), f32)

    @pl.when(jnp.logical_not(has_low))
    def _():
        halo_low[...] = jnp.zeros_like(halo_low)
        route_low[...] = jnp.zeros_like(route_low)

    @pl.when(jnp.logical_not(has_high))
    def _():
        halo_high[...] = jnp.zeros_like(halo_high)
        route_high[...] = jnp.zeros_like(route_high)

    for one in load_grid:
        one.wait()

    steps = CYCLES * SUB
    all_rows = sea_raw.shape[0]
    wide = (8, block)

    def grid_row(at):
        whole = jnp.clip(band * rows - DEPTH + at, 0, all_rows - 1)
        there = has_low if at < DEPTH else (None if at < DEPTH + rows else has_high)
        flag = strided(flag_raw, steps, 0, whole)
        sea = sea_raw[pl.ds(whole, 1), :].astype(f32)
        flag = flag.astype(f32)
        if there is not None:
            there = there.astype(f32)
            flag, sea = flag * there, sea * there
        return flag, sea

    for k in range(n):
        pieces = [grid_row(k + n * s) for s in range(slots)]
        flag_blk[k] = jnp.concatenate([flag for flag, _ in pieces], axis=1)
        sea = jnp.concatenate([sea for _, sea in pieces], axis=1)
        sea_blk[8 * k : 8 * (k + 1), :] = jnp.broadcast_to(sea, wide)

    for k in range(n):
        here = flag_blk[k]
        above = flag_blk[k + 1] if k + 1 < n else rolled(flag_blk[0], -cols)
        beside = rolled(here, -1)
        for sub in range(SUB):
            there = slice(8 * k, 8 * (k + 1))
            flag_north[sub, there, :] = jnp.broadcast_to(above[sub : sub + 1], wide)
            flag_east[sub, there, :] = jnp.broadcast_to(beside[sub : sub + 1], wide)

    lane = lax.broadcasted_iota(jnp.int32, (8, LANES), 1)
    column = me * tile_cols - HALO + (lane & (pitch - 1))
    inside = (column >= 0) & (column < cols)
    window_flags, window_sea = [], []
    for m in range(planes):
        total_flags, total_sea = jnp.zeros((8, LANES), f32), jnp.zeros((8, LANES), f32)
        for q in range(per):
            at = m + planes * q + DEPTH - HALO
            k, s = at % n, at // n
            shift = lax.rem(q * pitch - cols * s - tile_cols * me + HALO + 2 * block, block)
            hit = (lane >= q * pitch) & (lane < (q + 1) * pitch) & inside
            total_flags = jnp.where(
                hit, pltpu.roll(flag_blk[k], shift, 1)[:, :LANES], total_flags
            )
            total_sea = jnp.where(hit, pltpu.roll(sea_blk[8 * k : 8 * (k + 1), :], shift, 1)[:, :LANES], total_sea)
        window_flags.append(total_flags)
        window_sea.append(total_sea)
    for m in range(planes):
        sea2[m] = jnp.concatenate([window_sea[m]] * GROUPS, axis=0)
        above = window_flags[m + 1] if m + 1 < planes else rolled(window_flags[0], -pitch)
        beside = rolled(window_flags[m], -1)
        for sub in range(SUB):
            step = SUB + sub
            flag_north2[sub, m] = jnp.broadcast_to(above[step : step + 1], (DIRP, LANES))
            flag_east2[sub, m] = jnp.broadcast_to(beside[step : step + 1], (DIRP, LANES))

    load_spec.wait()
    load_stokes.wait()
    for one in loads:
        one.wait()

    for raw, padded in ((gain_raw, gain), (quad_raw, quad)):
        half = jnp.dot(widen[...], raw[...], preferred_element_type=f32).astype(jnp.bfloat16)
        padded[...] = lax.dot_general(
            half, widen[...], (((1,), (1,)), ((), ())), preferred_element_type=f32
        ).astype(jnp.bfloat16)

    layer = lax.broadcasted_iota(jnp.int32, (LAYERS, 1), 0)
    component = lax.broadcasted_iota(jnp.int32, (LAYERS, freqs * DIRP), 1)
    deposits = jnp.zeros((LAYERS, freqs * DIRP), f32)
    for g in range(freqs):
        deposit = jnp.zeros((LAYERS, 1), f32)
        for j in range(stokes_route.shape[0]):
            hit = (layer == stokes_route[j, g]).astype(f32)
            deposit = deposit + hit * (1.0 / (1.0 + j))
        own = (component >= g * DIRP) & (component < (g + 1) * DIRP)
        deposits = jnp.where(own, deposit, deposits)
    for c in range(2):
        weight[c * LAYERS : (c + 1) * LAYERS, :] = deposits * trig[c : c + 1, :]

    await_bytes(route_own.at[rest], route_sems.at[1, 0])

    @pl.when(has_low)
    def _():
        await_bytes(route_low, route_sems.at[1, 2])

    @pl.when(has_high)
    def _():
        await_bytes(route_high, route_sems.at[1, 1])

    stacks = [
        jnp.concatenate(
            [route_low[j], route_own[j], route_high[j], jnp.zeros((2, LANES), f32)], axis=0
        )
        for j in range(freqs)
    ]
    reach = min(cols, LANES) // tile_cols
    places = LANES // tile_cols
    spot_masks = [
        (lane >= spot * tile_cols) & (lane < (spot + 1) * tile_cols) for spot in range(places)
    ]
    for row in range(rows):
        halves = []
        for half in range(block // LANES):
            total = stacks[half * reach]
            for j in range(1, reach):
                total = jnp.where(
                    spot_masks[(row + j) % places], stacks[half * reach + j], total
                )
            halves.append(total)
        moved = []
        for s in range(slots):
            turned = [rolled(x, cols * s - row * tile_cols) for x in halves]
            moved.append(turned[0] if len(turned) == 1 else jnp.concatenate(turned, axis=1))
        for source in range(3):
            at = row + DEPTH + rows * (source - 1)
            if at < 0 or at >= tall:
                continue
            k, s = at % n, at // n
            for c in range(2):
                line = 2 * source + c
                drift[c, k : k + 1, cols * s : cols * (s + 1)] = moved[s][
                    line : line + 1, cols * s : cols * (s + 1)
                ]
    blane = lax.broadcasted_iota(jnp.int32, (1, block), 1)
    last = ((blane & (cols - 1)) == cols - 1).astype(f32)
    inner = 1.0 - last
    east, north = drift[0], drift[1]
    above = jnp.concatenate([north[1:], rolled(north[0:1], -cols)], axis=0)
    for i, face in enumerate(
        (0.5 * (north + above), 0.5 * (inner * east + rolled(east, -1)), 0.5 * east)
    ):
        for k in range(n):
            faces[i, 8 * k : 8 * (k + 1), :] = jnp.broadcast_to(face[k : k + 1], wide)

    @pl.when(has_low)
    def _():
        halo_to_high.wait_recv()

    @pl.when(has_high)
    def _():
        halo_to_low.wait_recv()

    number = me.astype(f32) + 0.5
    my_rate = 0.5 + 0.3 * number / freqs

    def row_of(base, at):
        if at < DEPTH:
            return strided(halo_low, GROUP, base, at)
        if at < DEPTH + rows:
            return strided(spec, GROUP, base, at - DEPTH)
        return strided(halo_high, GROUP, base, at - DEPTH - rows)

    def up(x, by):
        return jnp.concatenate([x[8:], rolled(x[:8], -by)], axis=0)

    def down(x, by):
        return jnp.concatenate([rolled(x[-8:], by), x[:-8]], axis=0)

    def advect_first(group, carry):
        base = group * GROUP
        table = wave[pl.ds(base, GROUP), :]

        def rate_of(i):
            rate = jnp.broadcast_to(table[:, i : i + 1] * my_rate, wide)
            return jnp.concatenate([rate] * n, axis=0)

        rate_east = rate_of(0)
        for axis, rate in ((0, rate_of(1)), (1, rate_east)):
            for i, one in enumerate(parts_of(rate + faces[axis])):
                coef[3 * axis + i] = one
        coef[6] = 1.0 - last * jnp.maximum(rate_east + faces[2], 0.0)
        state = jnp.concatenate(
            [
                jnp.concatenate([row_of(base, k + n * s) for s in range(slots)], axis=1)
                for k in range(n)
            ],
            axis=0,
        )
        for sub in range(SUB):
            more = flag_north[sub] * coef[2]
            flux = (coef[0] + more) * state + (coef[1] - more) * up(state, cols)
            state = state - (flux - down(flux, cols))
            more = flag_east[sub] * coef[5]
            flux = (coef[3] + more) * (inner * state) + (coef[4] - more) * rolled(state, -1)
            state = (coef[6] * state - (inner * flux - rolled(flux, 1))) * sea_blk[...]
        width = min(cols, LANES) // pitch
        low_half = lax.broadcasted_iota(jnp.int32, (8 * planes, LANES), 1) < width * pitch
        for odd in range(2):
            turned = rolled(state, HALO - odd * tile_cols)
            for half in range(block // LANES):
                sources = []
                for i in range(width):
                    pieces = []
                    for s in range(slots):
                        lines = []
                        for m in range(planes):
                            at = m + planes * (i + width * s) + DEPTH - HALO
                            assert at // n == s
                            k = at % n
                            lines.append(
                                turned[8 * k : 8 * (k + 1), half * LANES : (half + 1) * LANES]
                            )
                        pieces.append(jnp.concatenate(lines, axis=0))
                    sources.append(pieces[0] if slots == 1 else jnp.where(low_half, *pieces))
                for e, one in enumerate(swap_pieces(sources, pitch, width)):
                    to = 2 * (e + width * half) + odd
                    for m in range(planes):
                        leave[to, pl.ds(base, GROUP), m * LANES : (m + 1) * LANES] = one[
                            8 * m : 8 * (m + 1)
                        ]
        return carry

    def part_rows(part):
        low, high = PARTS[part]
        return pl.ds(low * GROUP, (high - low) * GROUP)

    def out_copy(part, f):
        there = part_rows(part)
        return copy(
            leave.at[f, there], arrive.at[me, there], out_sems, (part,), (part,), band, f
        )

    for part, (low, high) in enumerate(PARTS):
        [advect_first(i, 0) for i in range(low, high)]
        others(lambda f: out_copy(part, f).start())
    arrive[me] = leave[me]

    deep = 1 + has_low.astype(jnp.int32) + has_high.astype(jnp.int32)
    broad = 1 + (me > 0).astype(jnp.int32) + (me < freqs - 1).astype(jnp.int32)

    def await_tiles(way):
        for a in (2, 3):
            for b in (2, 3):

                @pl.when((deep == a) & (broad == b))
                def _():
                    await_bytes(tiles.at[pl.ds(0, a * b - 1)], tile_sems.at[way])

    await_tiles(1)
    tall_lane = lax.broadcasted_iota(jnp.int32, tile.shape, 1)
    for m in range(planes):
        total = jnp.zeros(tile.shape, f32)
        for q in range(per):
            row = m + planes * q - HALO
            down = 0 if row < 0 else (1 if row < rows else 2)
            from_row = row + rows * (1 - down)
            lead = q * pitch
            for side, width, from_col in (
                (0, HALO, tile_cols - HALO), (1, tile_cols, 0), (2, HALO, 0),
            ):
                piece = rolled(tiles[3 * down + side], lead - from_row * tile_cols - from_col)
                total = jnp.where((tall_lane >= lead) & (tall_lane < lead + width), piece, total)
                lead += width
        ocean[:, m * LANES : (m + 1) * LANES] = total

    def face_step(g, carry):
        east = 0.15 * jnp.tanh(ocean[pl.ds(route[g], 1), :])
        north = 0.15 * jnp.tanh(ocean[pl.ds(LAYERS + route[g], 1), :])
        for m in range(planes):
            here = north[:, m * LANES : (m + 1) * LANES]
            above = (
                north[:, (m + 1) * LANES : (m + 2) * LANES]
                if m + 1 < planes
                else rolled(north[:, :LANES], -pitch)
            )
            faces2[g, m : m + 1, :] = 0.5 * (here + above)
            here = east[:, m * LANES : (m + 1) * LANES]
            faces2[g, planes + m : planes + m + 1, :] = 0.5 * (here + rolled(here, -1))
        return carry

    [face_step(g, 0) for g in range(freqs)]

    for part in range(len(PARTS)):
        await_bytes(arrive.at[rest, part_rows(part)], out_sems.at[1, part])

    def source(whole):
        grown = jnp.dot(gain[...], whole.astype(jnp.bfloat16), preferred_element_type=f32)
        quartic = jnp.dot(
            quad[...], (whole * whole).astype(jnp.bfloat16), preferred_element_type=f32
        )
        return whole * (1.0 + 0.5 * jnp.tanh(grown) - 0.25 * jnp.tanh(quartic))

    total_rows = freqs * DIRP
    for m in range(planes):
        there = slice(m * LANES, (m + 1) * LANES)
        whole = arrive[:, :, there].reshape(total_rows, LANES) * sea2[m][0:1]
        first[:, :, there] = source(whole).reshape(freqs, DIRP, LANES)

    def advect_second(g, carry):
        rate = 0.5 + 0.3 * (g.astype(f32) + 0.5) / freqs
        table = wave[...] * rate
        rate_east = jnp.broadcast_to(table[:, 0:1], (DIRP, LANES))
        rate_north = jnp.broadcast_to(table[:, 1:2], (DIRP, LANES))
        state = [first[g, :, m * LANES : (m + 1) * LANES] for m in range(planes)]
        for m in range(planes):
            for axis, rate in ((0, rate_north), (planes, rate_east)):
                face = faces2[g, axis + m : axis + m + 1, :]
                for i, one in enumerate(parts_of(rate + face)):
                    coef2[3 * (axis + m) + i] = one
        for sub in range(SUB):
            fluxes = []
            for m in range(planes):
                here = 3 * m
                more = flag_north2[sub, m] * coef2[here + 2]
                above = state[m + 1] if m + 1 < planes else rolled(state[0], -pitch)
                fluxes.append(
                    (coef2[here] + more) * state[m] + (coef2[here + 1] - more) * above
                )
            cells = [
                state[m] - (fluxes[m] - (fluxes[m - 1] if m else rolled(fluxes[-1], pitch)))
                for m in range(planes)
            ]
            fluxes = []
            for m in range(planes):
                here = 3 * (planes + m)
                more = flag_east2[sub, m] * coef2[here + 2]
                fluxes.append(
                    (coef2[here] + more) * cells[m]
                    + (coef2[here + 1] - more) * rolled(cells[m], -1)
                )
            state = [
                (cells[m] - (fluxes[m] - rolled(fluxes[m], 1))) * sea2[m] for m in range(planes)
            ]
        packed[g] = pack(state, moves, tile_cols)
        return carry

    [advect_second(jnp.int32(g), 0) for g in range(freqs)]
    back[...] = source(packed[...].reshape(total_rows, LANES)).reshape(freqs, DIRP, LANES)

    def back_copy(f):
        return copy(back.at[f], final.at[me], back_sems, (), (), band, f)

    others(lambda f: back_copy(f).start())
    keep = pltpu.make_async_copy(back.at[me], final.at[me], store_sems.at[0])
    keep.start()

    stokes = jnp.dot(
        weight[...], arrive[...].reshape(total_rows, planes * LANES),
        precision=precise, preferred_element_type=f32,
    )
    level = lax.broadcasted_iota(jnp.int32, (LAYERS, LANES), 0)
    planes_of = range(planes)

    def split(x, c):
        return [
            x[c * LAYERS : (c + 1) * LAYERS, m * LANES : (m + 1) * LANES] for m in planes_of
        ]

    def spreading(field):
        outs = []
        for m in planes_of:
            here = field[m]
            above = field[m + 1] if m + 1 < planes else rolled(field[0], -pitch)
            below = field[m - 1] if m else rolled(field[-1], pitch)
            sides = rolled(here, 1) + rolled(here, -1)
            over = jnp.where(level < LAYERS - 1, pltpu.roll(here, LAYERS - 1, 0), 0.0)
            under = jnp.where(level > 0, pltpu.roll(here, 1, 0), 0.0)
            outs.append(
                viscous * (sides + above + below - 4.0 * here)
                + mixing * (over + under - 2.0 * here)
                - friction * here
            )
        return outs

    both = ocean[...]
    u, v = split(both, 0), split(both, 1)
    stokes_east, stokes_north = split(stokes, 0), split(stokes, 1)
    for _ in range(OSTEPS):
        change_u, change_v = spreading(u), spreading(v)
        u, v = (
            [
                (u[m] + ocean_dt * (change_u[m] + coriolis * (v[m] + stokes_north[m])))
                * sea2[m][0:1]
                for m in planes_of
            ],
            [
                (v[m] + ocean_dt * (change_v[m] - coriolis * (u[m] + stokes_east[m])))
                * sea2[m][0:1]
                for m in planes_of
            ],
        )
    for c, field in enumerate((u, v)):
        flat[c * LAYERS : (c + 1) * LAYERS, :] = pack(field, moves, tile_cols)
    store_ocean = pltpu.make_async_copy(flat, ocean_out, store_sems.at[1])
    store_ocean.start()

    await_bytes(route_out.at[rest], route_sems.at[0, 0])

    @pl.when(has_low)
    def _():
        await_bytes(route_out, route_sems.at[0, 1])
        halo_to_low.wait_send()

    @pl.when(has_high)
    def _():
        await_bytes(route_out, route_sems.at[0, 2])
        halo_to_high.wait_send()

    await_tiles(0)
    for part in range(len(PARTS)):
        await_bytes(leave.at[rest, part_rows(part)], out_sems.at[0, part])

    await_bytes(final.at[rest], back_sems.at[1])
    await_bytes(back.at[rest], back_sems.at[0])
    store_ocean.wait()
    keep.wait()


def finish(final, flat, result, ocean_out):
    freqs = final.shape[0]
    rows, cols = result.shape[1:]
    tile_cols = ocean_out.shape[2]
    pitch = tile_cols + 2 * HALO
    planes = (rows + 2 * HALO) * pitch // LANES
    _, spot_of = packing(rows, planes, pitch, tile_cols)
    width = min(freqs, LANES // tile_cols)
    reach = width * tile_cols
    row_at = {spot: row for row, spot in spot_of.items()}
    for c in range(2):
        turned = flat[c * LAYERS : (c + 1) * LAYERS, :].T
        for row in range(rows):
            spot = spot_of[row]
            ocean_out[c, row] = turned[spot * tile_cols : (spot + 1) * tile_cols, :]
    for chunk in range(freqs // width):
        columns = [final[chunk * width + j] for j in range(width)]
        for i, one in enumerate(swap_pieces(columns, tile_cols, width)):
            for s in range(LANES // reach):
                row = row_at[s * width + i]
                cells = pltpu.roll(one, LANES - s * reach, 1) if s else one
                cells = cells[:DIR, :reach]
                if cols > LANES:
                    result[:, row, chunk * reach : (chunk + 1) * reach] = cells
                else:
                    result.reshape(DIR * rows, cols)[pl.ds(row, DIR, stride=rows), :] = cells


def body(
    spectrum,
    velocity,
    gain_matrix,
    quad_matrix,
    limiter_flags,
    sea_mask,
    current_route,
    stokes_route,
):
    bands = lax.axis_size("band")
    freqs = lax.axis_size("freq")
    rows, cols = spectrum.shape[2:]
    tile_cols = velocity.shape[3]
    pitch = tile_cols + 2 * HALO
    planes = (rows + 2 * HALO) * pitch // LANES
    tall = rows + 2 * DEPTH
    block = max(LANES, cols)
    n = tall * cols // block
    parts = freqs * DIRP
    assert CYCLES == 2 and spectrum.shape[0] == 1 and rows % 8 == 0 and DEPTH % 8 == 0
    assert rows * tile_cols == LANES and rows >= DEPTH and tile_cols >= HALO >= OSTEPS
    assert pitch == 2 * tile_cols and LANES % pitch == 0 and freqs * tile_cols == cols
    assert (rows + 2 * HALO) % (LANES // pitch) == 0 and cols & (cols - 1) == 0
    assert block % cols == 0 and n * block == tall * cols and cols % pitch == 0
    assert bands > 1 and freqs % 4 == 0 and CYCLES * SUB == 8 and 2 * planes <= 8 and block // cols <= 2
    angles = (np.arange(DIR) + 0.5) * (2.0 * np.pi / DIR)
    waves = np.stack([np.cos(angles), np.sin(angles)])
    wave = np.zeros((DIRP, 2), np.float32)
    wave[:DIR] = waves.T
    factor = (0.5 + 1.5 * (np.arange(freqs) + 0.5) / freqs) * DIR ** (-0.5)
    trig = np.zeros((2, freqs, DIRP), np.float32)
    trig[:, :, :DIR] = waves[:, None, :] * factor[None, :, None]
    comps = freqs * DIR
    widen = np.zeros((parts, comps), np.float32)
    index = np.arange(comps)
    widen[index // DIR * DIRP + index % DIR, index] = 1.0
    f32, bf16 = jnp.float32, jnp.bfloat16
    anywhere = pl.BlockSpec(memory_space=pl.ANY)
    dma = pltpu.SemaphoreType.DMA
    vmem = pltpu.VMEM
    tile_cells = rows * tile_cols
    layers = 2 * LAYERS
    final, flat = pl.pallas_call(
        functools.partial(kernel, bands, freqs, cols),
        out_shape=(
            jax.ShapeDtypeStruct((freqs, DIRP, LANES), f32),
            jax.ShapeDtypeStruct((layers, LANES), f32),
        ),
        in_specs=[anywhere] * 11,
        out_specs=(anywhere, anywhere),
        scratch_shapes=[
            pltpu.SMEM((freqs,), jnp.int32),
            pltpu.SMEM(stokes_route.shape[::-1], jnp.int32),
            vmem((DIRP, rows, cols), f32),
            vmem((DIRP, DEPTH, cols), f32),
            vmem((DIRP, DEPTH, cols), f32),
            vmem((2, rows, tile_cols, LAYERS), f32),
            vmem((comps, comps), bf16),
            vmem((comps, comps), bf16),
            vmem((parts, comps), bf16),
            vmem((DIRP, 2), f32),
            vmem((2, parts), f32),
            vmem((parts, parts), bf16),
            vmem((parts, parts), bf16),
            vmem(limiter_flags.shape, jnp.int32),
            vmem(sea_mask.shape, jnp.int32),
            vmem((n, 8, block), f32),
            vmem((8 * n, block), f32),
            vmem((SUB, 8 * n, block), f32),
            vmem((SUB, 8 * n, block), f32),
            vmem((SUB, planes, DIRP, LANES), f32),
            vmem((SUB, planes, DIRP, LANES), f32),
            vmem((planes, DIRP, LANES), f32),
            vmem((layers, tile_cells), f32),
            vmem((layers, tile_cells), f32),
            vmem((9, layers, tile_cells), f32),
            vmem((freqs, 2, tile_cells), f32),
            vmem((freqs, 2, tile_cells), f32),
            vmem((freqs, 2, tile_cells), f32),
            vmem((freqs, 2, tile_cells), f32),
            vmem((2, n, block), f32),
            vmem((3, 8 * n, block), f32),
            vmem((freqs, 8, LANES), f32),
            vmem((7, 8 * n, block), f32),
            vmem((6 * planes, DIRP, LANES), f32),
            vmem((freqs, DIRP, planes * LANES), f32),
            vmem((freqs, DIRP, planes * LANES), f32),
            vmem((freqs, DIRP, planes * LANES), f32),
            vmem((freqs, DIRP, LANES), f32),
            vmem((freqs, DIRP, LANES), f32),
            vmem((layers, planes * LANES), f32),
            vmem((layers, parts), f32),
            vmem((layers, LANES), f32),
            dma((11,)),
            dma((2, 2)),
            dma((2, 3)),
            dma((2,)),
            dma((2, len(PARTS))),
            dma((2,)),
            dma((2,)),
        ],
        compiler_params=pltpu.CompilerParams(
            collective_id=0, has_side_effects=True, vmem_limit_bytes=60 * 1024 * 1024
        ),
    )(
        current_route,
        stokes_route.T,
        spectrum.reshape(DIR, rows, cols),
        velocity.transpose(0, 2, 3, 1),
        gain_matrix,
        quad_matrix,
        limiter_flags,
        sea_mask,
        jnp.asarray(widen, bf16),
        jnp.asarray(wave),
        jnp.asarray(trig.reshape(2, parts)),
    )
    whole = pl.BlockSpec(memory_space=vmem)
    result, ocean = pl.pallas_call(
        finish,
        out_shape=(
            jax.ShapeDtypeStruct((DIR, rows, cols), f32),
            jax.ShapeDtypeStruct((2, rows, tile_cols, LAYERS), f32),
        ),
        in_specs=[whole] * 2,
        out_specs=(whole, whole),
    )(final, flat)
    return (result.reshape(1, DIR, rows, cols), ocean.transpose(0, 3, 1, 2))


def solution(mesh):
    return jax.shard_map(
        body,
        mesh=mesh,
        in_specs=(
            P("freq", None, "band", None),
            P(None, None, "band", "freq"),
            P(),
            P(),
            P(),
            P(),
            P(),
            P(),
        ),
        out_specs=(P("freq", None, "band", None), P(None, None, "band", "freq")),
        check_vma=False,
    )
```

```python
import functools

import jax
import jax.numpy as jnp
import numpy as np
from jax import lax
from jax.experimental import pallas as pl
from jax.experimental.pallas import tpu as pltpu
from jax.sharding import PartitionSpec as P

DIR = 36
LAYERS = 24
SUB = 4
CYCLES = 2
OSTEPS = 3


precise = lax.Precision.HIGHEST
ocean_dt = 0.2
viscous = 0.5
coriolis = 1.0
mixing = 0.5
friction = 0.1


GROUP = 8
LANES = 128
DIRP = -(-DIR // GROUP) * GROUP
GROUPS = DIRP // GROUP
HALO = SUB
DEPTH = CYCLES * SUB
PARTS = ((0, 1), (1, 3))
REST = 3
QUAD = 4
QUADS = (DIR - REST * GROUP) // QUAD
MESH = pl.DeviceIdType.MESH


def swap_pieces(blocks, piece, width):
    lane = lax.broadcasted_iota(jnp.int32, blocks[0].shape, 1)
    out = list(blocks)
    far = width // 2
    while far:
        low = (lane & (far * piece)) == 0
        for a in range(width):
            if a & far:
                continue
            b = a + far
            x, y = out[a], out[b]
            out[a] = jnp.where(low, x, pltpu.roll(y, far * piece, 1))
            out[b] = jnp.where(low, pltpu.roll(x, LANES - far * piece, 1), y)
        far //= 2
    return out


def packing(rows, planes, pitch, tile_cols):
    places = LANES // tile_cols
    free = set(range(places))
    left = {
        m: [q for q in range(LANES // pitch) if 0 <= m + planes * q - HALO < rows]
        for m in range(planes)
    }
    moves, where = [], {}
    while any(left.values()):
        best = None
        for m in range(planes):
            for by in range(places):
                fits = [
                    q for q in left[m] if (q * pitch // tile_cols + by) % places in free
                ]
                if best is None or len(fits) > len(best[2]):
                    best = (m, by, fits)
        m, by, fits = best
        spots = [(q * pitch // tile_cols + by) % places for q in fits]
        moves.append((m, (by * tile_cols - HALO) % LANES, spots))
        for q, spot in zip(fits, spots):
            where[m + planes * q - HALO] = spot
            free.remove(spot)
            left[m].remove(q)
    return moves, where


def pack(blocks, moves, tile_cols):
    lane = lax.broadcasted_iota(jnp.int32, blocks[0].shape, 1)
    total = None
    for m, shift, spots in moves:
        piece = pltpu.roll(blocks[m], shift, 1) if shift else blocks[m]
        if total is None:
            total = piece
            continue
        hit = None
        for spot in spots:
            one = (lane >= spot * tile_cols) & (lane < (spot + 1) * tile_cols)
            hit = one if hit is None else hit | one
        total = jnp.where(hit, piece, total)
    return total


def parts_of(courant):
    up, down = jnp.maximum(courant, 0.0), jnp.minimum(courant, 0.0)
    return up, down, 0.5 * (courant * courant - (up - down))


def kernel(
    bands,
    freqs,
    cols,
    route_in,
    stokes_in,
    spectrum,
    velocity,
    gain_in,
    quad_in,
    flags_in,
    sea_in,
    widen_in,
    wave_in,
    trig_in,
    final,
    ocean_out,
    route,
    stokes_route,
    spec,
    halo_low,
    halo_high,
    vel,
    gain_raw,
    quad_raw,
    widen,
    wave,
    trig,
    gain,
    quad,
    flag_raw,
    sea_raw,
    flag_blk,
    sea_blk,
    flag_north,
    flag_east,
    flag_north2,
    flag_east2,
    sea2,
    tile,
    ready,
    tiles,
    route_out,
    route_own,
    route_low,
    route_high,
    drift,
    faces,
    faces2,
    coef,
    coef2,
    start,
    leave,
    leave_end,
    leave_last,
    arrive,
    arrive_end,
    arrive_last,
    clean,
    first,
    packed,
    back,
    ocean,
    weight,
    flat,
    load_sems,
    halo_sems,
    route_sems,
    tile_sems,
    out_sems,
    back_sems,
    store_sems,
):
    band = lax.axis_index("band")
    me = lax.axis_index("freq")
    f32 = jnp.float32
    rows = spectrum.shape[1]
    tile_cols = velocity.shape[2]
    tall = rows + 2 * DEPTH
    block = max(LANES, cols)
    slots = block // cols
    n = tall // slots
    pitch = tile_cols + 2 * HALO
    per = LANES // pitch
    planes = (rows + 2 * HALO) // per
    seam = LANES - pitch
    moves, spot_of = packing(rows, planes, pitch, tile_cols)
    has_low = band > 0
    has_high = band < bands - 1

    mid = freqs // 2
    side, place = me // mid, lax.rem(me, mid)
    near = [side * mid + lax.rem(place + i, mid) for i in [*range(2, mid), 1][: mid - 1]]
    far = [(1 - side) * mid + lax.rem(2 * mid - 1 - place - i, mid) for i in range(mid)]
    partners = []
    for i in range(mid):
        partners += near[i : i + 1] + [far[i]]

    def others(fn):
        for f in partners:
            fn(f)

    def every(fn):
        for f in range(freqs):
            fn(f)

    def copy(src, dst, sems, slot_send, slot_recv, to_band, to_freq):
        return pltpu.make_async_remote_copy(
            src_ref=src,
            dst_ref=dst,
            send_sem=sems.at[(0,) + slot_send],
            recv_sem=sems.at[(1,) + slot_recv],
            device_id=(to_band, to_freq),
            device_id_type=MESH,
        )

    def rolled(x, shift):
        shift %= x.shape[1]
        return pltpu.roll(x, shift, 1) if shift else x

    def locate(at):
        return (at, 0) if at < n else (tall - 1 - at, 1)

    def row_at(k, s):
        return tall - 1 - k if s else k

    def strided(ref, size, base, at):
        depth = ref.shape[1]
        if cols > LANES:
            return ref[pl.ds(base, size), at, :]
        return ref.reshape(ref.shape[0] * depth, cols)[
            pl.ds(base * depth + at, size, stride=depth), :
        ]

    def await_bytes(ref, sem):
        pltpu.make_async_copy(ref, ref, sem).wait()

    rest = pl.ds(0, freqs - 1)

    barrier = pltpu.get_barrier_semaphore()

    def greet(to_band, to_freq):
        pl.semaphore_signal(barrier, inc=1, device_id=(to_band, to_freq), device_id_type=MESH)

    others(lambda f: greet(band, f))

    @pl.when(has_low)
    def _():
        every(lambda f: greet(band - 1, f))

    @pl.when(has_high)
    def _():
        every(lambda f: greet(band + 1, f))

    load_vel = pltpu.make_async_copy(velocity, vel, load_sems.at[0])
    load_vel.start()
    load_route = pltpu.make_async_copy(route_in, route, load_sems.at[9])
    load_route.start()
    load_stokes = pltpu.make_async_copy(stokes_in, stokes_route, load_sems.at[10])
    load_stokes.start()
    load_spec = pltpu.make_async_copy(spectrum, spec.at[pl.ds(0, DIR)], load_sems.at[1])
    load_grid = [
        pltpu.make_async_copy(src, dst, load_sems.at[2 + i])
        for i, (src, dst) in enumerate(((flags_in, flag_raw), (sea_in, sea_raw)))
    ]
    loads = [
        pltpu.make_async_copy(src, dst, load_sems.at[4 + i])
        for i, (src, dst) in enumerate(
            (
                (wave_in, wave),
                (gain_in, gain_raw),
                (quad_in, quad_raw),
                (widen_in, widen),
                (trig_in, trig),
            )
        )
    ]
    for one in load_grid:
        one.start()
    load_spec.start()
    for one in loads:
        one.start()

    load_vel.wait()
    for c in range(2):
        field = vel[c].reshape(rows * tile_cols, LAYERS)
        tile[c * LAYERS : (c + 1) * LAYERS, :] = field.T

    ready[...] = pltpu.roll(
        0.15 * jnp.tanh(tile[...]), lax.rem(me * tile_cols, LANES), 1
    )

    def prepare(f):
        route_out[f, 0:1, :] = ready[pl.ds(route[f], 1), :]
        route_out[f, 1:2, :] = ready[pl.ds(LAYERS + route[f], 1), :]

    load_route.wait()
    every(prepare)
    count = freqs - 1 + freqs * (has_low.astype(jnp.int32) + has_high.astype(jnp.int32))
    pl.semaphore_wait(barrier, count)

    halo_to_low = copy(
        spectrum.at[:, pl.ds(0, DEPTH)], halo_high.at[pl.ds(0, DIR)], halo_sems,
        (0,), (0,), band - 1, me,
    )
    halo_to_high = copy(
        spectrum.at[:, pl.ds(rows - DEPTH, DEPTH)], halo_low.at[pl.ds(0, DIR)], halo_sems,
        (1,), (1,), band + 1, me,
    )

    def route_copy(f):
        return copy(route_out.at[f], route_own.at[me], route_sems, (0,), (0,), band, f)

    def route_to_low(f):
        return copy(
            route_out.at[f], route_high.at[me], route_sems, (1,), (1,), band - 1, f
        )

    def route_to_high(f):
        return copy(
            route_out.at[f], route_low.at[me], route_sems, (2,), (2,), band + 1, f
        )

    others(lambda f: route_copy(f).start())

    @pl.when(has_low)
    def _():
        every(lambda f: route_to_low(f).start())
        halo_to_low.start()

    @pl.when(has_high)
    def _():
        every(lambda f: route_to_high(f).start())
        halo_to_high.start()

    def near_tiles(fn):
        for down in (-1, 0, 1):
            for side in (-1, 0, 1):
                if down == 0 and side == 0:
                    continue
                to_band, to_freq = band + down, me + side
                there = (to_band >= 0) & (to_band < bands) & (to_freq >= 0) & (to_freq < freqs)
                mine = 3 * (1 + down) + 1 + side
                fn(there, mine, 8 - mine, to_band, to_freq)

    def tile_copy(mine, theirs, to_band, to_freq):
        return copy(tile, tiles.at[theirs], tile_sems, (), (), to_band, to_freq)

    def tile_start(there, mine, theirs, to_band, to_freq):
        @pl.when(there)
        def _():
            tile_copy(mine, theirs, to_band, to_freq).start()

        @pl.when(jnp.logical_not(there))
        def _():
            tiles[mine] = jnp.zeros_like(tile)

    near_tiles(tile_start)
    tiles[4] = tile[...]
    route_own[me] = route_out[me]

    pads = ((DIR, DIRP - DIR),)
    for at, size in pads:
        spec[at : at + size] = jnp.zeros((size, rows, cols), f32)
        halo_low[at : at + size] = jnp.zeros((size, DEPTH, cols), f32)
        halo_high[at : at + size] = jnp.zeros((size, DEPTH, cols), f32)

    @pl.when(jnp.logical_not(has_low))
    def _():
        halo_low[...] = jnp.zeros_like(halo_low)
        route_low[...] = jnp.zeros_like(route_low)

    @pl.when(jnp.logical_not(has_high))
    def _():
        halo_high[...] = jnp.zeros_like(halo_high)
        route_high[...] = jnp.zeros_like(route_high)

    for one in load_grid:
        one.wait()

    steps = CYCLES * SUB
    all_rows = sea_raw.shape[0]
    wide = (8, block)

    def grid_row(at):
        whole = jnp.clip(band * rows - DEPTH + at, 0, all_rows - 1)
        there = has_low if at < DEPTH else (None if at < DEPTH + rows else has_high)
        flag = strided(flag_raw, steps, 0, whole)
        sea = sea_raw[pl.ds(whole, 1), :].astype(f32)
        flag = flag.astype(f32)
        if there is not None:
            there = there.astype(f32)
            flag, sea = flag * there, sea * there
        return flag, sea

    for k in range(n):
        pieces = [grid_row(row_at(k, s)) for s in range(slots)]
        flag_blk[k] = jnp.concatenate([flag for flag, _ in pieces], axis=1)
        sea = jnp.concatenate([sea for _, sea in pieces], axis=1)
        sea_blk[8 * k : 8 * (k + 1), :] = jnp.broadcast_to(sea, wide)

    first_slot = lax.broadcasted_iota(jnp.int32, wide, 1) < cols
    for k in range(n):
        here = flag_blk[k]
        above = flag_blk[k + 1] if k + 1 < n else rolled(here, cols)
        if slots > 1:
            above = jnp.where(first_slot, above, here)
        beside = rolled(here, -1)
        for sub in range(SUB):
            there = slice(8 * k, 8 * (k + 1))
            flag_north[sub, there, :] = jnp.broadcast_to(above[sub : sub + 1], wide)
            flag_east[sub, there, :] = jnp.broadcast_to(beside[sub : sub + 1], wide)

    lane = lax.broadcasted_iota(jnp.int32, (8, LANES), 1)
    column = me * tile_cols - HALO + (lane & (pitch - 1))
    inside = (column >= 0) & (column < cols)
    window_flags, window_sea = [], []
    for m in range(planes):
        total_flags, total_sea = jnp.zeros((8, LANES), f32), jnp.zeros((8, LANES), f32)
        for q in range(per):
            k, s = locate(m + planes * q + DEPTH - HALO)
            shift = lax.rem(q * pitch - cols * s - tile_cols * me + HALO + 2 * block, block)
            hit = (lane >= q * pitch) & (lane < (q + 1) * pitch) & inside
            total_flags = jnp.where(
                hit, pltpu.roll(flag_blk[k], shift, 1)[:, :LANES], total_flags
            )
            total_sea = jnp.where(hit, pltpu.roll(sea_blk[8 * k : 8 * (k + 1), :], shift, 1)[:, :LANES], total_sea)
        window_flags.append(total_flags)
        window_sea.append(total_sea)
    for m in range(planes):
        sea2[m] = jnp.concatenate([window_sea[m]] * GROUPS, axis=0)
        above = window_flags[m + 1] if m + 1 < planes else rolled(window_flags[0], -pitch)
        beside = rolled(window_flags[m], -1)
        for sub in range(SUB):
            step = SUB + sub
            flag_north2[sub, m] = jnp.broadcast_to(above[step : step + 1], (DIRP, LANES))
            flag_east2[sub, m] = jnp.broadcast_to(beside[step : step + 1], (DIRP, LANES))

    load_spec.wait()
    load_stokes.wait()
    for one in loads:
        one.wait()

    for raw, padded in ((gain_raw, gain), (quad_raw, quad)):
        half = jnp.dot(widen[...], raw[...], preferred_element_type=f32).astype(jnp.bfloat16)
        padded[...] = lax.dot_general(
            half, widen[...], (((1,), (1,)), ((), ())), preferred_element_type=f32
        ).astype(jnp.bfloat16)

    layer = lax.broadcasted_iota(jnp.int32, (LAYERS, 1), 0)
    component = lax.broadcasted_iota(jnp.int32, (LAYERS, freqs * DIRP), 1)
    deposits = jnp.zeros((LAYERS, freqs * DIRP), f32)
    for g in range(freqs):
        deposit = jnp.zeros((LAYERS, 1), f32)
        for j in range(stokes_route.shape[0]):
            hit = (layer == stokes_route[j, g]).astype(f32)
            deposit = deposit + hit * (1.0 / (1.0 + j))
        own = (component >= g * DIRP) & (component < (g + 1) * DIRP)
        deposits = jnp.where(own, deposit, deposits)
    for c in range(2):
        weight[c * LAYERS : (c + 1) * LAYERS, :] = deposits * trig[c : c + 1, :]

    @pl.when(has_low)
    def _():
        halo_to_high.wait_recv()

    @pl.when(has_high)
    def _():
        halo_to_low.wait_recv()

    number = me.astype(f32) + 0.5
    my_rate = 0.5 + 0.3 * number / freqs

    def row_of(base, at):
        if at < DEPTH:
            return strided(halo_low, GROUP, base, at)
        if at < DEPTH + rows:
            return strided(spec, GROUP, base, at - DEPTH)
        return strided(halo_high, GROUP, base, at - DEPTH - rows)

    starts = [
        jnp.concatenate([row_of(group * GROUP, row_at(k, s)) for s in range(slots)], axis=1)
        for group in range(GROUPS)
        for k in range(n)
    ]
    for i, one in enumerate(starts):
        start[i // n, 8 * (i % n) : 8 * (i % n + 1), :] = one

    await_bytes(route_own.at[rest], route_sems.at[1, 0])

    @pl.when(has_low)
    def _():
        await_bytes(route_low, route_sems.at[1, 2])

    @pl.when(has_high)
    def _():
        await_bytes(route_high, route_sems.at[1, 1])

    stacks = [
        jnp.concatenate(
            [route_low[j], route_own[j], route_high[j], jnp.zeros((2, LANES), f32)], axis=0
        )
        for j in range(freqs)
    ]
    reach = min(cols, LANES) // tile_cols
    places = LANES // tile_cols
    spot_masks = [
        (lane >= spot * tile_cols) & (lane < (spot + 1) * tile_cols) for spot in range(places)
    ]
    for row in range(rows):
        halves = []
        for half in range(block // LANES):
            total = stacks[half * reach]
            for j in range(1, reach):
                total = jnp.where(
                    spot_masks[(row + j) % places], stacks[half * reach + j], total
                )
            halves.append(total)
        moved = []
        for s in range(slots):
            turned = [rolled(x, cols * s - row * tile_cols) for x in halves]
            moved.append(turned[0] if len(turned) == 1 else jnp.concatenate(turned, axis=1))
        for source in range(3):
            at = row + DEPTH + rows * (source - 1)
            if at < 0 or at >= tall:
                continue
            k, s = locate(at)
            for c in range(2):
                line = 2 * source + c
                drift[c, k : k + 1, cols * s : cols * (s + 1)] = moved[s][
                    line : line + 1, cols * s : cols * (s + 1)
                ]
    blane = lax.broadcasted_iota(jnp.int32, (1, block), 1)
    last = ((blane & (cols - 1)) == cols - 1).astype(f32)
    inner = 1.0 - last
    east, north = drift[0], drift[1]
    above = jnp.concatenate([north[1:], rolled(north[n - 1 :], cols)], axis=0)
    sign = jnp.where(blane < cols, 1.0, -1.0)
    for i, face in enumerate(
        (sign * (0.5 * (north + above)), 0.5 * (inner * east + rolled(east, -1)), 0.5 * east)
    ):
        for k in range(n):
            faces[i, 8 * k : 8 * (k + 1), :] = jnp.broadcast_to(face[k : k + 1], wide)

    def advect_first(group):
        table = wave[group * GROUP : (group + 1) * GROUP, :]

        def rate_of(i):
            rate = jnp.broadcast_to(table[:, i : i + 1] * my_rate, wide)
            return jnp.concatenate([rate] * n, axis=0)

        rate_east = rate_of(0)
        for axis, rate in ((0, rate_of(1)), (1, rate_east)):
            if axis == 0 and slots > 1:
                rate = rate * sign
            for i, one in enumerate(parts_of(rate + faces[axis])):
                coef[group, 3 * axis + i] = one
        coef[group, 6] = 1.0 - last * jnp.maximum(rate_east + faces[2], 0.0)
        state = start[group]
        for sub in range(SUB):
            here, new = slice(8 * sub, 8 * n), slice(8 * (sub + 1), 8 * n)
            beyond = rolled(state[-8:], cols)
            more = flag_north[sub, here] * coef[group, 2, here]
            flux = (coef[group, 0, here] + more) * state + (
                coef[group, 1, here] - more
            ) * jnp.concatenate([state[8:], beyond], axis=0)
            state = state[8:] - (flux[8:] - flux[:-8])
            more = flag_east[sub, new] * coef[group, 5, new]
            flux = (coef[group, 3, new] + more) * (inner * state) + (
                coef[group, 4, new] - more
            ) * rolled(state, -1)
            state = (
                coef[group, 6, new] * state - (inner * flux - rolled(flux, 1))
            ) * sea_blk[new, :]
        width = min(cols, LANES) // pitch
        low_half = lax.broadcasted_iota(jnp.int32, (8 * planes, LANES), 1) < width * pitch
        for odd in range(2):
            turned = rolled(state, HALO - odd * tile_cols)
            for half in range(block // LANES):
                sources = []
                for i in range(width):
                    pieces = []
                    for s in range(slots):
                        lines = []
                        for m in range(planes):
                            k, slot = locate(m + planes * (i + width * s) + DEPTH - HALO)
                            assert slot == s and k >= SUB
                            k -= SUB
                            lines.append(
                                turned[8 * k : 8 * (k + 1), half * LANES : (half + 1) * LANES]
                            )
                        pieces.append(jnp.concatenate(lines, axis=0))
                    sources.append(pieces[0] if slots == 1 else jnp.where(low_half, *pieces))
                for e, one in enumerate(swap_pieces(sources, pitch, width)):
                    to = 2 * (e + width * half) + odd
                    for m in range(planes):
                        cells = one[8 * m : 8 * (m + 1)]
                        at = slice(m * LANES, (m + 1) * LANES)
                        if group < REST:
                            leave[to, group * GROUP : (group + 1) * GROUP, at] = cells
                            continue
                        end, at = (leave_last, slice(0, LANES)) if m == planes - 1 else (leave_end, at)
                        first_quad = (group - REST) * GROUP // QUAD
                        for i in range(min(GROUP // QUAD, QUADS - first_quad)):
                            end[to, first_quad + i, :, at] = cells[i * QUAD : (i + 1) * QUAD]

    def part_rows(part):
        low, high = PARTS[part]
        return pl.ds(low * GROUP, (high - low) * GROUP)

    def out_copy(part, f):
        there = part_rows(part)
        return copy(
            leave.at[f, there], arrive.at[me, there], out_sems, (part,), (part,), band, f
        )

    ends = ((leave_end, arrive_end, len(PARTS)), (leave_last, arrive_last, len(PARTS) + 1))

    def end_copy(leaving, arriving, part, f):
        return copy(leaving.at[f], arriving.at[me], out_sems, (part,), (part,), band, f)

    def received():
        for part in range(len(PARTS)):
            yield arrive.at[rest, part_rows(part)], part
        for _, arriving, part in ends:
            yield arriving.at[rest], part

    for part, (low, high) in enumerate(PARTS):
        for group in range(low, high):
            advect_first(group)
        others(lambda f: out_copy(part, f).start())
    for group in range(REST, GROUPS):
        advect_first(group)
    for leaving, arriving, part in ends:
        others(lambda f: end_copy(leaving, arriving, part, f).start())
    arrive[me] = leave[me]
    arrive_end[me] = leave_end[me]
    arrive_last[me] = leave_last[me]

    deep = 1 + has_low.astype(jnp.int32) + has_high.astype(jnp.int32)
    broad = 1 + (me > 0).astype(jnp.int32) + (me < freqs - 1).astype(jnp.int32)

    def await_tiles(way):
        for a in (2, 3):
            for b in (2, 3):

                @pl.when((deep == a) & (broad == b))
                def _():
                    await_bytes(tiles.at[pl.ds(0, a * b - 1)], tile_sems.at[way])

    await_tiles(1)
    tall_lane = lax.broadcasted_iota(jnp.int32, tile.shape, 1)
    for m in range(planes):
        total = jnp.zeros(tile.shape, f32)
        for q in range(per):
            row = m + planes * q - HALO
            down = 0 if row < 0 else (1 if row < rows else 2)
            from_row = row + rows * (1 - down)
            lead = q * pitch
            for side, width, from_col in (
                (0, HALO, tile_cols - HALO), (1, tile_cols, 0), (2, HALO, 0),
            ):
                piece = rolled(tiles[3 * down + side], lead - from_row * tile_cols - from_col)
                total = jnp.where((tall_lane >= lead) & (tall_lane < lead + width), piece, total)
                lead += width
        ocean[:, m * LANES : (m + 1) * LANES] = total

    def face_step(g, carry):
        east = 0.15 * jnp.tanh(ocean[pl.ds(route[g], 1), :])
        north = 0.15 * jnp.tanh(ocean[pl.ds(LAYERS + route[g], 1), :])
        for m in range(planes):
            here = north[:, m * LANES : (m + 1) * LANES]
            above = (
                north[:, (m + 1) * LANES : (m + 2) * LANES]
                if m + 1 < planes
                else rolled(north[:, :LANES], -pitch)
            )
            faces2[g, m : m + 1, :] = 0.5 * (here + above)
            here = east[:, m * LANES : (m + 1) * LANES]
            faces2[g, planes + m : planes + m + 1, :] = 0.5 * (here + rolled(here, -1))
        return carry

    [face_step(g, 0) for g in range(freqs)]

    def source(whole):
        grown = jnp.dot(gain[...], whole.astype(jnp.bfloat16), preferred_element_type=f32)
        quartic = jnp.dot(
            quad[...], (whole * whole).astype(jnp.bfloat16), preferred_element_type=f32
        )
        return whole * (1.0 + 0.5 * jnp.tanh(grown) - 0.25 * jnp.tanh(quartic))

    total_rows = freqs * DIRP
    incoming = list(received())
    for ref, part in incoming[:-1]:
        await_bytes(ref, out_sems.at[1, part])
    pad = jnp.zeros((DIRP - DIR, LANES), f32)
    for m in range(planes):
        there = slice(m * LANES, (m + 1) * LANES)
        end, at = (arrive_end, there)
        if m == planes - 1:
            await_bytes(incoming[-1][0], out_sems.at[1, incoming[-1][1]])
            end, at = (arrive_last, slice(0, LANES))
        pieces = []
        for f in range(freqs):
            pieces.append(arrive[f, :, there])
            pieces += [end[f, i, :, at] for i in range(QUADS)]
            pieces.append(pad)
        whole = jnp.concatenate(pieces, axis=0) * sea2[m][0:1]
        clean[:, there] = whole
        first[:, :, there] = source(whole).reshape(freqs, DIRP, LANES)

    def advect_second(g):
        rate = 0.5 + 0.3 * (g + 0.5) / freqs
        table = wave[...] * rate
        rate_east = jnp.broadcast_to(table[:, 0:1], (DIRP, LANES))
        rate_north = jnp.broadcast_to(table[:, 1:2], (DIRP, LANES))
        state = [first[g, :, m * LANES : (m + 1) * LANES] for m in range(planes)]
        for m in range(planes):
            for axis, rate in ((0, rate_north), (planes, rate_east)):
                face = faces2[g, axis + m : axis + m + 1, :]
                for i, one in enumerate(parts_of(rate + face)):
                    coef2[g, 3 * (axis + m) + i] = one
        for sub in range(SUB):
            fluxes = []
            for m in range(planes):
                here = 3 * m
                more = flag_north2[sub, m] * coef2[g, here + 2]
                above = state[m + 1] if m + 1 < planes else rolled(state[0], -pitch)
                fluxes.append(
                    (coef2[g, here] + more) * state[m] + (coef2[g, here + 1] - more) * above
                )
            cells = [
                state[m] - (fluxes[m] - (fluxes[m - 1] if m else rolled(fluxes[-1], pitch)))
                for m in range(planes)
            ]
            fluxes = []
            for m in range(planes):
                here = 3 * (planes + m)
                more = flag_east2[sub, m] * coef2[g, here + 2]
                fluxes.append(
                    (coef2[g, here] + more) * cells[m]
                    + (coef2[g, here + 1] - more) * rolled(cells[m], -1)
                )
            state = [
                (cells[m] - (fluxes[m] - rolled(fluxes[m], 1))) * sea2[m] for m in range(planes)
            ]
        packed[g] = pack(state, moves, tile_cols)

    for g in range(freqs):
        advect_second(g)
    back[...] = source(packed[...].reshape(total_rows, LANES)).reshape(freqs, DIRP, LANES)

    def back_copy(f):
        return copy(back.at[f], final.at[me], back_sems, (), (), band, f)

    others(lambda f: back_copy(f).start())
    keep = pltpu.make_async_copy(back.at[me], final.at[me], store_sems.at[0])
    keep.start()

    stokes = jnp.dot(
        weight[...], clean[...],
        precision=precise, preferred_element_type=f32,
    )
    level = lax.broadcasted_iota(jnp.int32, (LAYERS, LANES), 0)
    planes_of = range(planes)

    def split(x, c):
        return [
            x[c * LAYERS : (c + 1) * LAYERS, m * LANES : (m + 1) * LANES] for m in planes_of
        ]

    def spreading(field):
        outs = []
        for m in planes_of:
            here = field[m]
            above = field[m + 1] if m + 1 < planes else rolled(field[0], -pitch)
            below = field[m - 1] if m else rolled(field[-1], pitch)
            sides = rolled(here, 1) + rolled(here, -1)
            over = jnp.where(level < LAYERS - 1, pltpu.roll(here, LAYERS - 1, 0), 0.0)
            under = jnp.where(level > 0, pltpu.roll(here, 1, 0), 0.0)
            outs.append(
                viscous * (sides + above + below - 4.0 * here)
                + mixing * (over + under - 2.0 * here)
                - friction * here
            )
        return outs

    both = ocean[...]
    u, v = split(both, 0), split(both, 1)
    stokes_east, stokes_north = split(stokes, 0), split(stokes, 1)
    for _ in range(OSTEPS):
        change_u, change_v = spreading(u), spreading(v)
        u, v = (
            [
                (u[m] + ocean_dt * (change_u[m] + coriolis * (v[m] + stokes_north[m])))
                * sea2[m][0:1]
                for m in planes_of
            ],
            [
                (v[m] + ocean_dt * (change_v[m] - coriolis * (u[m] + stokes_east[m])))
                * sea2[m][0:1]
                for m in planes_of
            ],
        )
    for c, field in enumerate((u, v)):
        flat[c * LAYERS : (c + 1) * LAYERS, :] = pack(field, moves, tile_cols)
    store_ocean = pltpu.make_async_copy(flat, ocean_out, store_sems.at[1])
    store_ocean.start()

    await_bytes(route_out.at[rest], route_sems.at[0, 0])

    @pl.when(has_low)
    def _():
        await_bytes(route_out, route_sems.at[0, 1])
        halo_to_low.wait_send()

    @pl.when(has_high)
    def _():
        await_bytes(route_out, route_sems.at[0, 2])
        halo_to_high.wait_send()

    await_tiles(0)
    for part in range(len(PARTS)):
        await_bytes(leave.at[rest, part_rows(part)], out_sems.at[0, part])
    for leaving, _, part in ends:
        await_bytes(leaving.at[rest], out_sems.at[0, part])

    await_bytes(final.at[rest], back_sems.at[1])
    await_bytes(back.at[rest], back_sems.at[0])
    store_ocean.wait()
    keep.wait()


def finish(final, flat, result, ocean_out):
    freqs = final.shape[0]
    rows, cols = result.shape[1:]
    tile_cols = ocean_out.shape[2]
    pitch = tile_cols + 2 * HALO
    planes = (rows + 2 * HALO) * pitch // LANES
    _, spot_of = packing(rows, planes, pitch, tile_cols)
    width = min(freqs, LANES // tile_cols)
    reach = width * tile_cols
    row_at = {spot: row for row, spot in spot_of.items()}
    for c in range(2):
        turned = flat[c * LAYERS : (c + 1) * LAYERS, :].T
        for row in range(rows):
            spot = spot_of[row]
            ocean_out[c, row] = turned[spot * tile_cols : (spot + 1) * tile_cols, :]
    for chunk in range(freqs // width):
        columns = [final[chunk * width + j] for j in range(width)]
        for i, one in enumerate(swap_pieces(columns, tile_cols, width)):
            for s in range(LANES // reach):
                row = row_at[s * width + i]
                cells = pltpu.roll(one, LANES - s * reach, 1) if s else one
                cells = cells[:DIR, :reach]
                if cols > LANES:
                    result[:, row, chunk * reach : (chunk + 1) * reach] = cells
                else:
                    result.reshape(DIR * rows, cols)[pl.ds(row, DIR, stride=rows), :] = cells


def body(
    spectrum,
    velocity,
    gain_matrix,
    quad_matrix,
    limiter_flags,
    sea_mask,
    current_route,
    stokes_route,
):
    bands = lax.axis_size("band")
    freqs = lax.axis_size("freq")
    rows, cols = spectrum.shape[2:]
    tile_cols = velocity.shape[3]
    pitch = tile_cols + 2 * HALO
    planes = (rows + 2 * HALO) * pitch // LANES
    tall = rows + 2 * DEPTH
    block = max(LANES, cols)
    n = tall * cols // block
    parts = freqs * DIRP
    assert CYCLES == 2 and spectrum.shape[0] == 1 and rows % 8 == 0 and DEPTH % 8 == 0
    assert rows * tile_cols == LANES and rows >= DEPTH and tile_cols >= HALO >= OSTEPS
    assert pitch == 2 * tile_cols and LANES % pitch == 0 and freqs * tile_cols == cols
    assert (rows + 2 * HALO) % (LANES // pitch) == 0 and cols & (cols - 1) == 0
    assert block % cols == 0 and rows % 2 == 0 and n * block == tall * cols and cols % pitch == 0
    assert bands > 1 and freqs % 4 == 0 and CYCLES * SUB == 8 and 2 * planes <= 8 and block // cols <= 2
    angles = (np.arange(DIR) + 0.5) * (2.0 * np.pi / DIR)
    waves = np.stack([np.cos(angles), np.sin(angles)])
    wave = np.zeros((DIRP, 2), np.float32)
    wave[:DIR] = waves.T
    factor = (0.5 + 1.5 * (np.arange(freqs) + 0.5) / freqs) * DIR ** (-0.5)
    trig = np.zeros((2, freqs, DIRP), np.float32)
    trig[:, :, :DIR] = waves[:, None, :] * factor[None, :, None]
    comps = freqs * DIR
    widen = np.zeros((parts, comps), np.float32)
    index = np.arange(comps)
    widen[index // DIR * DIRP + index % DIR, index] = 1.0
    f32, bf16 = jnp.float32, jnp.bfloat16
    anywhere = pl.BlockSpec(memory_space=pl.ANY)
    dma = pltpu.SemaphoreType.DMA
    vmem = pltpu.VMEM
    tile_cells = rows * tile_cols
    layers = 2 * LAYERS
    leaving = [
        vmem((freqs, REST * GROUP, planes * LANES), f32),
        vmem((freqs, QUADS, QUAD, (planes - 1) * LANES), f32),
        vmem((freqs, QUADS, QUAD, LANES), f32),
    ]
    final, flat = pl.pallas_call(
        functools.partial(kernel, bands, freqs, cols),
        out_shape=(
            jax.ShapeDtypeStruct((freqs, DIRP, LANES), f32),
            jax.ShapeDtypeStruct((layers, LANES), f32),
        ),
        in_specs=[anywhere] * 11,
        out_specs=(anywhere, anywhere),
        scratch_shapes=[
            pltpu.SMEM((freqs,), jnp.int32),
            pltpu.SMEM(stokes_route.shape[::-1], jnp.int32),
            vmem((DIRP, rows, cols), f32),
            vmem((DIRP, DEPTH, cols), f32),
            vmem((DIRP, DEPTH, cols), f32),
            vmem((2, rows, tile_cols, LAYERS), f32),
            vmem((comps, comps), bf16),
            vmem((comps, comps), bf16),
            vmem((parts, comps), bf16),
            vmem((DIRP, 2), f32),
            vmem((2, parts), f32),
            vmem((parts, parts), bf16),
            vmem((parts, parts), bf16),
            vmem(limiter_flags.shape, jnp.int32),
            vmem(sea_mask.shape, jnp.int32),
            vmem((n, 8, block), f32),
            vmem((8 * n, block), f32),
            vmem((SUB, 8 * n, block), f32),
            vmem((SUB, 8 * n, block), f32),
            vmem((SUB, planes, DIRP, LANES), f32),
            vmem((SUB, planes, DIRP, LANES), f32),
            vmem((planes, DIRP, LANES), f32),
            vmem((layers, tile_cells), f32),
            vmem((layers, tile_cells), f32),
            vmem((9, layers, tile_cells), f32),
            vmem((freqs, 2, tile_cells), f32),
            vmem((freqs, 2, tile_cells), f32),
            vmem((freqs, 2, tile_cells), f32),
            vmem((freqs, 2, tile_cells), f32),
            vmem((2, n, block), f32),
            vmem((3, 8 * n, block), f32),
            vmem((freqs, 8, LANES), f32),
            vmem((GROUPS, 7, 8 * n, block), f32),
            vmem((freqs, 6 * planes, DIRP, LANES), f32),
            vmem((GROUPS, 8 * n, block), f32),
            *leaving,
            *leaving,
            vmem((parts, planes * LANES), f32),
            vmem((freqs, DIRP, planes * LANES), f32),
            vmem((freqs, DIRP, LANES), f32),
            vmem((freqs, DIRP, LANES), f32),
            vmem((layers, planes * LANES), f32),
            vmem((layers, parts), f32),
            vmem((layers, LANES), f32),
            dma((11,)),
            dma((2, 2)),
            dma((2, 3)),
            dma((2,)),
            dma((2, len(PARTS) + 2)),
            dma((2,)),
            dma((2,)),
        ],
        compiler_params=pltpu.CompilerParams(
            collective_id=0, has_side_effects=True, vmem_limit_bytes=60 * 1024 * 1024
        ),
    )(
        current_route,
        stokes_route.T,
        spectrum.reshape(DIR, rows, cols),
        velocity.transpose(0, 2, 3, 1),
        gain_matrix,
        quad_matrix,
        limiter_flags,
        sea_mask,
        jnp.asarray(widen, bf16),
        jnp.asarray(wave),
        jnp.asarray(trig.reshape(2, parts)),
    )
    whole = pl.BlockSpec(memory_space=vmem)
    result, ocean = pl.pallas_call(
        finish,
        out_shape=(
            jax.ShapeDtypeStruct((DIR, rows, cols), f32),
            jax.ShapeDtypeStruct((2, rows, tile_cols, LAYERS), f32),
        ),
        in_specs=[whole] * 2,
        out_specs=(whole, whole),
    )(final, flat)
    return (result.reshape(1, DIR, rows, cols), ocean.transpose(0, 3, 1, 2))


def solution(mesh):
    return jax.shard_map(
        body,
        mesh=mesh,
        in_specs=(
            P("freq", None, "band", None),
            P(None, None, "band", "freq"),
            P(),
            P(),
            P(),
            P(),
            P(),
            P(),
        ),
        out_specs=(P("freq", None, "band", None), P(None, None, "band", "freq")),
        check_vma=False,
    )
```

```python
import functools

import jax
import jax.numpy as jnp
import numpy as np
from jax import lax
from jax.experimental import pallas as pl
from jax.experimental.pallas import tpu as pltpu
from jax.sharding import PartitionSpec as P

DIR = 36
LAYERS = 24
SUB = 4
CYCLES = 2
OSTEPS = 3


precise = lax.Precision.HIGHEST
ocean_dt = 0.2
viscous = 0.5
coriolis = 1.0
mixing = 0.5
friction = 0.1


GROUP = 8
LANES = 128
DIRP = -(-DIR // GROUP) * GROUP
GROUPS = DIRP // GROUP
FULL = DIR // GROUP * GROUP
TAIL = DIR - FULL
HALO = SUB
DEPTH = CYCLES * SUB
PARTS = ((0, 1), (1, 3))
REST = 3
QUAD = 4
QUADS = (DIR - REST * GROUP) // QUAD
MESH = pl.DeviceIdType.MESH


def swap_pieces(blocks, piece, width):
    lane = lax.broadcasted_iota(jnp.int32, blocks[0].shape, 1)
    out = list(blocks)
    far = width // 2
    while far:
        low = (lane & (far * piece)) == 0
        for a in range(width):
            if a & far:
                continue
            b = a + far
            x, y = out[a], out[b]
            out[a] = jnp.where(low, x, pltpu.roll(y, far * piece, 1))
            out[b] = jnp.where(low, pltpu.roll(x, LANES - far * piece, 1), y)
        far //= 2
    return out


def packing(rows, planes, pitch, tile_cols):
    places = LANES // tile_cols
    free = set(range(places))
    left = {
        m: [q for q in range(LANES // pitch) if 0 <= m + planes * q - HALO < rows]
        for m in range(planes)
    }
    moves, where = [], {}
    while any(left.values()):
        best = None
        for m in range(planes):
            for by in range(places):
                fits = [
                    q for q in left[m] if (q * pitch // tile_cols + by) % places in free
                ]
                if best is None or len(fits) > len(best[2]):
                    best = (m, by, fits)
        m, by, fits = best
        spots = [(q * pitch // tile_cols + by) % places for q in fits]
        moves.append((m, (by * tile_cols - HALO) % LANES, spots))
        for q, spot in zip(fits, spots):
            where[m + planes * q - HALO] = spot
            free.remove(spot)
            left[m].remove(q)
    return moves, where


def pack(blocks, moves, tile_cols):
    lane = lax.broadcasted_iota(jnp.int32, blocks[0].shape, 1)
    total = None
    for m, shift, spots in moves:
        piece = pltpu.roll(blocks[m], shift, 1) if shift else blocks[m]
        if total is None:
            total = piece
            continue
        hit = None
        for spot in spots:
            one = (lane >= spot * tile_cols) & (lane < (spot + 1) * tile_cols)
            hit = one if hit is None else hit | one
        total = jnp.where(hit, piece, total)
    return total


def parts_of(courant):
    up, down = jnp.maximum(courant, 0.0), jnp.minimum(courant, 0.0)
    return up, down, 0.5 * (courant * courant - (up - down))


def kernel(
    bands,
    freqs,
    cols,
    route_in,
    stokes_in,
    spectrum,
    velocity,
    gain_in,
    quad_in,
    flags_in,
    sea_in,
    widen_in,
    wave_in,
    trig_in,
    final,
    ocean_out,
    route,
    stokes_route,
    spec,
    halo_low,
    halo_high,
    vel,
    gain_raw,
    quad_raw,
    widen,
    wave,
    trig,
    gain,
    quad,
    flag_raw,
    sea_raw,
    flag_blk,
    sea_blk,
    flag_north,
    flag_east,
    flag_north2,
    flag_east2,
    sea2,
    tile,
    ready,
    tiles,
    route_out,
    route_own,
    route_low,
    route_high,
    drift,
    faces,
    faces2,
    coef,
    coef2,
    start,
    leave,
    leave_end,
    leave_last,
    arrive,
    arrive_end,
    arrive_last,
    clean,
    first,
    packed,
    back,
    ocean,
    weight,
    flat,
    load_sems,
    halo_sems,
    route_sems,
    tile_sems,
    out_sems,
    back_sems,
    store_sems,
):
    band = lax.axis_index("band")
    me = lax.axis_index("freq")
    f32 = jnp.float32
    rows = spectrum.shape[1]
    tile_cols = velocity.shape[2]
    tall = rows + 2 * DEPTH
    block = max(LANES, cols)
    slots = block // cols
    n = tall // slots
    pitch = tile_cols + 2 * HALO
    per = LANES // pitch
    planes = (rows + 2 * HALO) // per
    seam = LANES - pitch
    moves, spot_of = packing(rows, planes, pitch, tile_cols)
    has_low = band > 0
    has_high = band < bands - 1

    mid = freqs // 2
    side, place = me // mid, lax.rem(me, mid)
    near = [side * mid + lax.rem(place + i, mid) for i in [*range(2, mid), 1][: mid - 1]]
    far = [(1 - side) * mid + lax.rem(2 * mid - 1 - place - i, mid) for i in range(mid)]
    partners = []
    for i in range(mid):
        partners += near[i : i + 1] + [far[i]]

    def others(fn):
        for f in partners:
            fn(f)

    def every(fn):
        for f in range(freqs):
            fn(f)

    def copy(src, dst, sems, slot_send, slot_recv, to_band, to_freq):
        return pltpu.make_async_remote_copy(
            src_ref=src,
            dst_ref=dst,
            send_sem=sems.at[(0,) + slot_send],
            recv_sem=sems.at[(1,) + slot_recv],
            device_id=(to_band, to_freq),
            device_id_type=MESH,
        )

    def rolled(x, shift):
        shift %= x.shape[1]
        return pltpu.roll(x, shift, 1) if shift else x

    def locate(at):
        return (at, 0) if at < n else (tall - 1 - at, 1)

    def row_at(k, s):
        return tall - 1 - k if s else k

    def strided(ref, size, base, at):
        depth = ref.shape[1]
        if cols > LANES:
            return ref[pl.ds(base, size), at, :]
        return ref.reshape(ref.shape[0] * depth, cols)[
            pl.ds(base * depth + at, size, stride=depth), :
        ]

    def await_bytes(ref, sem):
        pltpu.make_async_copy(ref, ref, sem).wait()

    rest = pl.ds(0, freqs - 1)

    barrier = pltpu.get_barrier_semaphore()

    def greet(to_band, to_freq):
        pl.semaphore_signal(barrier, inc=1, device_id=(to_band, to_freq), device_id_type=MESH)

    others(lambda f: greet(band, f))

    @pl.when(has_low)
    def _():
        every(lambda f: greet(band - 1, f))

    @pl.when(has_high)
    def _():
        every(lambda f: greet(band + 1, f))

    load_vel = pltpu.make_async_copy(velocity, vel, load_sems.at[0])
    load_vel.start()
    load_route = pltpu.make_async_copy(route_in, route, load_sems.at[9])
    load_route.start()
    load_stokes = pltpu.make_async_copy(stokes_in, stokes_route, load_sems.at[10])
    load_stokes.start()
    load_spec = pltpu.make_async_copy(spectrum, spec.at[pl.ds(0, DIR)], load_sems.at[1])
    load_grid = [
        pltpu.make_async_copy(src, dst, load_sems.at[2 + i])
        for i, (src, dst) in enumerate(((flags_in, flag_raw), (sea_in, sea_raw)))
    ]
    loads = [
        pltpu.make_async_copy(src, dst, load_sems.at[4 + i])
        for i, (src, dst) in enumerate(
            (
                (wave_in, wave),
                (gain_in, gain_raw),
                (quad_in, quad_raw),
                (widen_in, widen),
                (trig_in, trig),
            )
        )
    ]
    for one in load_grid:
        one.start()
    load_spec.start()
    for one in loads:
        one.start()

    load_vel.wait()
    for c in range(2):
        field = vel[c].reshape(rows * tile_cols, LAYERS)
        tile[c * LAYERS : (c + 1) * LAYERS, :] = field.T

    ready[...] = pltpu.roll(
        0.15 * jnp.tanh(tile[...]), lax.rem(me * tile_cols, LANES), 1
    )

    def prepare(f):
        route_out[f, 0:1, :] = ready[pl.ds(route[f], 1), :]
        route_out[f, 1:2, :] = ready[pl.ds(LAYERS + route[f], 1), :]

    load_route.wait()
    every(prepare)
    count = freqs - 1 + freqs * (has_low.astype(jnp.int32) + has_high.astype(jnp.int32))
    pl.semaphore_wait(barrier, count)

    halo_to_low = copy(
        spectrum.at[:, pl.ds(0, DEPTH)], halo_high.at[pl.ds(0, DIR)], halo_sems,
        (0,), (0,), band - 1, me,
    )
    halo_to_high = copy(
        spectrum.at[:, pl.ds(rows - DEPTH, DEPTH)], halo_low.at[pl.ds(0, DIR)], halo_sems,
        (1,), (1,), band + 1, me,
    )

    def route_copy(f):
        return copy(route_out.at[f], route_own.at[me], route_sems, (0,), (0,), band, f)

    def route_to_low(f):
        return copy(
            route_out.at[f], route_high.at[me], route_sems, (1,), (1,), band - 1, f
        )

    def route_to_high(f):
        return copy(
            route_out.at[f], route_low.at[me], route_sems, (2,), (2,), band + 1, f
        )

    others(lambda f: route_copy(f).start())

    @pl.when(has_low)
    def _():
        every(lambda f: route_to_low(f).start())
        halo_to_low.start()

    @pl.when(has_high)
    def _():
        every(lambda f: route_to_high(f).start())
        halo_to_high.start()

    def near_tiles(fn):
        for down in (-1, 0, 1):
            for side in (-1, 0, 1):
                if down == 0 and side == 0:
                    continue
                to_band, to_freq = band + down, me + side
                there = (to_band >= 0) & (to_band < bands) & (to_freq >= 0) & (to_freq < freqs)
                mine = 3 * (1 + down) + 1 + side
                fn(there, mine, 8 - mine, to_band, to_freq)

    def tile_copy(mine, theirs, to_band, to_freq):
        return copy(tile, tiles.at[theirs], tile_sems, (), (), to_band, to_freq)

    def tile_start(there, mine, theirs, to_band, to_freq):
        @pl.when(there)
        def _():
            tile_copy(mine, theirs, to_band, to_freq).start()

        @pl.when(jnp.logical_not(there))
        def _():
            tiles[mine] = jnp.zeros_like(tile)

    near_tiles(tile_start)
    tiles[4] = tile[...]
    route_own[me] = route_out[me]

    pads = ((DIR, DIRP - DIR),)
    for at, size in pads:
        spec[at : at + size] = jnp.zeros((size, rows, cols), f32)
        halo_low[at : at + size] = jnp.zeros((size, DEPTH, cols), f32)
        halo_high[at : at + size] = jnp.zeros((size, DEPTH, cols), f32)

    @pl.when(jnp.logical_not(has_low))
    def _():
        halo_low[...] = jnp.zeros_like(halo_low)
        route_low[...] = jnp.zeros_like(route_low)

    @pl.when(jnp.logical_not(has_high))
    def _():
        halo_high[...] = jnp.zeros_like(halo_high)
        route_high[...] = jnp.zeros_like(route_high)

    for one in load_grid:
        one.wait()

    steps = CYCLES * SUB
    all_rows = sea_raw.shape[0]
    wide = (8, block)

    def grid_row(at):
        whole = jnp.clip(band * rows - DEPTH + at, 0, all_rows - 1)
        there = has_low if at < DEPTH else (None if at < DEPTH + rows else has_high)
        flag = strided(flag_raw, steps, 0, whole)
        sea = sea_raw[pl.ds(whole, 1), :].astype(f32)
        flag = flag.astype(f32)
        if there is not None:
            there = there.astype(f32)
            flag, sea = flag * there, sea * there
        return flag, sea

    for k in range(n):
        pieces = [grid_row(row_at(k, s)) for s in range(slots)]
        flag_blk[k] = jnp.concatenate([flag for flag, _ in pieces], axis=1)
        sea = jnp.concatenate([sea for _, sea in pieces], axis=1)
        sea_blk[8 * k : 8 * (k + 1), :] = jnp.broadcast_to(sea, wide)

    first_slot = lax.broadcasted_iota(jnp.int32, wide, 1) < cols
    for k in range(n):
        here = flag_blk[k]
        above = flag_blk[k + 1] if k + 1 < n else rolled(here, cols)
        if slots > 1:
            above = jnp.where(first_slot, above, here)
        beside = rolled(here, -1)
        for sub in range(SUB):
            there = slice(8 * k, 8 * (k + 1))
            flag_north[sub, there, :] = jnp.broadcast_to(above[sub : sub + 1], wide)
            flag_east[sub, there, :] = jnp.broadcast_to(beside[sub : sub + 1], wide)

    lane = lax.broadcasted_iota(jnp.int32, (8, LANES), 1)
    column = me * tile_cols - HALO + (lane & (pitch - 1))
    inside = (column >= 0) & (column < cols)
    window_flags, window_sea = [], []
    for m in range(planes):
        total_flags, total_sea = jnp.zeros((8, LANES), f32), jnp.zeros((8, LANES), f32)
        for q in range(per):
            k, s = locate(m + planes * q + DEPTH - HALO)
            shift = lax.rem(q * pitch - cols * s - tile_cols * me + HALO + 2 * block, block)
            hit = (lane >= q * pitch) & (lane < (q + 1) * pitch) & inside
            total_flags = jnp.where(
                hit, pltpu.roll(flag_blk[k], shift, 1)[:, :LANES], total_flags
            )
            total_sea = jnp.where(hit, pltpu.roll(sea_blk[8 * k : 8 * (k + 1), :], shift, 1)[:, :LANES], total_sea)
        window_flags.append(total_flags)
        window_sea.append(total_sea)
    for m in range(planes):
        sea2[m] = jnp.concatenate([window_sea[m]] * (FULL // 8), axis=0)
        above = window_flags[m + 1] if m + 1 < planes else rolled(window_flags[0], -pitch)
        beside = rolled(window_flags[m], -1)
        for sub in range(SUB):
            step = SUB + sub
            flag_north2[sub, m] = jnp.broadcast_to(above[step : step + 1], (FULL, LANES))
            flag_east2[sub, m] = jnp.broadcast_to(beside[step : step + 1], (FULL, LANES))

    load_spec.wait()
    load_stokes.wait()
    for one in loads:
        one.wait()

    for raw, padded in ((gain_raw, gain), (quad_raw, quad)):
        half = jnp.dot(widen[...], raw[...], preferred_element_type=f32).astype(jnp.bfloat16)
        padded[...] = lax.dot_general(
            half, widen[...], (((1,), (1,)), ((), ())), preferred_element_type=f32
        ).astype(jnp.bfloat16)

    layer = lax.broadcasted_iota(jnp.int32, (LAYERS, 1), 0)
    component = lax.broadcasted_iota(jnp.int32, (LAYERS, freqs * DIR), 1)
    deposits = jnp.zeros((LAYERS, freqs * DIR), f32)
    for g in range(freqs):
        deposit = jnp.zeros((LAYERS, 1), f32)
        for j in range(stokes_route.shape[0]):
            hit = (layer == stokes_route[j, g]).astype(f32)
            deposit = deposit + hit * (1.0 / (1.0 + j))
        tail = freqs * FULL + g * TAIL
        own = (component >= g * FULL) & (component < (g + 1) * FULL)
        own = own | ((component >= tail) & (component < tail + TAIL))
        deposits = jnp.where(own, deposit, deposits)
    for c in range(2):
        weight[c * LAYERS : (c + 1) * LAYERS, :] = deposits * trig[c : c + 1, :]

    @pl.when(has_low)
    def _():
        halo_to_high.wait_recv()
        await_bytes(route_low, route_sems.at[1, 2])

    @pl.when(has_high)
    def _():
        halo_to_low.wait_recv()
        await_bytes(route_high, route_sems.at[1, 1])

    number = me.astype(f32) + 0.5
    my_rate = 0.5 + 0.3 * number / freqs

    def row_of(base, at):
        if at < DEPTH:
            return strided(halo_low, GROUP, base, at)
        if at < DEPTH + rows:
            return strided(spec, GROUP, base, at - DEPTH)
        return strided(halo_high, GROUP, base, at - DEPTH - rows)

    starts = [
        jnp.concatenate([row_of(group * GROUP, row_at(k, s)) for s in range(slots)], axis=1)
        for group in range(GROUPS)
        for k in range(n)
    ]
    for i, one in enumerate(starts):
        start[i // n, 8 * (i % n) : 8 * (i % n + 1), :] = one

    await_bytes(route_own.at[rest], route_sems.at[1, 0])

    stacks = [
        jnp.concatenate(
            [route_low[j], route_own[j], route_high[j], jnp.zeros((2, LANES), f32)], axis=0
        )
        for j in range(freqs)
    ]
    reach = min(cols, LANES) // tile_cols
    places = LANES // tile_cols
    spot_masks = [
        (lane >= spot * tile_cols) & (lane < (spot + 1) * tile_cols) for spot in range(places)
    ]
    for row in range(rows):
        halves = []
        for half in range(block // LANES):
            total = stacks[half * reach]
            for j in range(1, reach):
                total = jnp.where(
                    spot_masks[(row + j) % places], stacks[half * reach + j], total
                )
            halves.append(total)
        moved = []
        for s in range(slots):
            turned = [rolled(x, cols * s - row * tile_cols) for x in halves]
            moved.append(turned[0] if len(turned) == 1 else jnp.concatenate(turned, axis=1))
        for source in range(3):
            at = row + DEPTH + rows * (source - 1)
            if at < 0 or at >= tall:
                continue
            k, s = locate(at)
            for c in range(2):
                line = 2 * source + c
                drift[c, k : k + 1, cols * s : cols * (s + 1)] = moved[s][
                    line : line + 1, cols * s : cols * (s + 1)
                ]
    blane = lax.broadcasted_iota(jnp.int32, (1, block), 1)
    last = ((blane & (cols - 1)) == cols - 1).astype(f32)
    inner = 1.0 - last
    east, north = drift[0], drift[1]
    above = jnp.concatenate([north[1:], rolled(north[n - 1 :], cols)], axis=0)
    sign = jnp.where(blane < cols, 1.0, -1.0)
    for i, face in enumerate(
        (sign * (0.5 * (north + above)), 0.5 * (inner * east + rolled(east, -1)), 0.5 * east)
    ):
        for k in range(n):
            faces[i, 8 * k : 8 * (k + 1), :] = jnp.broadcast_to(face[k : k + 1], wide)

    def advect_first(group):
        table = wave[group * GROUP : (group + 1) * GROUP, :]

        def rate_of(i):
            rate = jnp.broadcast_to(table[:, i : i + 1] * my_rate, wide)
            return jnp.concatenate([rate] * n, axis=0)

        rate_east = rate_of(0)
        for axis, rate in ((0, rate_of(1)), (1, rate_east)):
            if axis == 0 and slots > 1:
                rate = rate * sign
            for i, one in enumerate(parts_of(rate + faces[axis])):
                coef[group, 3 * axis + i] = one
        coef[group, 6] = 1.0 - last * jnp.maximum(rate_east + faces[2], 0.0)
        state = start[group]
        for sub in range(SUB):
            here, new = slice(8 * sub, 8 * n), slice(8 * (sub + 1), 8 * n)
            beyond = rolled(state[-8:], cols)
            more = flag_north[sub, here] * coef[group, 2, here]
            flux = (coef[group, 0, here] + more) * state + (
                coef[group, 1, here] - more
            ) * jnp.concatenate([state[8:], beyond], axis=0)
            state = state[8:] - (flux[8:] - flux[:-8])
            more = flag_east[sub, new] * coef[group, 5, new]
            flux = (coef[group, 3, new] + more) * (inner * state) + (
                coef[group, 4, new] - more
            ) * rolled(state, -1)
            state = (
                coef[group, 6, new] * state - (inner * flux - rolled(flux, 1))
            ) * sea_blk[new, :]
        width = min(cols, LANES) // pitch
        low_half = lax.broadcasted_iota(jnp.int32, (8 * planes, LANES), 1) < width * pitch
        for odd in range(2):
            turned = rolled(state, HALO - odd * tile_cols)
            for half in range(block // LANES):
                sources = []
                for i in range(width):
                    pieces = []
                    for s in range(slots):
                        lines = []
                        for m in range(planes):
                            k, slot = locate(m + planes * (i + width * s) + DEPTH - HALO)
                            assert slot == s and k >= SUB
                            k -= SUB
                            lines.append(
                                turned[8 * k : 8 * (k + 1), half * LANES : (half + 1) * LANES]
                            )
                        pieces.append(jnp.concatenate(lines, axis=0))
                    sources.append(pieces[0] if slots == 1 else jnp.where(low_half, *pieces))
                for e, one in enumerate(swap_pieces(sources, pitch, width)):
                    to = 2 * (e + width * half) + odd
                    for m in range(planes):
                        cells = one[8 * m : 8 * (m + 1)]
                        at = slice(m * LANES, (m + 1) * LANES)
                        if group < REST:
                            leave[to, group * GROUP : (group + 1) * GROUP, at] = cells
                            continue
                        end, at = (leave_last, slice(0, LANES)) if m == planes - 1 else (leave_end, at)
                        first_quad = (group - REST) * GROUP // QUAD
                        for i in range(min(GROUP // QUAD, QUADS - first_quad)):
                            end[to, first_quad + i, :, at] = cells[i * QUAD : (i + 1) * QUAD]

    def part_rows(part):
        low, high = PARTS[part]
        return pl.ds(low * GROUP, (high - low) * GROUP)

    def out_copy(part, f):
        there = part_rows(part)
        return copy(
            leave.at[f, there], arrive.at[me, there], out_sems, (part,), (part,), band, f
        )

    ends = ((leave_end, arrive_end, len(PARTS)), (leave_last, arrive_last, len(PARTS) + 1))

    def end_copy(leaving, arriving, part, f):
        return copy(leaving.at[f], arriving.at[me], out_sems, (part,), (part,), band, f)

    def received():
        for part in range(len(PARTS)):
            yield arrive.at[rest, part_rows(part)], part
        for _, arriving, part in ends:
            yield arriving.at[rest], part

    for part, (low, high) in enumerate(PARTS):
        for group in range(low, high):
            advect_first(group)
        others(lambda f: out_copy(part, f).start())
    for group in range(REST, GROUPS):
        advect_first(group)
    for leaving, arriving, part in ends:
        others(lambda f: end_copy(leaving, arriving, part, f).start())
    arrive[me] = leave[me]
    arrive_end[me] = leave_end[me]
    arrive_last[me] = leave_last[me]

    deep = 1 + has_low.astype(jnp.int32) + has_high.astype(jnp.int32)
    broad = 1 + (me > 0).astype(jnp.int32) + (me < freqs - 1).astype(jnp.int32)

    def await_tiles(way):
        for a in (2, 3):
            for b in (2, 3):

                @pl.when((deep == a) & (broad == b))
                def _():
                    await_bytes(tiles.at[pl.ds(0, a * b - 1)], tile_sems.at[way])

    await_tiles(1)
    tall_lane = lax.broadcasted_iota(jnp.int32, tile.shape, 1)
    for m in range(planes):
        total = jnp.zeros(tile.shape, f32)
        for q in range(per):
            row = m + planes * q - HALO
            down = 0 if row < 0 else (1 if row < rows else 2)
            from_row = row + rows * (1 - down)
            lead = q * pitch
            for side, width, from_col in (
                (0, HALO, tile_cols - HALO), (1, tile_cols, 0), (2, HALO, 0),
            ):
                piece = rolled(tiles[3 * down + side], lead - from_row * tile_cols - from_col)
                total = jnp.where((tall_lane >= lead) & (tall_lane < lead + width), piece, total)
                lead += width
        ocean[:, m * LANES : (m + 1) * LANES] = total

    def face_step(g, carry):
        east = 0.15 * jnp.tanh(ocean[pl.ds(route[g], 1), :])
        north = 0.15 * jnp.tanh(ocean[pl.ds(LAYERS + route[g], 1), :])
        for m in range(planes):
            here = north[:, m * LANES : (m + 1) * LANES]
            above = (
                north[:, (m + 1) * LANES : (m + 2) * LANES]
                if m + 1 < planes
                else rolled(north[:, :LANES], -pitch)
            )
            faces2[g, m : m + 1, :] = 0.5 * (here + above)
            here = east[:, m * LANES : (m + 1) * LANES]
            faces2[g, planes + m : planes + m + 1, :] = 0.5 * (here + rolled(here, -1))
        return carry

    [face_step(g, 0) for g in range(freqs)]

    def source(whole):
        grown = jnp.dot(gain[...], whole.astype(jnp.bfloat16), preferred_element_type=f32)
        quartic = jnp.dot(
            quad[...], (whole * whole).astype(jnp.bfloat16), preferred_element_type=f32
        )
        return whole * (1.0 + 0.5 * jnp.tanh(grown) - 0.25 * jnp.tanh(quartic))

    total_rows = freqs * DIR
    incoming = list(received())
    for ref, part in incoming[:-1]:
        await_bytes(ref, out_sems.at[1, part])
    for m in range(planes):
        there = slice(m * LANES, (m + 1) * LANES)
        end, at = (arrive_end, there)
        if m == planes - 1:
            await_bytes(incoming[-1][0], out_sems.at[1, incoming[-1][1]])
            end, at = (arrive_last, slice(0, LANES))
        pieces = []
        for f in range(freqs):
            pieces.append(arrive[f, :, there])
            pieces += [end[f, i, :, at] for i in range(QUADS - 1)]
        pieces += [end[f, QUADS - 1, :, at] for f in range(freqs)]
        whole = jnp.concatenate(pieces, axis=0) * sea2[m][0:1]
        clean[:, there] = whole
        first[:, there] = source(whole)

    def advect_second(g, at, rates, face_of):
        rate_east, rate_north = [jnp.broadcast_to(x, (FULL, LANES)) for x in rates]
        state = [first[at, m * LANES : (m + 1) * LANES] for m in range(planes)]
        for m in range(planes):
            for axis, rate in ((0, rate_north), (planes, rate_east)):
                for i, one in enumerate(parts_of(rate + face_of(axis + m))):
                    coef2[g, 3 * (axis + m) + i] = one
        for sub in range(SUB):
            fluxes = []
            for m in range(planes):
                here = 3 * m
                more = flag_north2[sub, m] * coef2[g, here + 2]
                above = state[m + 1] if m + 1 < planes else rolled(state[0], -pitch)
                fluxes.append(
                    (coef2[g, here] + more) * state[m] + (coef2[g, here + 1] - more) * above
                )
            cells = [
                state[m] - (fluxes[m] - (fluxes[m - 1] if m else rolled(fluxes[-1], pitch)))
                for m in range(planes)
            ]
            fluxes = []
            for m in range(planes):
                here = 3 * (planes + m)
                more = flag_east2[sub, m] * coef2[g, here + 2]
                fluxes.append(
                    (coef2[g, here] + more) * cells[m]
                    + (coef2[g, here + 1] - more) * rolled(cells[m], -1)
                )
            state = [
                (cells[m] - (fluxes[m] - rolled(fluxes[m], 1))) * sea2[m] for m in range(planes)
            ]
        packed[at, :] = pack(state, moves, tile_cols)

    for g in range(freqs):
        speed = 0.5 + 0.3 * (g + 0.5) / freqs
        table = wave[:FULL, :] * speed
        advect_second(
            g,
            slice(g * FULL, (g + 1) * FULL),
            (table[:, 0:1], table[:, 1:2]),
            lambda i: faces2[g, i : i + 1, :],
        )
    share = FULL // TAIL
    for chunk in range(freqs // share):
        table = wave[DIRP + chunk * FULL : DIRP + (chunk + 1) * FULL, :]
        advect_second(
            freqs + chunk,
            slice((freqs + chunk) * FULL, (freqs + chunk + 1) * FULL),
            (table[:, 0:1], table[:, 1:2]),
            lambda i: jnp.concatenate(
                [
                    jnp.broadcast_to(faces2[chunk * share + j, i : i + 1, :], (TAIL, LANES))
                    for j in range(share)
                ],
                axis=0,
            ),
        )
    updated = source(packed[...])
    for f in range(freqs):
        for i in range(FULL // QUAD):
            at = f * FULL + i * QUAD
            back[f, i] = updated[at : at + QUAD]
        at = freqs * FULL + f * TAIL
        back[f, FULL // QUAD] = updated[at : at + TAIL]

    def back_copy(f):
        return copy(back.at[f], final.at[me], back_sems, (), (), band, f)

    others(lambda f: back_copy(f).start())
    keep = pltpu.make_async_copy(back.at[me], final.at[me], store_sems.at[0])
    keep.start()

    stokes = jnp.dot(
        weight[...], clean[...],
        precision=precise, preferred_element_type=f32,
    )
    level = lax.broadcasted_iota(jnp.int32, (LAYERS, LANES), 0)
    planes_of = range(planes)

    def split(x, c):
        return [
            x[c * LAYERS : (c + 1) * LAYERS, m * LANES : (m + 1) * LANES] for m in planes_of
        ]

    def spreading(field):
        outs = []
        for m in planes_of:
            here = field[m]
            above = field[m + 1] if m + 1 < planes else rolled(field[0], -pitch)
            below = field[m - 1] if m else rolled(field[-1], pitch)
            sides = rolled(here, 1) + rolled(here, -1)
            over = jnp.where(level < LAYERS - 1, pltpu.roll(here, LAYERS - 1, 0), 0.0)
            under = jnp.where(level > 0, pltpu.roll(here, 1, 0), 0.0)
            outs.append(
                viscous * (sides + above + below - 4.0 * here)
                + mixing * (over + under - 2.0 * here)
                - friction * here
            )
        return outs

    both = ocean[...]
    u, v = split(both, 0), split(both, 1)
    stokes_east, stokes_north = split(stokes, 0), split(stokes, 1)
    for _ in range(OSTEPS):
        change_u, change_v = spreading(u), spreading(v)
        u, v = (
            [
                (u[m] + ocean_dt * (change_u[m] + coriolis * (v[m] + stokes_north[m])))
                * sea2[m][0:1]
                for m in planes_of
            ],
            [
                (v[m] + ocean_dt * (change_v[m] - coriolis * (u[m] + stokes_east[m])))
                * sea2[m][0:1]
                for m in planes_of
            ],
        )
    for c, field in enumerate((u, v)):
        flat[c * LAYERS : (c + 1) * LAYERS, :] = pack(field, moves, tile_cols)
    store_ocean = pltpu.make_async_copy(flat, ocean_out, store_sems.at[1])
    store_ocean.start()

    await_bytes(route_out.at[rest], route_sems.at[0, 0])

    @pl.when(has_low)
    def _():
        await_bytes(route_out, route_sems.at[0, 1])
        halo_to_low.wait_send()

    @pl.when(has_high)
    def _():
        await_bytes(route_out, route_sems.at[0, 2])
        halo_to_high.wait_send()

    await_tiles(0)
    for part in range(len(PARTS)):
        await_bytes(leave.at[rest, part_rows(part)], out_sems.at[0, part])
    for leaving, _, part in ends:
        await_bytes(leaving.at[rest], out_sems.at[0, part])

    await_bytes(final.at[rest], back_sems.at[1])
    await_bytes(back.at[rest], back_sems.at[0])
    store_ocean.wait()
    keep.wait()


def finish(final, flat, result, ocean_out):
    freqs = final.shape[0]
    rows, cols = result.shape[1:]
    tile_cols = ocean_out.shape[2]
    pitch = tile_cols + 2 * HALO
    planes = (rows + 2 * HALO) * pitch // LANES
    _, spot_of = packing(rows, planes, pitch, tile_cols)
    width = min(freqs, LANES // tile_cols)
    reach = width * tile_cols
    row_at = {spot: row for row, spot in spot_of.items()}
    for c in range(2):
        turned = flat[c * LAYERS : (c + 1) * LAYERS, :].T
        for row in range(rows):
            spot = spot_of[row]
            ocean_out[c, row] = turned[spot * tile_cols : (spot + 1) * tile_cols, :]
    for chunk in range(freqs // width):
        columns = [
            jnp.concatenate(
                [final[chunk * width + j, i] for i in range(DIR // QUAD)], axis=0
            )
            for j in range(width)
        ]
        for i, one in enumerate(swap_pieces(columns, tile_cols, width)):
            for s in range(LANES // reach):
                row = row_at[s * width + i]
                cells = pltpu.roll(one, LANES - s * reach, 1) if s else one
                cells = cells[:, :reach]
                if cols > LANES:
                    result[:, row, chunk * reach : (chunk + 1) * reach] = cells
                else:
                    result.reshape(DIR * rows, cols)[pl.ds(row, DIR, stride=rows), :] = cells


def body(
    spectrum,
    velocity,
    gain_matrix,
    quad_matrix,
    limiter_flags,
    sea_mask,
    current_route,
    stokes_route,
):
    bands = lax.axis_size("band")
    freqs = lax.axis_size("freq")
    rows, cols = spectrum.shape[2:]
    tile_cols = velocity.shape[3]
    pitch = tile_cols + 2 * HALO
    planes = (rows + 2 * HALO) * pitch // LANES
    tall = rows + 2 * DEPTH
    block = max(LANES, cols)
    n = tall * cols // block
    parts = freqs * DIR
    assert CYCLES == 2 and spectrum.shape[0] == 1 and rows % 8 == 0 and DEPTH % 8 == 0
    assert rows * tile_cols == LANES and rows >= DEPTH and tile_cols >= HALO >= OSTEPS
    assert pitch == 2 * tile_cols and LANES % pitch == 0 and freqs * tile_cols == cols
    assert (rows + 2 * HALO) % (LANES // pitch) == 0 and cols & (cols - 1) == 0
    assert block % cols == 0 and rows % 2 == 0 and n * block == tall * cols and cols % pitch == 0
    assert bands > 1 and freqs * TAIL % FULL == 0 and TAIL == QUAD and 2 * TAIL == GROUP and CYCLES * SUB == 8 and 2 * planes <= 8 and block // cols <= 2
    angles = (np.arange(DIR) + 0.5) * (2.0 * np.pi / DIR)
    waves = np.stack([np.cos(angles), np.sin(angles)])
    comps = freqs * DIR
    which, dirs = np.divmod(np.arange(comps), DIR)
    order = np.where(
        dirs < FULL, which * FULL + dirs, freqs * FULL + which * TAIL + dirs - FULL
    )
    wave = np.zeros((DIRP + freqs * TAIL, 2), np.float32)
    wave[:DIR] = waves.T
    speeds = 0.5 + 0.3 * (np.arange(freqs) + 0.5) / freqs
    wave[DIRP:] = (speeds[:, None, None] * waves.T[FULL:]).reshape(-1, 2)
    factor = (0.5 + 1.5 * (np.arange(freqs) + 0.5) / freqs) * DIR ** (-0.5)
    trig = np.zeros((2, comps), np.float32)
    trig[:, order] = waves[:, dirs] * factor[which]
    widen = np.zeros((comps, comps), np.float32)
    widen[order, np.arange(comps)] = 1.0
    f32, bf16 = jnp.float32, jnp.bfloat16
    anywhere = pl.BlockSpec(memory_space=pl.ANY)
    dma = pltpu.SemaphoreType.DMA
    vmem = pltpu.VMEM
    tile_cells = rows * tile_cols
    layers = 2 * LAYERS
    leaving = [
        vmem((freqs, REST * GROUP, planes * LANES), f32),
        vmem((freqs, QUADS, QUAD, (planes - 1) * LANES), f32),
        vmem((freqs, QUADS, QUAD, LANES), f32),
    ]
    final, flat = pl.pallas_call(
        functools.partial(kernel, bands, freqs, cols),
        out_shape=(
            jax.ShapeDtypeStruct((freqs, DIR // QUAD, QUAD, LANES), f32),
            jax.ShapeDtypeStruct((layers, LANES), f32),
        ),
        in_specs=[anywhere] * 11,
        out_specs=(anywhere, anywhere),
        scratch_shapes=[
            pltpu.SMEM((freqs,), jnp.int32),
            pltpu.SMEM(stokes_route.shape[::-1], jnp.int32),
            vmem((DIRP, rows, cols), f32),
            vmem((DIRP, DEPTH, cols), f32),
            vmem((DIRP, DEPTH, cols), f32),
            vmem((2, rows, tile_cols, LAYERS), f32),
            vmem((comps, comps), bf16),
            vmem((comps, comps), bf16),
            vmem((parts, comps), bf16),
            vmem(wave.shape, f32),
            vmem((2, parts), f32),
            vmem((parts, parts), bf16),
            vmem((parts, parts), bf16),
            vmem(limiter_flags.shape, jnp.int32),
            vmem(sea_mask.shape, jnp.int32),
            vmem((n, 8, block), f32),
            vmem((8 * n, block), f32),
            vmem((SUB, 8 * n, block), f32),
            vmem((SUB, 8 * n, block), f32),
            vmem((SUB, planes, FULL, LANES), f32),
            vmem((SUB, planes, FULL, LANES), f32),
            vmem((planes, FULL, LANES), f32),
            vmem((layers, tile_cells), f32),
            vmem((layers, tile_cells), f32),
            vmem((9, layers, tile_cells), f32),
            vmem((freqs, 2, tile_cells), f32),
            vmem((freqs, 2, tile_cells), f32),
            vmem((freqs, 2, tile_cells), f32),
            vmem((freqs, 2, tile_cells), f32),
            vmem((2, n, block), f32),
            vmem((3, 8 * n, block), f32),
            vmem((freqs, 8, LANES), f32),
            vmem((GROUPS, 7, 8 * n, block), f32),
            vmem((parts // FULL, 6 * planes, FULL, LANES), f32),
            vmem((GROUPS, 8 * n, block), f32),
            *leaving,
            *leaving,
            vmem((parts, planes * LANES), f32),
            vmem((parts, planes * LANES), f32),
            vmem((parts, LANES), f32),
            vmem((freqs, DIR // QUAD, QUAD, LANES), f32),
            vmem((layers, planes * LANES), f32),
            vmem((layers, parts), f32),
            vmem((layers, LANES), f32),
            dma((11,)),
            dma((2, 2)),
            dma((2, 3)),
            dma((2,)),
            dma((2, len(PARTS) + 2)),
            dma((2,)),
            dma((2,)),
        ],
        compiler_params=pltpu.CompilerParams(
            collective_id=0, has_side_effects=True, vmem_limit_bytes=60 * 1024 * 1024
        ),
    )(
        current_route,
        stokes_route.T,
        spectrum.reshape(DIR, rows, cols),
        velocity.transpose(0, 2, 3, 1),
        gain_matrix,
        quad_matrix,
        limiter_flags,
        sea_mask,
        jnp.asarray(widen, bf16),
        jnp.asarray(wave),
        jnp.asarray(trig),
    )
    whole = pl.BlockSpec(memory_space=vmem)
    result, ocean = pl.pallas_call(
        finish,
        out_shape=(
            jax.ShapeDtypeStruct((DIR, rows, cols), f32),
            jax.ShapeDtypeStruct((2, rows, tile_cols, LAYERS), f32),
        ),
        in_specs=[whole] * 2,
        out_specs=(whole, whole),
    )(final, flat)
    return (result.reshape(1, DIR, rows, cols), ocean.transpose(0, 3, 1, 2))


def solution(mesh):
    return jax.shard_map(
        body,
        mesh=mesh,
        in_specs=(
            P("freq", None, "band", None),
            P(None, None, "band", "freq"),
            P(),
            P(),
            P(),
            P(),
            P(),
            P(),
        ),
        out_specs=(P("freq", None, "band", None), P(None, None, "band", "freq")),
        check_vma=False,
    )
```

```python
import functools

import jax
import jax.numpy as jnp
import numpy as np
from jax import lax
from jax.experimental import pallas as pl
from jax.experimental.pallas import tpu as pltpu
from jax.sharding import PartitionSpec as P

DIR = 36
LAYERS = 24
SUB = 4
CYCLES = 2
OSTEPS = 3


precise = lax.Precision.HIGHEST
ocean_dt = 0.2
viscous = 0.5
coriolis = 1.0
mixing = 0.5
friction = 0.1


GROUP = 8
LANES = 128
DIRP = -(-DIR // GROUP) * GROUP
GROUPS = DIRP // GROUP
FULL = DIR // GROUP * GROUP
TAIL = DIR - FULL
HALO = SUB
DEPTH = CYCLES * SUB
PARTS = ((0, 1), (1, 3))
REST = 3
QUAD = 4
QUADS = (DIR - REST * GROUP) // QUAD
MESH = pl.DeviceIdType.MESH


def swap_pieces(blocks, piece, width):
    lane = lax.broadcasted_iota(jnp.int32, blocks[0].shape, 1)
    out = list(blocks)
    far = width // 2
    while far:
        low = (lane & (far * piece)) == 0
        for a in range(width):
            if a & far:
                continue
            b = a + far
            x, y = out[a], out[b]
            out[a] = jnp.where(low, x, pltpu.roll(y, far * piece, 1))
            out[b] = jnp.where(low, pltpu.roll(x, LANES - far * piece, 1), y)
        far //= 2
    return out


def packing(rows, planes, pitch, tile_cols):
    places = LANES // tile_cols
    free = set(range(places))
    left = {
        m: [q for q in range(LANES // pitch) if 0 <= m + planes * q - HALO < rows]
        for m in range(planes)
    }
    moves, where = [], {}
    while any(left.values()):
        best = None
        for m in range(planes):
            for by in range(places):
                fits = [
                    q for q in left[m] if (q * pitch // tile_cols + by) % places in free
                ]
                if best is None or len(fits) > len(best[2]):
                    best = (m, by, fits)
        m, by, fits = best
        spots = [(q * pitch // tile_cols + by) % places for q in fits]
        moves.append((m, (by * tile_cols - HALO) % LANES, spots))
        for q, spot in zip(fits, spots):
            where[m + planes * q - HALO] = spot
            free.remove(spot)
            left[m].remove(q)
    return moves, where


def pack(blocks, moves, tile_cols):
    lane = lax.broadcasted_iota(jnp.int32, blocks[0].shape, 1)
    total = None
    for m, shift, spots in moves:
        piece = pltpu.roll(blocks[m], shift, 1) if shift else blocks[m]
        if total is None:
            total = piece
            continue
        hit = None
        for spot in spots:
            one = (lane >= spot * tile_cols) & (lane < (spot + 1) * tile_cols)
            hit = one if hit is None else hit | one
        total = jnp.where(hit, piece, total)
    return total


def parts_of(courant):
    up, down = jnp.maximum(courant, 0.0), jnp.minimum(courant, 0.0)
    return up, down, 0.5 * (courant * courant - (up - down))


def kernel(
    bands,
    freqs,
    cols,
    route_in,
    stokes_in,
    spectrum,
    velocity,
    gain_in,
    quad_in,
    flags_in,
    sea_in,
    widen_in,
    wave_in,
    trig_in,
    final,
    ocean_out,
    route,
    stokes_route,
    spec,
    halo_low,
    halo_high,
    vel,
    gain_raw,
    quad_raw,
    widen,
    wave,
    trig,
    gain,
    quad,
    flag_raw,
    sea_raw,
    flag_blk,
    sea_blk,
    flag_north,
    flag_east,
    flag_north2,
    flag_east2,
    sea2,
    tile,
    ready,
    tiles,
    route_out,
    route_own,
    route_low,
    route_high,
    drift,
    faces,
    faces2,
    coef,
    coef2,
    start,
    leave,
    leave_end,
    leave_last,
    arrive,
    arrive_end,
    arrive_last,
    clean,
    first,
    packed,
    back,
    ocean,
    weight,
    flat,
    load_sems,
    halo_sems,
    route_sems,
    tile_sems,
    out_sems,
    back_sems,
    store_sems,
):
    band = lax.axis_index("band")
    me = lax.axis_index("freq")
    f32 = jnp.float32
    rows = spectrum.shape[1]
    tile_cols = velocity.shape[2]
    tall = rows + 2 * DEPTH
    block = max(LANES, cols)
    slots = block // cols
    n = tall // slots
    pitch = tile_cols + 2 * HALO
    per = LANES // pitch
    planes = (rows + 2 * HALO) // per
    seam = LANES - pitch
    moves, spot_of = packing(rows, planes, pitch, tile_cols)
    has_low = band > 0
    has_high = band < bands - 1

    mid = freqs // 2
    side, place = me // mid, lax.rem(me, mid)
    near = [side * mid + lax.rem(place + i, mid) for i in [*range(2, mid), 1][: mid - 1]]
    far = [(1 - side) * mid + lax.rem(2 * mid - 1 - place - i, mid) for i in range(mid)]
    partners = []
    for i in range(mid):
        partners += near[i : i + 1] + [far[i]]

    def across(mask):
        total, bit = 0, 1
        while bit < freqs:
            on = lax.rem(me // bit, 2)
            total = total + bit * (1 - on if mask & bit else on)
            bit *= 2
        return total

    distant = [across(mask) for mask in range(freqs - 1, 0, -1)]
    rising = [i + (i >= me).astype(jnp.int32) for i in range(freqs - 1)]
    ring = [lax.rem(me + i, freqs) for i in range(1, freqs)]

    def others(fn, order=None):
        for f in order or partners:
            fn(f)

    def every(fn):
        for f in range(freqs):
            fn(f)

    def copy(src, dst, sems, slot_send, slot_recv, to_band, to_freq):
        return pltpu.make_async_remote_copy(
            src_ref=src,
            dst_ref=dst,
            send_sem=sems.at[(0,) + slot_send],
            recv_sem=sems.at[(1,) + slot_recv],
            device_id=(to_band, to_freq),
            device_id_type=MESH,
        )

    def rolled(x, shift):
        shift %= x.shape[1]
        return pltpu.roll(x, shift, 1) if shift else x

    def locate(at):
        return (at, 0) if at < n else (tall - 1 - at, 1)

    def row_at(k, s):
        return tall - 1 - k if s else k

    def strided(ref, size, base, at):
        depth = ref.shape[1]
        if cols > LANES:
            return ref[pl.ds(base, size), at, :]
        return ref.reshape(ref.shape[0] * depth, cols)[
            pl.ds(base * depth + at, size, stride=depth), :
        ]

    def await_bytes(ref, sem):
        pltpu.make_async_copy(ref, ref, sem).wait()

    rest = pl.ds(0, freqs - 1)

    barrier = pltpu.get_barrier_semaphore()

    def greet(to_band, to_freq):
        pl.semaphore_signal(barrier, inc=1, device_id=(to_band, to_freq), device_id_type=MESH)

    others(lambda f: greet(band, f))

    @pl.when(has_low)
    def _():
        every(lambda f: greet(band - 1, f))

    @pl.when(has_high)
    def _():
        every(lambda f: greet(band + 1, f))

    load_vel = pltpu.make_async_copy(velocity, vel, load_sems.at[0])
    load_vel.start()
    load_route = pltpu.make_async_copy(route_in, route, load_sems.at[9])
    load_route.start()
    load_stokes = pltpu.make_async_copy(stokes_in, stokes_route, load_sems.at[10])
    load_stokes.start()
    load_spec = pltpu.make_async_copy(spectrum, spec.at[pl.ds(0, DIR)], load_sems.at[1])
    load_grid = [
        pltpu.make_async_copy(src, dst, load_sems.at[2 + i])
        for i, (src, dst) in enumerate(((flags_in, flag_raw), (sea_in, sea_raw)))
    ]
    loads = [
        pltpu.make_async_copy(src, dst, load_sems.at[4 + i])
        for i, (src, dst) in enumerate(
            (
                (wave_in, wave),
                (gain_in, gain_raw),
                (quad_in, quad_raw),
                (widen_in, widen),
                (trig_in, trig),
            )
        )
    ]
    for one in load_grid:
        one.start()
    load_spec.start()
    for one in loads:
        one.start()

    load_vel.wait()
    for c in range(2):
        field = vel[c].reshape(rows * tile_cols, LAYERS)
        tile[c * LAYERS : (c + 1) * LAYERS, :] = field.T

    ready[...] = pltpu.roll(
        0.15 * jnp.tanh(tile[...]), lax.rem(me * tile_cols, LANES), 1
    )

    def prepare(f):
        route_out[f, 0:1, :] = ready[pl.ds(route[f], 1), :]
        route_out[f, 1:2, :] = ready[pl.ds(LAYERS + route[f], 1), :]

    load_route.wait()
    every(prepare)
    count = freqs - 1 + freqs * (has_low.astype(jnp.int32) + has_high.astype(jnp.int32))
    pl.semaphore_wait(barrier, count)

    halo_to_low = copy(
        spectrum.at[:, pl.ds(0, DEPTH)], halo_high.at[pl.ds(0, DIR)], halo_sems,
        (0,), (0,), band - 1, me,
    )
    halo_to_high = copy(
        spectrum.at[:, pl.ds(rows - DEPTH, DEPTH)], halo_low.at[pl.ds(0, DIR)], halo_sems,
        (1,), (1,), band + 1, me,
    )

    def route_copy(f):
        return copy(route_out.at[f], route_own.at[me], route_sems, (0,), (0,), band, f)

    def route_to_low(f):
        return copy(
            route_out.at[f], route_high.at[me], route_sems, (1,), (1,), band - 1, f
        )

    def route_to_high(f):
        return copy(
            route_out.at[f], route_low.at[me], route_sems, (2,), (2,), band + 1, f
        )

    others(lambda f: route_copy(f).start())

    @pl.when(has_low)
    def _():
        every(lambda f: route_to_low(f).start())
        halo_to_low.start()

    @pl.when(has_high)
    def _():
        every(lambda f: route_to_high(f).start())
        halo_to_high.start()

    def near_tiles(fn):
        for down in (-1, 0, 1):
            for side in (-1, 0, 1):
                if down == 0 and side == 0:
                    continue
                to_band, to_freq = band + down, me + side
                there = (to_band >= 0) & (to_band < bands) & (to_freq >= 0) & (to_freq < freqs)
                mine = 3 * (1 + down) + 1 + side
                fn(there, mine, 8 - mine, to_band, to_freq)

    def tile_copy(mine, theirs, to_band, to_freq):
        return copy(tile, tiles.at[theirs], tile_sems, (), (), to_band, to_freq)

    def tile_start(there, mine, theirs, to_band, to_freq):
        @pl.when(there)
        def _():
            tile_copy(mine, theirs, to_band, to_freq).start()

        @pl.when(jnp.logical_not(there))
        def _():
            tiles[mine] = jnp.zeros_like(tile)

    near_tiles(tile_start)
    tiles[4] = tile[...]
    route_own[me] = route_out[me]

    pads = ((DIR, DIRP - DIR),)
    for at, size in pads:
        spec[at : at + size] = jnp.zeros((size, rows, cols), f32)
        halo_low[at : at + size] = jnp.zeros((size, DEPTH, cols), f32)
        halo_high[at : at + size] = jnp.zeros((size, DEPTH, cols), f32)

    @pl.when(jnp.logical_not(has_low))
    def _():
        halo_low[...] = jnp.zeros_like(halo_low)
        route_low[...] = jnp.zeros_like(route_low)

    @pl.when(jnp.logical_not(has_high))
    def _():
        halo_high[...] = jnp.zeros_like(halo_high)
        route_high[...] = jnp.zeros_like(route_high)

    for one in load_grid:
        one.wait()

    steps = CYCLES * SUB
    all_rows = sea_raw.shape[0]
    wide = (8, block)

    def grid_row(at):
        whole = jnp.clip(band * rows - DEPTH + at, 0, all_rows - 1)
        there = has_low if at < DEPTH else (None if at < DEPTH + rows else has_high)
        flag = strided(flag_raw, steps, 0, whole)
        sea = sea_raw[pl.ds(whole, 1), :].astype(f32)
        flag = flag.astype(f32)
        if there is not None:
            there = there.astype(f32)
            flag, sea = flag * there, sea * there
        return flag, sea

    for k in range(n):
        pieces = [grid_row(row_at(k, s)) for s in range(slots)]
        flag_blk[k] = jnp.concatenate([flag for flag, _ in pieces], axis=1)
        sea = jnp.concatenate([sea for _, sea in pieces], axis=1)
        sea_blk[8 * k : 8 * (k + 1), :] = jnp.broadcast_to(sea, wide)

    first_slot = lax.broadcasted_iota(jnp.int32, wide, 1) < cols
    for k in range(n):
        here = flag_blk[k]
        above = flag_blk[k + 1] if k + 1 < n else rolled(here, cols)
        if slots > 1:
            above = jnp.where(first_slot, above, here)
        beside = rolled(here, -1)
        for sub in range(SUB):
            there = slice(8 * k, 8 * (k + 1))
            flag_north[sub, there, :] = jnp.broadcast_to(above[sub : sub + 1], wide)
            flag_east[sub, there, :] = jnp.broadcast_to(beside[sub : sub + 1], wide)

    lane = lax.broadcasted_iota(jnp.int32, (8, LANES), 1)
    column = me * tile_cols - HALO + (lane & (pitch - 1))
    inside = (column >= 0) & (column < cols)
    window_flags, window_sea = [], []
    for m in range(planes):
        total_flags, total_sea = jnp.zeros((8, LANES), f32), jnp.zeros((8, LANES), f32)
        for q in range(per):
            k, s = locate(m + planes * q + DEPTH - HALO)
            shift = lax.rem(q * pitch - cols * s - tile_cols * me + HALO + 2 * block, block)
            hit = (lane >= q * pitch) & (lane < (q + 1) * pitch) & inside
            total_flags = jnp.where(
                hit, pltpu.roll(flag_blk[k], shift, 1)[:, :LANES], total_flags
            )
            total_sea = jnp.where(hit, pltpu.roll(sea_blk[8 * k : 8 * (k + 1), :], shift, 1)[:, :LANES], total_sea)
        window_flags.append(total_flags)
        window_sea.append(total_sea)
    for m in range(planes):
        sea2[m] = jnp.concatenate([window_sea[m]] * (FULL // 8), axis=0)
        above = window_flags[m + 1] if m + 1 < planes else rolled(window_flags[0], -pitch)
        beside = rolled(window_flags[m], -1)
        for sub in range(SUB):
            step = SUB + sub
            flag_north2[sub, m] = jnp.broadcast_to(above[step : step + 1], (FULL, LANES))
            flag_east2[sub, m] = jnp.broadcast_to(beside[step : step + 1], (FULL, LANES))

    load_spec.wait()
    load_stokes.wait()
    for one in loads:
        one.wait()

    for raw, padded in ((gain_raw, gain), (quad_raw, quad)):
        half = jnp.dot(widen[...], raw[...], preferred_element_type=f32).astype(jnp.bfloat16)
        padded[...] = lax.dot_general(
            half, widen[...], (((1,), (1,)), ((), ())), preferred_element_type=f32
        ).astype(jnp.bfloat16)

    layer = lax.broadcasted_iota(jnp.int32, (LAYERS, 1), 0)
    component = lax.broadcasted_iota(jnp.int32, (LAYERS, freqs * DIR), 1)
    deposits = jnp.zeros((LAYERS, freqs * DIR), f32)
    for g in range(freqs):
        deposit = jnp.zeros((LAYERS, 1), f32)
        for j in range(stokes_route.shape[0]):
            hit = (layer == stokes_route[j, g]).astype(f32)
            deposit = deposit + hit * (1.0 / (1.0 + j))
        tail = freqs * FULL + g * TAIL
        own = (component >= g * FULL) & (component < (g + 1) * FULL)
        own = own | ((component >= tail) & (component < tail + TAIL))
        deposits = jnp.where(own, deposit, deposits)
    for c in range(2):
        weight[c * LAYERS : (c + 1) * LAYERS, :] = deposits * trig[c : c + 1, :]

    @pl.when(has_low)
    def _():
        halo_to_high.wait_recv()
        await_bytes(route_low, route_sems.at[1, 2])

    @pl.when(has_high)
    def _():
        halo_to_low.wait_recv()
        await_bytes(route_high, route_sems.at[1, 1])

    number = me.astype(f32) + 0.5
    my_rate = 0.5 + 0.3 * number / freqs

    def row_of(base, at):
        if at < DEPTH:
            return strided(halo_low, GROUP, base, at)
        if at < DEPTH + rows:
            return strided(spec, GROUP, base, at - DEPTH)
        return strided(halo_high, GROUP, base, at - DEPTH - rows)

    starts = [
        jnp.concatenate([row_of(group * GROUP, row_at(k, s)) for s in range(slots)], axis=1)
        for group in range(GROUPS)
        for k in range(n)
    ]
    for i, one in enumerate(starts):
        start[i // n, 8 * (i % n) : 8 * (i % n + 1), :] = one

    await_bytes(route_own.at[rest], route_sems.at[1, 0])

    stacks = [
        jnp.concatenate(
            [route_low[j], route_own[j], route_high[j], jnp.zeros((2, LANES), f32)], axis=0
        )
        for j in range(freqs)
    ]
    reach = min(cols, LANES) // tile_cols
    places = LANES // tile_cols
    spot_masks = [
        (lane >= spot * tile_cols) & (lane < (spot + 1) * tile_cols) for spot in range(places)
    ]
    for row in range(rows):
        halves = []
        for half in range(block // LANES):
            total = stacks[half * reach]
            for j in range(1, reach):
                total = jnp.where(
                    spot_masks[(row + j) % places], stacks[half * reach + j], total
                )
            halves.append(total)
        moved = []
        for s in range(slots):
            turned = [rolled(x, cols * s - row * tile_cols) for x in halves]
            moved.append(turned[0] if len(turned) == 1 else jnp.concatenate(turned, axis=1))
        for source in range(3):
            at = row + DEPTH + rows * (source - 1)
            if at < 0 or at >= tall:
                continue
            k, s = locate(at)
            for c in range(2):
                line = 2 * source + c
                drift[c, k : k + 1, cols * s : cols * (s + 1)] = moved[s][
                    line : line + 1, cols * s : cols * (s + 1)
                ]
    blane = lax.broadcasted_iota(jnp.int32, (1, block), 1)
    last = ((blane & (cols - 1)) == cols - 1).astype(f32)
    inner = 1.0 - last
    east, north = drift[0], drift[1]
    above = jnp.concatenate([north[1:], rolled(north[n - 1 :], cols)], axis=0)
    sign = jnp.where(blane < cols, 1.0, -1.0)
    for i, face in enumerate(
        (sign * (0.5 * (north + above)), 0.5 * (inner * east + rolled(east, -1)), 0.5 * east)
    ):
        for k in range(n):
            faces[i, 8 * k : 8 * (k + 1), :] = jnp.broadcast_to(face[k : k + 1], wide)

    def advect_first(group):
        table = wave[group * GROUP : (group + 1) * GROUP, :]

        def rate_of(i):
            rate = jnp.broadcast_to(table[:, i : i + 1] * my_rate, wide)
            return jnp.concatenate([rate] * n, axis=0)

        rate_east = rate_of(0)
        for axis, rate in ((0, rate_of(1)), (1, rate_east)):
            if axis == 0 and slots > 1:
                rate = rate * sign
            for i, one in enumerate(parts_of(rate + faces[axis])):
                coef[group, 3 * axis + i] = one
        coef[group, 6] = 1.0 - last * jnp.maximum(rate_east + faces[2], 0.0)
        state = start[group]
        for sub in range(SUB):
            here, new = slice(8 * sub, 8 * n), slice(8 * (sub + 1), 8 * n)
            beyond = rolled(state[-8:], cols)
            more = flag_north[sub, here] * coef[group, 2, here]
            flux = (coef[group, 0, here] + more) * state + (
                coef[group, 1, here] - more
            ) * jnp.concatenate([state[8:], beyond], axis=0)
            state = state[8:] - (flux[8:] - flux[:-8])
            more = flag_east[sub, new] * coef[group, 5, new]
            flux = (coef[group, 3, new] + more) * (inner * state) + (
                coef[group, 4, new] - more
            ) * rolled(state, -1)
            state = (
                coef[group, 6, new] * state - (inner * flux - rolled(flux, 1))
            ) * sea_blk[new, :]
        width = min(cols, LANES) // pitch
        low_half = lax.broadcasted_iota(jnp.int32, (8 * planes, LANES), 1) < width * pitch
        for odd in range(2):
            turned = rolled(state, HALO - odd * tile_cols)
            for half in range(block // LANES):
                sources = []
                for i in range(width):
                    pieces = []
                    for s in range(slots):
                        lines = []
                        for m in range(planes):
                            k, slot = locate(m + planes * (i + width * s) + DEPTH - HALO)
                            assert slot == s and k >= SUB
                            k -= SUB
                            lines.append(
                                turned[8 * k : 8 * (k + 1), half * LANES : (half + 1) * LANES]
                            )
                        pieces.append(jnp.concatenate(lines, axis=0))
                    sources.append(pieces[0] if slots == 1 else jnp.where(low_half, *pieces))
                for e, one in enumerate(swap_pieces(sources, pitch, width)):
                    to = 2 * (e + width * half) + odd
                    for m in range(planes):
                        cells = one[8 * m : 8 * (m + 1)]
                        at = slice(m * LANES, (m + 1) * LANES)
                        if group < REST:
                            leave[to, group * GROUP : (group + 1) * GROUP, at] = cells
                            continue
                        end, at = (leave_last, slice(0, LANES)) if m == planes - 1 else (leave_end, at)
                        first_quad = (group - REST) * GROUP // QUAD
                        for i in range(min(GROUP // QUAD, QUADS - first_quad)):
                            end[to, first_quad + i, :, at] = cells[i * QUAD : (i + 1) * QUAD]

    def part_rows(part):
        low, high = PARTS[part]
        return pl.ds(low * GROUP, (high - low) * GROUP)

    def out_copy(part, f):
        there = part_rows(part)
        return copy(
            leave.at[f, there], arrive.at[me, there], out_sems, (part,), (part,), band, f
        )

    ends = ((leave_end, arrive_end, len(PARTS)), (leave_last, arrive_last, len(PARTS) + 1))

    def end_copy(leaving, arriving, part, f):
        return copy(leaving.at[f], arriving.at[me], out_sems, (part,), (part,), band, f)

    def received():
        for part in range(len(PARTS)):
            yield arrive.at[rest, part_rows(part)], part
        for _, arriving, part in ends:
            yield arriving.at[rest], part

    for part, (low, high) in enumerate(PARTS):
        for group in range(low, high):
            advect_first(group)
        others(lambda f: out_copy(part, f).start())
    for group in range(REST, GROUPS):
        advect_first(group)
    for leaving, arriving, part in ends:
        others(lambda f: end_copy(leaving, arriving, part, f).start())
    arrive[me] = leave[me]
    arrive_end[me] = leave_end[me]
    arrive_last[me] = leave_last[me]

    deep = 1 + has_low.astype(jnp.int32) + has_high.astype(jnp.int32)
    broad = 1 + (me > 0).astype(jnp.int32) + (me < freqs - 1).astype(jnp.int32)

    def await_tiles(way):
        for a in (2, 3):
            for b in (2, 3):

                @pl.when((deep == a) & (broad == b))
                def _():
                    await_bytes(tiles.at[pl.ds(0, a * b - 1)], tile_sems.at[way])

    await_tiles(1)
    tall_lane = lax.broadcasted_iota(jnp.int32, tile.shape, 1)
    for m in range(planes):
        total = jnp.zeros(tile.shape, f32)
        for q in range(per):
            row = m + planes * q - HALO
            down = 0 if row < 0 else (1 if row < rows else 2)
            from_row = row + rows * (1 - down)
            lead = q * pitch
            for side, width, from_col in (
                (0, HALO, tile_cols - HALO), (1, tile_cols, 0), (2, HALO, 0),
            ):
                piece = rolled(tiles[3 * down + side], lead - from_row * tile_cols - from_col)
                total = jnp.where((tall_lane >= lead) & (tall_lane < lead + width), piece, total)
                lead += width
        ocean[:, m * LANES : (m + 1) * LANES] = total

    def face_step(g, carry):
        east = 0.15 * jnp.tanh(ocean[pl.ds(route[g], 1), :])
        north = 0.15 * jnp.tanh(ocean[pl.ds(LAYERS + route[g], 1), :])
        for m in range(planes):
            here = north[:, m * LANES : (m + 1) * LANES]
            above = (
                north[:, (m + 1) * LANES : (m + 2) * LANES]
                if m + 1 < planes
                else rolled(north[:, :LANES], -pitch)
            )
            faces2[g, m : m + 1, :] = 0.5 * (here + above)
            here = east[:, m * LANES : (m + 1) * LANES]
            faces2[g, planes + m : planes + m + 1, :] = 0.5 * (here + rolled(here, -1))
        return carry

    [face_step(g, 0) for g in range(freqs)]

    def source(whole):
        grown = jnp.dot(gain[...], whole.astype(jnp.bfloat16), preferred_element_type=f32)
        quartic = jnp.dot(
            quad[...], (whole * whole).astype(jnp.bfloat16), preferred_element_type=f32
        )
        return whole * (1.0 + 0.5 * jnp.tanh(grown) - 0.25 * jnp.tanh(quartic))

    total_rows = freqs * DIR
    incoming = list(received())
    for ref, part in incoming[:-1]:
        await_bytes(ref, out_sems.at[1, part])
    for m in range(planes):
        there = slice(m * LANES, (m + 1) * LANES)
        end, at = (arrive_end, there)
        if m == planes - 1:
            await_bytes(incoming[-1][0], out_sems.at[1, incoming[-1][1]])
            end, at = (arrive_last, slice(0, LANES))
        pieces = []
        for f in range(freqs):
            pieces.append(arrive[f, :, there])
            pieces += [end[f, i, :, at] for i in range(QUADS - 1)]
        pieces += [end[f, QUADS - 1, :, at] for f in range(freqs)]
        whole = jnp.concatenate(pieces, axis=0) * sea2[m][0:1]
        clean[:, there] = whole
        first[:, there] = source(whole)

    def advect_second(g, at, rates, face_of):
        rate_east, rate_north = [jnp.broadcast_to(x, (FULL, LANES)) for x in rates]
        state = [first[at, m * LANES : (m + 1) * LANES] for m in range(planes)]
        for m in range(planes):
            for axis, rate in ((0, rate_north), (planes, rate_east)):
                for i, one in enumerate(parts_of(rate + face_of(axis + m))):
                    coef2[g, 3 * (axis + m) + i] = one
        for sub in range(SUB):
            fluxes = []
            for m in range(planes):
                here = 3 * m
                more = flag_north2[sub, m] * coef2[g, here + 2]
                above = state[m + 1] if m + 1 < planes else rolled(state[0], -pitch)
                fluxes.append(
                    (coef2[g, here] + more) * state[m] + (coef2[g, here + 1] - more) * above
                )
            cells = [
                state[m] - (fluxes[m] - (fluxes[m - 1] if m else rolled(fluxes[-1], pitch)))
                for m in range(planes)
            ]
            fluxes = []
            for m in range(planes):
                here = 3 * (planes + m)
                more = flag_east2[sub, m] * coef2[g, here + 2]
                fluxes.append(
                    (coef2[g, here] + more) * cells[m]
                    + (coef2[g, here + 1] - more) * rolled(cells[m], -1)
                )
            state = [
                (cells[m] - (fluxes[m] - rolled(fluxes[m], 1))) * sea2[m] for m in range(planes)
            ]
        packed[at, :] = pack(state, moves, tile_cols)

    for g in range(freqs):
        speed = 0.5 + 0.3 * (g + 0.5) / freqs
        table = wave[:FULL, :] * speed
        advect_second(
            g,
            slice(g * FULL, (g + 1) * FULL),
            (table[:, 0:1], table[:, 1:2]),
            lambda i: faces2[g, i : i + 1, :],
        )
    share = FULL // TAIL
    for chunk in range(freqs // share):
        table = wave[DIRP + chunk * FULL : DIRP + (chunk + 1) * FULL, :]
        advect_second(
            freqs + chunk,
            slice((freqs + chunk) * FULL, (freqs + chunk + 1) * FULL),
            (table[:, 0:1], table[:, 1:2]),
            lambda i: jnp.concatenate(
                [
                    jnp.broadcast_to(faces2[chunk * share + j, i : i + 1, :], (TAIL, LANES))
                    for j in range(share)
                ],
                axis=0,
            ),
        )
    def back_copy(f):
        return copy(back.at[f], final.at[me], back_sems, (), (), band, f)

    whole = packed[...]
    rounded, squared = whole.astype(jnp.bfloat16), (whole * whole).astype(jnp.bfloat16)

    def source_rows(low, high):
        at = slice(low, high)
        grown = jnp.dot(gain[at, :], rounded, preferred_element_type=f32)
        quartic = jnp.dot(quad[at, :], squared, preferred_element_type=f32)
        return whole[at] * (1.0 + 0.5 * jnp.tanh(grown) - 0.25 * jnp.tanh(quartic))

    tails = freqs * FULL
    early = 2
    for low, high, tail_low, tail_high in (
        (0, early, 0, 2 * early), (early, freqs, 2 * early, freqs),
    ):
        body_rows = source_rows(low * FULL, high * FULL)
        tail_rows = source_rows(tails + tail_low * TAIL, tails + tail_high * TAIL)
        for f in range(low, high):
            for i in range(FULL // QUAD):
                at = (f - low) * FULL + i * QUAD
                back[f, i] = body_rows[at : at + QUAD]
        for f in range(tail_low, tail_high):
            at = (f - tail_low) * TAIL
            back[f, FULL // QUAD] = tail_rows[at : at + TAIL]
        for f in rising[:1] if low == 0 else rising[1:]:
            back_copy(f).start()
    keep = pltpu.make_async_copy(back.at[me], final.at[me], store_sems.at[0])
    keep.start()

    stokes = jnp.dot(
        weight[...], clean[...],
        precision=precise, preferred_element_type=f32,
    )
    level = lax.broadcasted_iota(jnp.int32, (LAYERS, LANES), 0)
    planes_of = range(planes)

    def split(x, c):
        return [
            x[c * LAYERS : (c + 1) * LAYERS, m * LANES : (m + 1) * LANES] for m in planes_of
        ]

    def spreading(field):
        outs = []
        for m in planes_of:
            here = field[m]
            above = field[m + 1] if m + 1 < planes else rolled(field[0], -pitch)
            below = field[m - 1] if m else rolled(field[-1], pitch)
            sides = rolled(here, 1) + rolled(here, -1)
            over = jnp.where(level < LAYERS - 1, pltpu.roll(here, LAYERS - 1, 0), 0.0)
            under = jnp.where(level > 0, pltpu.roll(here, 1, 0), 0.0)
            outs.append(
                viscous * (sides + above + below - 4.0 * here)
                + mixing * (over + under - 2.0 * here)
                - friction * here
            )
        return outs

    both = ocean[...]
    u, v = split(both, 0), split(both, 1)
    stokes_east, stokes_north = split(stokes, 0), split(stokes, 1)
    for _ in range(OSTEPS):
        change_u, change_v = spreading(u), spreading(v)
        u, v = (
            [
                (u[m] + ocean_dt * (change_u[m] + coriolis * (v[m] + stokes_north[m])))
                * sea2[m][0:1]
                for m in planes_of
            ],
            [
                (v[m] + ocean_dt * (change_v[m] - coriolis * (u[m] + stokes_east[m])))
                * sea2[m][0:1]
                for m in planes_of
            ],
        )
    for c, field in enumerate((u, v)):
        flat[c * LAYERS : (c + 1) * LAYERS, :] = pack(field, moves, tile_cols)
    store_ocean = pltpu.make_async_copy(flat, ocean_out, store_sems.at[1])
    store_ocean.start()

    await_bytes(route_out.at[rest], route_sems.at[0, 0])

    @pl.when(has_low)
    def _():
        await_bytes(route_out, route_sems.at[0, 1])
        halo_to_low.wait_send()

    @pl.when(has_high)
    def _():
        await_bytes(route_out, route_sems.at[0, 2])
        halo_to_high.wait_send()

    await_tiles(0)
    for part in range(len(PARTS)):
        await_bytes(leave.at[rest, part_rows(part)], out_sems.at[0, part])
    for leaving, _, part in ends:
        await_bytes(leaving.at[rest], out_sems.at[0, part])

    await_bytes(final.at[rest], back_sems.at[1])
    await_bytes(back.at[rest], back_sems.at[0])
    store_ocean.wait()
    keep.wait()


def finish(final, flat, result, ocean_out):
    freqs = final.shape[0]
    rows, cols = result.shape[1:]
    tile_cols = ocean_out.shape[2]
    pitch = tile_cols + 2 * HALO
    planes = (rows + 2 * HALO) * pitch // LANES
    _, spot_of = packing(rows, planes, pitch, tile_cols)
    width = min(freqs, LANES // tile_cols)
    reach = width * tile_cols
    row_at = {spot: row for row, spot in spot_of.items()}
    for c in range(2):
        turned = flat[c * LAYERS : (c + 1) * LAYERS, :].T
        for row in range(rows):
            spot = spot_of[row]
            ocean_out[c, row] = turned[spot * tile_cols : (spot + 1) * tile_cols, :]
    for chunk in range(freqs // width):
        columns = [
            jnp.concatenate(
                [final[chunk * width + j, i] for i in range(DIR // QUAD)], axis=0
            )
            for j in range(width)
        ]
        for i, one in enumerate(swap_pieces(columns, tile_cols, width)):
            for s in range(LANES // reach):
                row = row_at[s * width + i]
                cells = pltpu.roll(one, LANES - s * reach, 1) if s else one
                cells = cells[:, :reach]
                if cols > LANES:
                    result[:, row, chunk * reach : (chunk + 1) * reach] = cells
                else:
                    result.reshape(DIR * rows, cols)[pl.ds(row, DIR, stride=rows), :] = cells


def body(
    spectrum,
    velocity,
    gain_matrix,
    quad_matrix,
    limiter_flags,
    sea_mask,
    current_route,
    stokes_route,
):
    bands = lax.axis_size("band")
    freqs = lax.axis_size("freq")
    rows, cols = spectrum.shape[2:]
    tile_cols = velocity.shape[3]
    pitch = tile_cols + 2 * HALO
    planes = (rows + 2 * HALO) * pitch // LANES
    tall = rows + 2 * DEPTH
    block = max(LANES, cols)
    n = tall * cols // block
    parts = freqs * DIR
    assert CYCLES == 2 and spectrum.shape[0] == 1 and rows % 8 == 0 and DEPTH % 8 == 0
    assert rows * tile_cols == LANES and rows >= DEPTH and tile_cols >= HALO >= OSTEPS
    assert pitch == 2 * tile_cols and LANES % pitch == 0 and freqs * tile_cols == cols
    assert (rows + 2 * HALO) % (LANES // pitch) == 0 and cols & (cols - 1) == 0
    assert block % cols == 0 and rows % 2 == 0 and n * block == tall * cols and cols % pitch == 0
    assert bands > 1 and freqs * TAIL % FULL == 0 and TAIL == QUAD and 2 * TAIL == GROUP and CYCLES * SUB == 8 and 2 * planes <= 8 and block // cols <= 2
    angles = (np.arange(DIR) + 0.5) * (2.0 * np.pi / DIR)
    waves = np.stack([np.cos(angles), np.sin(angles)])
    comps = freqs * DIR
    which, dirs = np.divmod(np.arange(comps), DIR)
    order = np.where(
        dirs < FULL, which * FULL + dirs, freqs * FULL + which * TAIL + dirs - FULL
    )
    wave = np.zeros((DIRP + freqs * TAIL, 2), np.float32)
    wave[:DIR] = waves.T
    speeds = 0.5 + 0.3 * (np.arange(freqs) + 0.5) / freqs
    wave[DIRP:] = (speeds[:, None, None] * waves.T[FULL:]).reshape(-1, 2)
    factor = (0.5 + 1.5 * (np.arange(freqs) + 0.5) / freqs) * DIR ** (-0.5)
    trig = np.zeros((2, comps), np.float32)
    trig[:, order] = waves[:, dirs] * factor[which]
    widen = np.zeros((comps, comps), np.float32)
    widen[order, np.arange(comps)] = 1.0
    f32, bf16 = jnp.float32, jnp.bfloat16
    anywhere = pl.BlockSpec(memory_space=pl.ANY)
    dma = pltpu.SemaphoreType.DMA
    vmem = pltpu.VMEM
    tile_cells = rows * tile_cols
    layers = 2 * LAYERS
    leaving = [
        vmem((freqs, REST * GROUP, planes * LANES), f32),
        vmem((freqs, QUADS, QUAD, (planes - 1) * LANES), f32),
        vmem((freqs, QUADS, QUAD, LANES), f32),
    ]
    final, flat = pl.pallas_call(
        functools.partial(kernel, bands, freqs, cols),
        out_shape=(
            jax.ShapeDtypeStruct((freqs, DIR // QUAD, QUAD, LANES), f32),
            jax.ShapeDtypeStruct((layers, LANES), f32),
        ),
        in_specs=[anywhere] * 11,
        out_specs=(anywhere, anywhere),
        scratch_shapes=[
            pltpu.SMEM((freqs,), jnp.int32),
            pltpu.SMEM(stokes_route.shape[::-1], jnp.int32),
            vmem((DIRP, rows, cols), f32),
            vmem((DIRP, DEPTH, cols), f32),
            vmem((DIRP, DEPTH, cols), f32),
            vmem((2, rows, tile_cols, LAYERS), f32),
            vmem((comps, comps), bf16),
            vmem((comps, comps), bf16),
            vmem((parts, comps), bf16),
            vmem(wave.shape, f32),
            vmem((2, parts), f32),
            vmem((parts, parts), bf16),
            vmem((parts, parts), bf16),
            vmem(limiter_flags.shape, jnp.int32),
            vmem(sea_mask.shape, jnp.int32),
            vmem((n, 8, block), f32),
            vmem((8 * n, block), f32),
            vmem((SUB, 8 * n, block), f32),
            vmem((SUB, 8 * n, block), f32),
            vmem((SUB, planes, FULL, LANES), f32),
            vmem((SUB, planes, FULL, LANES), f32),
            vmem((planes, FULL, LANES), f32),
            vmem((layers, tile_cells), f32),
            vmem((layers, tile_cells), f32),
            vmem((9, layers, tile_cells), f32),
            vmem((freqs, 2, tile_cells), f32),
            vmem((freqs, 2, tile_cells), f32),
            vmem((freqs, 2, tile_cells), f32),
            vmem((freqs, 2, tile_cells), f32),
            vmem((2, n, block), f32),
            vmem((3, 8 * n, block), f32),
            vmem((freqs, 8, LANES), f32),
            vmem((GROUPS, 7, 8 * n, block), f32),
            vmem((parts // FULL, 6 * planes, FULL, LANES), f32),
            vmem((GROUPS, 8 * n, block), f32),
            *leaving,
            *leaving,
            vmem((parts, planes * LANES), f32),
            vmem((parts, planes * LANES), f32),
            vmem((parts, LANES), f32),
            vmem((freqs, DIR // QUAD, QUAD, LANES), f32),
            vmem((layers, planes * LANES), f32),
            vmem((layers, parts), f32),
            vmem((layers, LANES), f32),
            dma((11,)),
            dma((2, 2)),
            dma((2, 3)),
            dma((2,)),
            dma((2, len(PARTS) + 2)),
            dma((2,)),
            dma((2,)),
        ],
        compiler_params=pltpu.CompilerParams(
            collective_id=0, has_side_effects=True, vmem_limit_bytes=60 * 1024 * 1024
        ),
    )(
        current_route,
        stokes_route.T,
        spectrum.reshape(DIR, rows, cols),
        velocity.transpose(0, 2, 3, 1),
        gain_matrix,
        quad_matrix,
        limiter_flags,
        sea_mask,
        jnp.asarray(widen, bf16),
        jnp.asarray(wave),
        jnp.asarray(trig),
    )
    whole = pl.BlockSpec(memory_space=vmem)
    result, ocean = pl.pallas_call(
        finish,
        out_shape=(
            jax.ShapeDtypeStruct((DIR, rows, cols), f32),
            jax.ShapeDtypeStruct((2, rows, tile_cols, LAYERS), f32),
        ),
        in_specs=[whole] * 2,
        out_specs=(whole, whole),
    )(final, flat)
    return (result.reshape(1, DIR, rows, cols), ocean.transpose(0, 3, 1, 2))


def solution(mesh):
    return jax.shard_map(
        body,
        mesh=mesh,
        in_specs=(
            P("freq", None, "band", None),
            P(None, None, "band", "freq"),
            P(),
            P(),
            P(),
            P(),
            P(),
            P(),
        ),
        out_specs=(P("freq", None, "band", None), P(None, None, "band", "freq")),
        check_vma=False,
    )
```
